32 devices in a mesh: ctx: 2 (over core), fsdp: 16 (over z, y, x).
Axes of the slice: x: 2, y: 2, z: 4, core: 2. Of those that a mesh axis runs over, the one named last changes fastest.
Arguments:
- tokens: bfloat16 [16, 1024, 2048], P('fsdp', 'ctx'), may hold values from -6 to 6
- route_ids: int32 [16, 1024, 2], P('fsdp', 'ctx'), may hold values from 0 to 3, all different within a row
- gate_values: float32 [16, 1024, 2], P('fsdp', 'ctx'), may hold values from 0.25 to 0.75
- deal: int32 [16, 4], P('fsdp'), may hold values from 0 to 3, each once within a row
- norm1_gain: float32 [2048], replicated, may hold values from 0.1 to 1.9
- w_query: bfloat16 [2048, 2048], P('fsdp'), may hold values from -0.125 to 0.125
- w_key: bfloat16 [2048, 2048], P('fsdp'), may hold values from -0.125 to 0.125
- w_value: bfloat16 [2048, 2048], P('fsdp'), may hold values from -0.125 to 0.125
- w_out: bfloat16 [2048, 2048], P('fsdp'), may hold values from -1.5 to 1.5
- norm2_gain: float32 [2048], replicated, may hold values from 0.1 to 1.9
- w_gate: bfloat16 [22528, 2048], P('fsdp'), may hold values from -0.125 to 0.125
- w_up: bfloat16 [22528, 2048], P('fsdp'), may hold values from -0.125 to 0.125
- w_down: bfloat16 [22528, 2048], P('fsdp'), may hold values from -0.078125 to 0.078125
- cotangent: bfloat16 [16, 1024, 2048], P('fsdp', 'ctx'), may hold values from -6 to 6
Outputs:
- mixed: bfloat16 [16, 1024, 2048], P('fsdp', 'ctx')
- tokens_grad: bfloat16 [16, 1024, 2048], P('fsdp', 'ctx')
- norm1_grad: float32 [2048], P(('ctx', 'fsdp'))
- query_grad: float32 [2048, 2048], P(('ctx', 'fsdp'))
- key_grad: float32 [2048, 2048], P(('ctx', 'fsdp'))
- value_grad: float32 [2048, 2048], P(('ctx', 'fsdp'))
- out_grad: float32 [2048, 2048], P(('ctx', 'fsdp'))
- norm2_grad: float32 [2048], P(('ctx', 'fsdp'))
- gate_grad: float32 [22528, 2048], P('fsdp', 'ctx')
- up_grad: float32 [22528, 2048], P('fsdp', 'ctx')
- down_grad: float32 [22528, 2048], P('fsdp', 'ctx')
The draws below stay inside these ranges and needn't reach their ends.
Inputs may be any that keep to these rules, and one draw needn't show every extreme that they name: Each row of deal names every block of the group once. `route_ids`: a token's two experts differ.
All inputs are finite; a program needn't handle non-finite values.
Results may differ from the reference program's by a relative error of at most 0.015.
Values may be sent and summed in bfloat16 or wider, within the bound.
No kernel may reach another device: no remote copies, remote signals or barrier semaphores. Data moves between devices by JAX's collectives and lax.ppermute only.
A program may use at most 448 MiB of HBM per device.

```python
import math
import jax
import jax.numpy as jnp
from jax import lax

D = 2048
HEADS = 16
HD = 128
FF = 5632
EXPERTS = 4
TOPK = 2
PROMPT = 512
CONT = 256
GTOK = 1024
NBLK = 4
TOK_DEV = 512
CAP = 320
GROUPS = 16
N_CTX = 2


def shard_levels(key, dims, cuts, low, high):
    loudness, own = 1.0, jax.random.fold_in(key, 6)
    for dim, blocks in cuts:
        heights = jnp.exp(jax.random.uniform(jax.random.fold_in(own, dim), (blocks,), jnp.float32, low / len(cuts), high / len(cuts)))
        loudness = loudness * jnp.repeat(heights, dims[dim] // blocks).reshape([-1 if axis == dim else 1 for axis in range(len(dims))])
    return loudness


def choose_distinct(stream_key, rows, count, top, lift):
    ranking = jax.random.permutation(jax.random.fold_in(stream_key, 1), count)
    pull = ranking
    for power in range(3):
        pull = pull * pull // count
    pull = pull * lift // count
    chance = jax.random.randint(jax.random.fold_in(stream_key, 2), (rows, count), 0, 4096) + pull
    sure = jax.random.permutation(jax.random.fold_in(stream_key, 3), rows)[jnp.arange(count) % rows]
    chance = jnp.where(jnp.arange(rows)[:, None] == sure[None, :], 1 << 14, chance)
    score = chance * count + jnp.arange(count)
    return lax.top_k(score.astype(jnp.int32), top)[1].astype(jnp.int32)


def normal_values(own_key, shape, width, bound, split=(), kind=jnp.bfloat16):
    values = jax.random.normal(own_key, shape, jnp.float32) * width
    if len(split) > 0:
        values = shard_levels(own_key, shape, split, -0.22, 0.18) * values
    return jnp.clip(values, min=-bound, max=bound).astype(kind)


def setup_inputs(seed: int = 0) -> dict:
    streams_of = jax.random.split(jax.random.key(seed), 15)
    return {
        "tokens": normal_values(streams_of[0], (GROUPS, GTOK, D), 1.0, 6.0, ((0, 16), (1, 2))),
        "route_ids": choose_distinct(streams_of[1], GROUPS * GTOK, EXPERTS, TOPK, 4096).reshape((GROUPS, GTOK, TOPK)),
        "gate_values": jnp.clip(0.25 + 0.5 * jax.random.uniform(streams_of[2], (GROUPS, GTOK, TOPK), jnp.float32) ** shard_levels(streams_of[2], (GROUPS, GTOK, TOPK), ((0, 16), (1, 2)), -0.2, 0.2), 0.25, 0.75),
        "deal": jax.vmap(lambda own: jax.random.permutation(own, NBLK))(jax.random.split(streams_of[3], GROUPS)).reshape((GROUPS, NBLK)).astype(jnp.int32),
        "norm1_gain": jnp.clip(1.0 + 0.18 * jax.random.normal(streams_of[4], (D,), jnp.float32), 0.1, 1.9),
        "w_query": normal_values(streams_of[5], (D, D), D ** -0.5, 0.125, ((0, 16),)),
        "w_key": normal_values(streams_of[6], (D, D), D ** -0.5, 0.125, ((0, 16),)),
        "w_value": normal_values(streams_of[7], (D, D), D ** -0.5, 0.125, ((0, 16),)),
        "w_out": normal_values(streams_of[8], (D, D), (D // 128) ** -0.5, 1.5, ((0, 16),)),
        "norm2_gain": jnp.clip(1.0 + 0.18 * jax.random.normal(streams_of[9], (D,), jnp.float32), 0.1, 1.9),
        "w_gate": normal_values(streams_of[10], (EXPERTS * FF, D), D ** -0.5, 0.125, ((0, 16),)),
        "w_up": normal_values(streams_of[11], (EXPERTS * FF, D), D ** -0.5, 0.125, ((0, 16),)),
        "w_down": normal_values(streams_of[12], (EXPERTS * FF, D), FF ** -0.5, 0.078125, ((0, 16),)),
        "cotangent": normal_values(streams_of[13], (GROUPS, GTOK, D), 1.0, 6.0, ((0, 16), (1, 2))),
    }


norm_eps = 1e-05
highest = lax.Precision.HIGHEST

@jax.custom_vjp
def low(v):
    return lax.optimization_barrier(v.astype(jnp.bfloat16)).astype(jnp.float32)

@jax.custom_vjp
def low_back(v):
    return v

def low_keep(v):
    return (low(v), None)

def low_pass(kept, grad):
    return (grad,)

def back_keep(v):
    return (v, None)

def back_low(kept, grad):
    return (low(grad),)
low.defvjp(low_keep, low_pass)
low_back.defvjp(back_keep, back_low)

def rotate(vector, position, orient):
    half_size = vector.shape[-1] // 2
    frequency = jnp.exp(-math.log(10000.0) * jnp.arange(half_size, dtype=jnp.float32) / half_size)
    angles = position.astype(jnp.float32)[:, None] * frequency[None, :]
    cosine = jnp.cos(angles)[:, None, :]
    sine_part = orient * jnp.sin(angles)[:, None, :]
    first_half = vector[..., :half_size]
    second = vector[..., half_size:]
    return jnp.concatenate([first_half * cosine - second * sine_part, second * cosine + first_half * sine_part], axis=-1)

def layout(deal_row):
    block_size = GTOK // NBLK
    token_index = jnp.arange(GTOK, dtype=jnp.int32)
    anchor = deal_row[token_index // block_size] * block_size + token_index % block_size
    after_prompt = anchor - PROMPT
    in_prompt = anchor < PROMPT
    segment = jnp.where(in_prompt, 0, after_prompt // CONT + 1).astype(jnp.int32)
    position = jnp.where(in_prompt, anchor, PROMPT + after_prompt % CONT).astype(jnp.int32)
    return (position, segment)

def visibility(query_pos, query_seg, key_pos, key_seg):
    earlier = key_pos[None, :] <= query_pos[:, None]
    shared = (key_seg[None, :] == 0) | (key_seg[None, :] == query_seg[:, None])
    return earlier & shared

def route_slots(expert_ids, capacity):
    flat_ids = expert_ids.reshape(-1)
    onehot = (flat_ids[:, None] == jnp.arange(EXPERTS, dtype=jnp.int32)[None, :]).astype(jnp.int32)
    earlier = jnp.cumsum(onehot, axis=0) - onehot
    slot_index = lax.optimization_barrier(jnp.sum(earlier * onehot, axis=1))
    kept_pair = slot_index < capacity
    place = flat_ids * capacity + jnp.minimum(slot_index, capacity - 1)
    target = jnp.arange(EXPERTS * capacity, dtype=jnp.int32)[None, :]
    return (place[:, None] == target) & kept_pair[:, None]

def normalize(values, gain):
    return values * lax.rsqrt(lax.optimization_barrier(jnp.mean(values * values, axis=-1, keepdims=True)) + norm_eps) * gain

def mixture(normed_two, expert_ids, gates, w_gate, w_up, w_down):
    block_rows = normed_two.reshape(N_CTX, TOK_DEV, D)
    block_ids = expert_ids.reshape(N_CTX, TOK_DEV, TOPK)

    def dispatch(rows_one, ids_one):
        select = route_slots(ids_one, CAP).astype(jnp.float32)
        pairs = jnp.repeat(rows_one, TOPK, axis=0)
        return (jnp.dot(select.T, pairs, precision=highest), select)
    slots, selects = jax.vmap(dispatch)(block_rows, block_ids)
    inputs = slots.reshape(N_CTX, EXPERTS, CAP, D).transpose(1, 0, 2, 3).reshape(EXPERTS, N_CTX * CAP, D)
    outputs = []
    for expert in range(EXPERTS):
        rows_gate = w_gate[expert * FF:(expert + 1) * FF]
        rows_up = w_up[expert * FF:(expert + 1) * FF]
        rows_down = w_down[expert * FF:(expert + 1) * FF]
        gate_act = low_back(jnp.dot(inputs[expert], rows_gate.T, precision=highest))
        up_act = low_back(jnp.dot(inputs[expert], rows_up.T, precision=highest))
        hidden = low(jax.nn.silu(gate_act) * up_act)
        outputs.append(low_back(jnp.dot(hidden, rows_down, precision=highest)))
    slot_out = jnp.stack(outputs).reshape(EXPERTS, N_CTX, CAP, D).transpose(1, 0, 2, 3).reshape(N_CTX, EXPERTS * CAP, D)
    pair_out = jnp.einsum('bps,bsd->bpd', selects, slot_out, precision=highest).reshape(GTOK, TOPK, D)
    return lax.optimization_barrier(jnp.sum(pair_out * gates[:, :, None], axis=1))

def group_layer(tokens_f, expert_ids, gates, deal_row, gain_one, w_query, w_key, w_value, w_out, gain_two, w_gate, w_up, w_down):
    position, segment = layout(deal_row)
    normed = low(normalize(tokens_f, gain_one))
    query = low(rotate(low_back(jnp.dot(normed, w_query, precision=highest)).reshape(GTOK, HEADS, HD), position, 1.0))
    keys = low(rotate(low_back(jnp.dot(normed, w_key, precision=highest)).reshape(GTOK, HEADS, HD), position, 1.0))
    values = low_back(low(jnp.dot(normed, w_value, precision=highest))).reshape(GTOK, HEADS, HD)
    scores = low_back(jnp.einsum('qhd,khd->hqk', query, keys, precision=highest) * (1.0 / math.sqrt(HD)))
    visible = visibility(position, segment, position, segment)
    scores = jnp.where(visible[None], scores, -1e+30)
    probs = low(jax.nn.softmax(scores, axis=-1))
    context = jnp.einsum('hqk,khd->qhd', probs, values, precision=highest).reshape(GTOK, D)
    context = low_back(low(context))
    attention = low_back(jnp.dot(context, w_out, precision=highest))
    hidden_in = tokens_f + attention
    normed_two = low(normalize(hidden_in, gain_two))
    return hidden_in + mixture(normed_two, expert_ids, gates, w_gate, w_up, w_down)

def reference(tokens, route_ids, gate_values, deal, norm1_gain, w_query, w_key, w_value, w_out, norm2_gain, w_gate, w_up, w_down, cotangent):
    floats = [arr.astype(jnp.float32) for arr in (tokens, norm1_gain, w_query, w_key, w_value, w_out, norm2_gain, w_gate, w_up, w_down)]
    gates_f = gate_values.astype(jnp.float32)

    def forward(tokens_all, gain_one, wq_f, wk_f, wv_f, wo_f, gain_two, wg_f, wu_f, wd_f):
        layer_fn = jax.checkpoint(group_layer)

        def one_group(state_unused, group_item):
            tokens_f, expert_ids, gates, deal_row = group_item
            result = layer_fn(tokens_f, expert_ids, gates, deal_row, gain_one, wq_f, wk_f, wv_f, wo_f, gain_two, wg_f, wu_f, wd_f)
            return (state_unused, result)
        _, outputs = lax.scan(one_group, jnp.zeros((), jnp.float32), (tokens_all, route_ids, gates_f, deal))
        return outputs
    mixed, pullback = jax.vjp(forward, *floats)
    grads = pullback(cotangent.astype(jnp.float32))
    return (mixed.astype(jnp.bfloat16), grads[0].astype(jnp.bfloat16), grads[1], grads[2], grads[3], grads[4], grads[5], grads[6], grads[7], grads[8], grads[9])
```

```python
import functools
import math

import jax
import jax.numpy as jnp
from jax import lax
from jax.experimental import pallas as pl
from jax.experimental.pallas import tpu as pltpu
from jax.sharding import PartitionSpec as P

D = 2048
HEADS = 16
HD = 128
EXPERTS = 4
TOPK = 2
PROMPT = 512
CONT = 256
TILE = 256

norm_eps = 1e-05
scale = 1.0 / math.sqrt(HD)
bf16 = jnp.bfloat16
f32 = jnp.float32


def dot(a, b, ca, cb, out=f32):
    r = lax.dot_general(a, b, (((ca,), (cb,)), ((), ())), preferred_element_type=f32)
    return r.astype(out)


def tile_keys(t):
    prompt_tiles = PROMPT // TILE
    if t < prompt_tiles:
        return list(range(t + 1))
    per = CONT // TILE
    first = prompt_tiles + ((t - prompt_tiles) // per) * per
    return list(range(prompt_tiles)) + list(range(first, t + 1))


def load_tile(ref, perm, t, block, cols):
    per = TILE // block
    parts = [
        ref[pl.ds(pl.multiple_of(perm[t * per + i] * block, block), block), cols]
        for i in range(per)
    ]
    return parts[0] if per == 1 else jnp.concatenate(parts, axis=0)


def store_tile(ref, perm, t, block, cols, value):
    per = TILE // block
    for i in range(per):
        ref[pl.ds(pl.multiple_of(perm[t * per + i] * block, block), block), cols] = value[
            i * block : (i + 1) * block
        ]


def spread_keys(ref, tiles):
    runs, start = [], tiles[0]
    for a, b in zip(tiles, tiles[1:] + [None]):
        if b != a + 1:
            runs.append((start, a + 1))
            start = b
    parts = [ref[lo * TILE : hi * TILE, :] for lo, hi in runs]
    return parts[0] if len(parts) == 1 else jnp.concatenate(parts, axis=0)


def causal_fill(scores, value):
    width = scores.shape[1] - TILE
    row = lax.broadcasted_iota(jnp.int32, (TILE, TILE), 0)
    col = lax.broadcasted_iota(jnp.int32, (TILE, TILE), 1)
    last = jnp.where(col <= row, scores[:, width:], value)
    return last if width == 0 else jnp.concatenate([scores[:, :width], last], axis=1)


def forward_kernel(block, perm, pre_ref, cos_ref, sin_ref, ctx_ref, q_ref, k_ref, v_ref, log_ref):
    tiles = pre_ref.shape[0] // TILE
    for t in range(tiles):
        rows = slice(t * TILE, (t + 1) * TILE)
        cos, sin = cos_ref[rows, :], sin_ref[rows, :]
        q = load_tile(pre_ref, perm, t, block, slice(0, HD))
        q_ref[rows, :] = (q * cos + pltpu.roll(q, HD // 2, 1) * sin).astype(bf16)
        k = load_tile(pre_ref, perm, t, block, slice(HD, 2 * HD))
        k_ref[rows, :] = (k * cos + pltpu.roll(k, HD // 2, 1) * sin).astype(bf16)
        v_ref[rows, :] = load_tile(pre_ref, perm, t, block, slice(2 * HD, 3 * HD)).astype(bf16)
    for t in range(tiles):
        rows = slice(t * TILE, (t + 1) * TILE)
        seen = tile_keys(t)
        keys, values = spread_keys(k_ref, seen), spread_keys(v_ref, seen)
        scores = dot(q_ref[rows, :], keys, 1, 1) * scale
        scores = causal_fill(scores, -1e30)
        top = jnp.max(scores, axis=1, keepdims=True)
        expo = jnp.exp(scores - top)
        total = jnp.sum(expo, axis=1, keepdims=True)
        probs = (expo * (1.0 / total)).astype(bf16)
        context = dot(probs, values, 1, 0).astype(bf16)
        store_tile(ctx_ref, perm, t, block, slice(None), context)
        log_ref[rows, :] = jnp.broadcast_to(top + jnp.log(total), (TILE, HD))


def backward_kernel(
    block, perm, q_ref, k_ref, v_ref, log_ref, do_ref, cos_ref, sin_ref, out_ref, dk_ref, dv_ref
):
    tiles = q_ref.shape[0] // TILE
    dk_ref[...] = jnp.zeros_like(dk_ref)
    dv_ref[...] = jnp.zeros_like(dv_ref)
    for t in range(tiles):
        rows = slice(t * TILE, (t + 1) * TILE)
        seen = tile_keys(t)
        keys, values = spread_keys(k_ref, seen), spread_keys(v_ref, seen)
        query = q_ref[rows, :]
        grad = load_tile(do_ref, perm, t, block, slice(None))
        scores = dot(query, keys, 1, 1) * scale
        soft = causal_fill(jnp.exp(scores - log_ref[rows, 0:1]), 0.0)
        grad_prob = dot(grad, values, 1, 1)
        delta = jnp.sum(grad_prob * soft, axis=1, keepdims=True)
        grad_scores = (soft * (grad_prob - delta)).astype(bf16)
        values_back = dot(soft.astype(bf16), grad, 0, 0)
        keys_back = dot(grad_scores, query, 0, 0)
        for i, s in enumerate(seen):
            part, own = slice(i * TILE, (i + 1) * TILE), slice(s * TILE, (s + 1) * TILE)
            dv_ref[own, :] += values_back[part]
            dk_ref[own, :] += keys_back[part]
        back = dot(grad_scores, keys, 1, 0) * scale
        cos, sin = cos_ref[rows, :], sin_ref[rows, :]
        back = back * cos - pltpu.roll(back, HD // 2, 1) * sin
        store_tile(out_ref, perm, t, block, slice(0, HD), back.astype(bf16))
    for t in range(tiles):
        rows = slice(t * TILE, (t + 1) * TILE)
        cos, sin = cos_ref[rows, :], sin_ref[rows, :]
        back = dk_ref[rows, :] * scale
        back = back * cos - pltpu.roll(back, HD // 2, 1) * sin
        store_tile(out_ref, perm, t, block, slice(HD, 2 * HD), back.astype(bf16))
        store_tile(out_ref, perm, t, block, slice(2 * HD, 3 * HD), dv_ref[rows, :].astype(bf16))


def attention_forward(perm, block, pre, cos, sin):
    rows, heads = pre.shape[0], pre.shape[1] // (3 * HD)
    per_head = pl.BlockSpec((rows, HD), lambda h, p: (0, h))
    table = pl.BlockSpec((rows, HD), lambda h, p: (0, 0))
    head_array = jax.ShapeDtypeStruct((rows, heads * HD), bf16)
    return pl.pallas_call(
        functools.partial(forward_kernel, block),
        grid_spec=pltpu.PrefetchScalarGridSpec(
            num_scalar_prefetch=1,
            grid=(heads,),
            in_specs=[pl.BlockSpec((rows, 3 * HD), lambda h, p: (0, h)), table, table],
            out_specs=[per_head] * 5,
        ),
        out_shape=[head_array] * 4 + [jax.ShapeDtypeStruct((rows, heads * HD), f32)],
        name="attention_forward",
    )(perm, pre, cos, sin)


def attention_backward(perm, block, q, k, v, log_total, grad, cos, sin):
    rows, heads = q.shape[0], q.shape[1] // HD
    per_head = pl.BlockSpec((rows, HD), lambda h, p: (0, h))
    table = pl.BlockSpec((rows, HD), lambda h, p: (0, 0))
    return pl.pallas_call(
        functools.partial(backward_kernel, block),
        grid_spec=pltpu.PrefetchScalarGridSpec(
            num_scalar_prefetch=1,
            grid=(heads,),
            in_specs=[per_head] * 5 + [table, table],
            out_specs=pl.BlockSpec((rows, 3 * HD), lambda h, p: (0, h)),
            scratch_shapes=[pltpu.VMEM((rows, HD), f32), pltpu.VMEM((rows, HD), f32)],
        ),
        out_shape=jax.ShapeDtypeStruct((rows, heads * 3 * HD), bf16),
        name="attention_backward",
    )(perm, q, k, v, log_total, grad, cos, sin)


def rope_tables(group_len):
    index = jnp.arange(group_len, dtype=jnp.int32)
    position = jnp.where(index < PROMPT, index, PROMPT + (index - PROMPT) % CONT).astype(f32)
    half = HD // 2
    frequency = jnp.exp(-math.log(10000.0) * jnp.arange(half, dtype=f32) / half)
    angles = position[:, None] * frequency[None, :]
    cosine, sine = jnp.cos(angles), jnp.sin(angles)
    return (
        jnp.concatenate([cosine, cosine], axis=1),
        jnp.concatenate([-sine, sine], axis=1),
    )


def normalize_parts(values, gain):
    inverse = lax.rsqrt(jnp.mean(values * values, axis=-1, keepdims=True) + norm_eps)
    unit_rows = values * inverse
    return (unit_rows * gain, unit_rows, inverse)


def norm_backward(grad_outer, unit_rows, inverse, gain):
    grad_unit = grad_outer * gain
    grad_inner = inverse * (
        grad_unit - unit_rows * jnp.mean(grad_unit * unit_rows, axis=-1, keepdims=True)
    )
    return (grad_inner, jnp.sum(grad_outer * unit_rows, axis=0))


def shards(
    tokens,
    route_ids,
    gate_values,
    deal,
    norm1_gain,
    w_query,
    w_key,
    w_value,
    w_out,
    norm2_gain,
    w_gate,
    w_up,
    w_down,
    cotangent,
):
    rows = tokens.shape[1]
    ctx_count = lax.axis_size("ctx")
    fsdp_count = lax.axis_size("fsdp")
    group_len = rows * ctx_count
    capacity = 5 * rows * TOPK // (4 * EXPERTS)
    repeats = fsdp_count // EXPERTS
    pair = 2
    columns = repeats // pair
    core = lax.axis_index("ctx")
    expert = lax.axis_index("fsdp") // repeats
    width = D // ctx_count
    heads = HEADS // ctx_count

    def core_shift(a, s):
        return lax.ppermute(a, "ctx", [(i, (i + s) % ctx_count) for i in range(ctx_count)])

    def fsdp_shift(a, move):
        return lax.ppermute(a, "fsdp", [(i, move(i)) for i in range(fsdp_count)])

    def expert_shift(a, k):
        return fsdp_shift(a, lambda i: (i + k * repeats) % fsdp_count)

    def column_shift(a, j):
        def move(i):
            e, r = divmod(i, repeats)
            t, w = divmod(r, pair)
            return e * repeats + ((t + j) % columns) * pair + w

        return fsdp_shift(a, move)

    def pair_swap(a):
        return fsdp_shift(a, lambda i: i ^ 1)

    def core_gather(a):
        return jnp.concatenate([a] + [core_shift(a, s) for s in range(1, ctx_count)], axis=0)

    block_count = deal.shape[1]
    block = group_len // block_count
    local_blocks = block_count // ctx_count
    dealt = jnp.argsort(deal[0]).astype(jnp.int32)
    perm = ((core - dealt // local_blocks) % ctx_count) * local_blocks + dealt % local_blocks
    cos, sin = rope_tables(group_len)

    def own_columns(w):
        return lax.dynamic_slice_in_dim(w, core * width, width, axis=1)

    stack = jnp.stack(
        [own_columns(w).reshape(-1, heads, HD) for w in (w_query, w_key, w_value)], axis=2
    ).reshape(-1, 3 * width)
    packed = jnp.concatenate([stack, own_columns(w_out)], axis=1)
    gathered = lax.all_gather(packed, "fsdp", axis=0, tiled=True)
    w_qkv = gathered[:, : 3 * width]
    out_columns = gathered[:, 3 * width :]

    def out_rows(c):
        return lax.dynamic_slice_in_dim(out_columns, (c % ctx_count) * width, width, axis=0)

    if ctx_count == 2:
        mine, other = out_rows(core), core_shift(out_rows(core + 1), 1)
        w_o = jnp.concatenate(
            [jnp.where(core == 0, mine, other), jnp.where(core == 0, other, mine)], axis=1
        )
    else:
        w_o = lax.all_to_all(
            out_columns.reshape(ctx_count, width, width), "ctx", 0, 0, tiled=False
        )
        w_o = w_o.transpose(1, 0, 2).reshape(width, D)

    def pair_weights(w):
        count = w.shape[0] // ctx_count
        part = pair_swap(lax.dynamic_slice_in_dim(w, core * count, count, axis=0))
        if ctx_count == 2:
            again = core_shift(part, 1)
            first, second = jnp.where(core == 0, part, again), jnp.where(core == 0, again, part)
            return jnp.concatenate([w, first, second], axis=0)
        return jnp.concatenate([w, lax.all_gather(part, "ctx", axis=0, tiled=True)], axis=0)

    wg, wu, wd = pair_weights(w_gate), pair_weights(w_up), pair_weights(w_down)

    ids = route_ids[0]
    flat = ids.reshape(-1)
    onehot = (flat[:, None] == jnp.arange(EXPERTS, dtype=jnp.int32)[None, :]).astype(jnp.int32)
    earlier = jnp.cumsum(onehot, axis=0) - onehot
    slot = jnp.sum(earlier * onehot, axis=1)
    relative = (flat - expert) % EXPERTS
    place = jnp.where(slot < capacity, relative * capacity + slot, -1).reshape(rows, TOPK)
    targets = jnp.arange(EXPERTS * capacity, dtype=jnp.int32)
    select = [(place[:, k : k + 1] == targets[None, :]).astype(bf16) for k in range(TOPK)]
    spread = [(targets[:, None] == place[None, :, k]).astype(bf16) for k in range(TOPK)]
    gates = gate_values[0]

    def send_slots(blocks):
        parts = []
        for k in range(EXPERTS):
            arrived = blocks[k] if k == 0 else expert_shift(blocks[k], k)
            parts.append(arrived)
            parts.extend(column_shift(arrived, j) for j in range(1, columns))
        return jnp.concatenate(parts, axis=0)

    def return_slots(partial):
        parts = partial.reshape(EXPERTS, columns, capacity, D)
        home = []
        for k in range(EXPERTS):
            total = parts[k, 0].astype(f32)
            for j in range(1, columns):
                total = total + column_shift(parts[k, j], -j).astype(f32)
            total = total.astype(bf16)
            home.append(total if k == 0 else expert_shift(total, -k))
        return jnp.concatenate(home, axis=0)

    dy = cotangent[0].astype(f32)
    grad_pairs = jnp.concatenate([(dy * gates[:, k : k + 1]).astype(bf16) for k in range(TOPK)])
    spread_both = jnp.concatenate(spread, axis=1)
    grad_arrived = send_slots(
        [
            dot(spread_both[k * capacity : (k + 1) * capacity], grad_pairs, 1, 0, bf16)
            for k in range(EXPERTS)
        ]
    )

    inputs = tokens[0].astype(f32)
    normed_f, _, _ = normalize_parts(inputs, norm1_gain)
    normed = core_gather(normed_f.astype(bf16))
    pre = dot(normed, w_qkv, 1, 0)
    context, q, k, v, log_total = attention_forward(perm, block, pre, cos, sin)
    attention = dot(context[:rows], w_o, 1, 0)
    for s in range(1, ctx_count):
        away = dot(context[s * rows : (s + 1) * rows], w_o, 1, 0, bf16)
        attention = attention + core_shift(away, -s).astype(f32)
    hidden_in = inputs + attention
    normed_two_f, unit_two, inverse_two = normalize_parts(hidden_in, norm2_gain)
    normed_two = normed_two_f.astype(bf16)

    spread_any = spread[0] + spread[1]
    arrived = send_slots(
        [
            dot(spread_any[k * capacity : (k + 1) * capacity], normed_two, 1, 0, bf16)
            for k in range(EXPERTS)
        ]
    )
    grad_hidden = dot(grad_arrived, wd, 1, 1, bf16)
    gate_act = dot(arrived, wg, 1, 1)
    up_act = dot(arrived, wu, 1, 1)
    sigmoid_gate = jax.nn.sigmoid(gate_act)
    silu_gate = gate_act * sigmoid_gate
    hidden = (silu_gate * up_act).astype(bf16)
    gh = grad_hidden.astype(f32)
    grad_gate = (gh * up_act * sigmoid_gate * (1.0 + gate_act * (1.0 - sigmoid_gate))).astype(bf16)
    grad_up = (gh * silu_gate).astype(bf16)
    grad_in = (dot(grad_gate, wg, 1, 0) + dot(grad_up, wu, 1, 0)).astype(bf16)
    grad_slot_in = return_slots(grad_in)
    slot_out = return_slots(dot(hidden, wd, 1, 0, bf16))

    grad_normed_two = dot(select[0] + select[1], grad_slot_in, 1, 0)
    grad_norm_two, norm2_part = norm_backward(grad_normed_two, unit_two, inverse_two, norm2_gain)
    grad_hidden_in = dy + grad_norm_two
    grad_attention = core_gather(grad_hidden_in.astype(bf16))
    grad_context = dot(grad_attention, w_o, 1, 1, bf16)
    out_part = dot(context, grad_attention, 0, 0, bf16)
    out_grad = lax.psum_scatter(out_part, "fsdp", scatter_dimension=0, tiled=True).astype(f32)

    grad_qkv = attention_backward(perm, block, q, k, v, log_total, grad_context, cos, sin)
    per = D // (ctx_count * fsdp_count)
    normed_mixed = (
        normed.reshape(group_len, ctx_count, fsdp_count, per)
        .transpose(0, 2, 1, 3)
        .reshape(group_len, D)
    )
    qkv_part = dot(normed_mixed, grad_qkv, 0, 0, bf16)
    qkv_sum = lax.psum_scatter(qkv_part, "fsdp", scatter_dimension=0, tiled=True)
    qkv_sum = qkv_sum.reshape(ctx_count, per, heads, 3, HD)
    if ctx_count == 2:
        mine = lax.dynamic_index_in_dim(qkv_sum, core, 0, keepdims=False)
        other = core_shift(lax.dynamic_index_in_dim(qkv_sum, 1 - core, 0, keepdims=False), 1)
        qkv_own = jnp.where(
            core == 0,
            jnp.concatenate([mine, other], axis=1),
            jnp.concatenate([other, mine], axis=1),
        )
    else:
        qkv_own = lax.all_to_all(qkv_sum, "ctx", 0, 0, tiled=False)
        qkv_own = qkv_own.transpose(1, 0, 2, 3, 4).reshape(per, HEADS, 3, HD)
    qkv_own = qkv_own.astype(f32)
    query_grad, key_grad, value_grad = (qkv_own[:, :, i].reshape(per, D) for i in range(3))

    grad_normed = dot(grad_qkv[:rows], w_qkv, 1, 1)
    for s in range(1, ctx_count):
        away = dot(grad_qkv[s * rows : (s + 1) * rows], w_qkv, 1, 1, bf16)
        grad_normed = grad_normed + core_shift(away, -s).astype(f32)
    _, unit_one, inverse_one = normalize_parts(inputs, norm1_gain)
    grad_norm_one, norm1_part = norm_backward(grad_normed, unit_one, inverse_one, norm1_gain)
    tokens_grad = (grad_hidden_in + grad_norm_one).astype(bf16)

    gains = jnp.stack([norm1_part, norm2_part])
    step = 1
    while step < ctx_count:
        gains = gains + lax.ppermute(gains, "ctx", [(i, i ^ step) for i in range(ctx_count)])
        step *= 2
    step = 1
    while step < fsdp_count:
        gains = gains + fsdp_shift(gains, lambda i, step=step: i ^ step)
        step *= 2
    place_own = (core * fsdp_count + lax.axis_index("fsdp")) * per
    gains_own = lax.dynamic_slice_in_dim(gains, place_own, per, axis=1)

    def expert_grad(left, right):
        part = dot(left, right, 0, 0, bf16)
        total = lax.dynamic_slice_in_dim(part, core * width, width, axis=1).astype(f32)
        for s in range(1, ctx_count):
            start = ((core + s) % ctx_count) * width
            total = total + core_shift(
                lax.dynamic_slice_in_dim(part, start, width, axis=1), s
            ).astype(f32)
        count = total.shape[0] // pair
        return total[:count] + pair_swap(total[count:].astype(bf16)).astype(f32)

    down_grad = expert_grad(hidden, grad_arrived)
    gate_grad = expert_grad(grad_gate, arrived)
    up_grad = expert_grad(grad_up, arrived)

    mixed = hidden_in
    for k in range(TOPK):
        mixed = mixed + dot(select[k], slot_out, 1, 0) * gates[:, k : k + 1]

    return (
        mixed.astype(bf16)[None],
        tokens_grad[None],
        gains_own[0],
        query_grad,
        key_grad,
        value_grad,
        out_grad,
        gains_own[1],
        gate_grad,
        up_grad,
        down_grad,
    )


def solution(mesh):
    in_specs = (
        P("fsdp", "ctx", None),
        P("fsdp", "ctx", None),
        P("fsdp", "ctx", None),
        P("fsdp", None),
        P(),
        P("fsdp", None),
        P("fsdp", None),
        P("fsdp", None),
        P("fsdp", None),
        P(),
        P("fsdp", None),
        P("fsdp", None),
        P("fsdp", None),
        P("fsdp", "ctx", None),
    )
    out_specs = (
        P("fsdp", "ctx", None),
        P("fsdp", "ctx", None),
        P(("ctx", "fsdp")),
        P(("ctx", "fsdp"), None),
        P(("ctx", "fsdp"), None),
        P(("ctx", "fsdp"), None),
        P(("ctx", "fsdp"), None),
        P(("ctx", "fsdp")),
        P("fsdp", "ctx"),
        P("fsdp", "ctx"),
        P("fsdp", "ctx"),
    )
    return jax.shard_map(shards, mesh=mesh, in_specs=in_specs, out_specs=out_specs, check_vma=False)
```

```python
import functools
import math

import jax
import jax.numpy as jnp
from jax import lax
from jax.experimental import pallas as pl
from jax.experimental.pallas import tpu as pltpu
from jax.sharding import PartitionSpec as P

D = 2048
HEADS = 16
HD = 128
EXPERTS = 4
TOPK = 2
PROMPT = 512
CONT = 256
TILE = 256

norm_eps = 1e-05
scale = 1.0 / math.sqrt(HD)
bf16 = jnp.bfloat16
f32 = jnp.float32


def dot(a, b, ca, cb, out=f32):
    r = lax.dot_general(a, b, (((ca,), (cb,)), ((), ())), preferred_element_type=f32)
    return r.astype(out)


def tile_keys(t):
    prompt_tiles = PROMPT // TILE
    if t < prompt_tiles:
        return list(range(t + 1))
    per = CONT // TILE
    first = prompt_tiles + ((t - prompt_tiles) // per) * per
    return list(range(prompt_tiles)) + list(range(first, t + 1))


def load_tile(ref, perm, t, block, cols):
    per = TILE // block
    parts = [
        ref[pl.ds(pl.multiple_of(perm[t * per + i] * block, block), block), cols]
        for i in range(per)
    ]
    return parts[0] if per == 1 else jnp.concatenate(parts, axis=0)


def store_tile(ref, perm, t, block, cols, value):
    per = TILE // block
    for i in range(per):
        ref[pl.ds(pl.multiple_of(perm[t * per + i] * block, block), block), cols] = value[
            i * block : (i + 1) * block
        ]


def spread_keys(ref, tiles):
    runs, start = [], tiles[0]
    for a, b in zip(tiles, tiles[1:] + [None]):
        if b != a + 1:
            runs.append((start, a + 1))
            start = b
    parts = [ref[lo * TILE : hi * TILE, :] for lo, hi in runs]
    return parts[0] if len(parts) == 1 else jnp.concatenate(parts, axis=0)


def causal_fill(scores, value):
    width = scores.shape[1] - TILE
    row = lax.broadcasted_iota(jnp.int32, (TILE, TILE), 0)
    col = lax.broadcasted_iota(jnp.int32, (TILE, TILE), 1)
    last = jnp.where(col <= row, scores[:, width:], value)
    return last if width == 0 else jnp.concatenate([scores[:, :width], last], axis=1)


def forward_kernel(
    block, perm, pre_q, pre_k, pre_v, cos_ref, sin_ref, ctx_ref, q_ref, k_ref, v_ref, log_ref
):
    tiles = pre_q.shape[0] // TILE
    for t in range(tiles):
        rows = slice(t * TILE, (t + 1) * TILE)
        cos, sin = cos_ref[rows, :], sin_ref[rows, :]
        q = load_tile(pre_q, perm, t, block, slice(None))
        q_ref[rows, :] = (q * cos + pltpu.roll(q, HD // 2, 1) * sin).astype(bf16)
        k = load_tile(pre_k, perm, t, block, slice(None))
        k_ref[rows, :] = (k * cos + pltpu.roll(k, HD // 2, 1) * sin).astype(bf16)
        v_ref[rows, :] = load_tile(pre_v, perm, t, block, slice(None)).astype(bf16)
    for t in range(tiles):
        rows = slice(t * TILE, (t + 1) * TILE)
        seen = tile_keys(t)
        keys, values = spread_keys(k_ref, seen), spread_keys(v_ref, seen)
        scores = dot(q_ref[rows, :], keys, 1, 1) * scale
        scores = causal_fill(scores, -1e30)
        top = jnp.max(scores, axis=1, keepdims=True)
        expo = jnp.exp(scores - top)
        total = jnp.sum(expo, axis=1, keepdims=True)
        probs = (expo * (1.0 / total)).astype(bf16)
        context = dot(probs, values, 1, 0).astype(bf16)
        store_tile(ctx_ref, perm, t, block, slice(None), context)
        log_ref[rows, :] = jnp.broadcast_to(top + jnp.log(total), (TILE, HD))


def backward_kernel(
    block,
    perm,
    q_ref,
    k_ref,
    v_ref,
    log_ref,
    do_ref,
    cos_ref,
    sin_ref,
    out_q,
    out_k,
    out_v,
    dk_ref,
    dv_ref,
):
    tiles = q_ref.shape[0] // TILE
    dk_ref[...] = jnp.zeros_like(dk_ref)
    dv_ref[...] = jnp.zeros_like(dv_ref)
    for t in range(tiles):
        rows = slice(t * TILE, (t + 1) * TILE)
        seen = tile_keys(t)
        keys, values = spread_keys(k_ref, seen), spread_keys(v_ref, seen)
        query = q_ref[rows, :]
        grad = load_tile(do_ref, perm, t, block, slice(None))
        scores = dot(query, keys, 1, 1) * scale
        soft = causal_fill(jnp.exp(scores - log_ref[rows, 0:1]), 0.0)
        grad_prob = dot(grad, values, 1, 1)
        delta = jnp.sum(grad_prob * soft, axis=1, keepdims=True)
        grad_scores = (soft * (grad_prob - delta)).astype(bf16)
        values_back = dot(soft.astype(bf16), grad, 0, 0)
        keys_back = dot(grad_scores, query, 0, 0)
        for i, s in enumerate(seen):
            part, own = slice(i * TILE, (i + 1) * TILE), slice(s * TILE, (s + 1) * TILE)
            dv_ref[own, :] += values_back[part]
            dk_ref[own, :] += keys_back[part]
        back = dot(grad_scores, keys, 1, 0) * scale
        cos, sin = cos_ref[rows, :], sin_ref[rows, :]
        back = back * cos - pltpu.roll(back, HD // 2, 1) * sin
        store_tile(out_q, perm, t, block, slice(None), back.astype(bf16))
    for t in range(tiles):
        rows = slice(t * TILE, (t + 1) * TILE)
        cos, sin = cos_ref[rows, :], sin_ref[rows, :]
        back = dk_ref[rows, :] * scale
        back = back * cos - pltpu.roll(back, HD // 2, 1) * sin
        store_tile(out_k, perm, t, block, slice(None), back.astype(bf16))
        store_tile(out_v, perm, t, block, slice(None), dv_ref[rows, :].astype(bf16))


def attention_forward(perm, block, pre, cos, sin):
    rows, heads = pre[0].shape[0], pre[0].shape[1] // HD
    per_head = pl.BlockSpec((rows, HD), lambda h, p: (0, h))
    table = pl.BlockSpec((rows, HD), lambda h, p: (0, 0))
    head_array = jax.ShapeDtypeStruct((rows, heads * HD), bf16)
    return pl.pallas_call(
        functools.partial(forward_kernel, block),
        grid_spec=pltpu.PrefetchScalarGridSpec(
            num_scalar_prefetch=1,
            grid=(heads,),
            in_specs=[per_head] * 3 + [table, table],
            out_specs=[per_head] * 5,
        ),
        out_shape=[head_array] * 4 + [jax.ShapeDtypeStruct((rows, heads * HD), f32)],
        name="attention_forward",
    )(perm, *pre, cos, sin)


def attention_backward(perm, block, q, k, v, log_total, grad, cos, sin):
    rows, heads = q.shape[0], q.shape[1] // HD
    per_head = pl.BlockSpec((rows, HD), lambda h, p: (0, h))
    table = pl.BlockSpec((rows, HD), lambda h, p: (0, 0))
    return pl.pallas_call(
        functools.partial(backward_kernel, block),
        grid_spec=pltpu.PrefetchScalarGridSpec(
            num_scalar_prefetch=1,
            grid=(heads,),
            in_specs=[per_head] * 5 + [table, table],
            out_specs=[per_head] * 3,
            scratch_shapes=[pltpu.VMEM((rows, HD), f32), pltpu.VMEM((rows, HD), f32)],
        ),
        out_shape=[jax.ShapeDtypeStruct((rows, heads * HD), bf16)] * 3,
        name="attention_backward",
    )(perm, q, k, v, log_total, grad, cos, sin)


def expert_kernel(kept, x_ref, g_ref, wg_ref, wu_ref, wd_ref, *refs):
    hidden_ref, gate_ref, up_ref = refs[kept:]
    count = x_ref.shape[0] // 2
    for p in range(2):
        rows = slice(p * count, (p + 1) * count)
        gate = dot(x_ref[rows, :], wg_ref[...], 1, 1)
        up = dot(x_ref[rows, :], wu_ref[...], 1, 1)
        grad = dot(g_ref[rows, :], wd_ref[...], 1, 1)
        sigmoid = jax.nn.sigmoid(gate)
        silu = gate * sigmoid
        hidden_ref[rows, :] = (silu * up).astype(bf16)
        gate_ref[rows, :] = (grad * up * sigmoid * (1.0 + gate * (1.0 - sigmoid))).astype(bf16)
        up_ref[rows, :] = (grad * silu).astype(bf16)


def expert_hidden(part, parts, slots, grads, weights, kept):
    rows, units = slots.shape[0], weights[0].shape[0]
    tile = 256 if units % 256 == 0 else 128
    whole = pl.BlockSpec((rows, D), lambda i: (0, 0))
    weight = pl.BlockSpec((tile, D), lambda i: (i, 0))
    result = pl.BlockSpec((rows, tile), lambda i: (part, i))
    return pl.pallas_call(
        functools.partial(expert_kernel, len(kept)),
        grid=(units // tile,),
        in_specs=[whole] * 2 + [weight] * 3 + [pl.BlockSpec(memory_space=pl.ANY)] * len(kept),
        out_specs=[result] * 3,
        out_shape=[jax.ShapeDtypeStruct((parts * rows, units), bf16)] * 3,
        input_output_aliases={5 + i: i for i in range(len(kept))},
        name="expert_hidden",
    )(slots, grads, *weights, *kept)


def rope_tables(group_len):
    index = jnp.arange(group_len, dtype=jnp.int32)
    position = jnp.where(index < PROMPT, index, PROMPT + (index - PROMPT) % CONT).astype(f32)
    half = HD // 2
    frequency = jnp.exp(-math.log(10000.0) * jnp.arange(half, dtype=f32) / half)
    angles = position[:, None] * frequency[None, :]
    cosine, sine = jnp.cos(angles), jnp.sin(angles)
    return (
        jnp.concatenate([cosine, cosine], axis=1),
        jnp.concatenate([-sine, sine], axis=1),
    )


def after(*arrays):
    return lax.optimization_barrier(arrays)


def normalize_parts(values, gain):
    inverse = lax.rsqrt(jnp.mean(values * values, axis=-1, keepdims=True) + norm_eps)
    unit_rows = values * inverse
    return (unit_rows * gain, unit_rows, inverse)


def norm_backward(grad_outer, unit_rows, inverse, gain):
    grad_unit = grad_outer * gain
    grad_inner = inverse * (
        grad_unit - unit_rows * jnp.mean(grad_unit * unit_rows, axis=-1, keepdims=True)
    )
    return (grad_inner, jnp.sum(grad_outer * unit_rows, axis=0))


def shards(
    tokens,
    route_ids,
    gate_values,
    deal,
    norm1_gain,
    w_query,
    w_key,
    w_value,
    w_out,
    norm2_gain,
    w_gate,
    w_up,
    w_down,
    cotangent,
):
    rows = tokens.shape[1]
    ctx_count = lax.axis_size("ctx")
    fsdp_count = lax.axis_size("fsdp")
    group_len = rows * ctx_count
    capacity = 5 * rows * TOPK // (4 * EXPERTS)
    repeats = fsdp_count // EXPERTS
    pair = 2
    columns = repeats // pair
    core = lax.axis_index("ctx")
    expert = lax.axis_index("fsdp") // repeats
    width = D // ctx_count
    heads = HEADS // ctx_count

    def core_shift(a, s):
        return lax.ppermute(a, "ctx", [(i, (i + s) % ctx_count) for i in range(ctx_count)])

    def fsdp_shift(a, move):
        return lax.ppermute(a, "fsdp", [(i, move(i)) for i in range(fsdp_count)])

    def expert_shift(a, k):
        return fsdp_shift(a, lambda i: (i + k * repeats) % fsdp_count)

    def column_shift(a, j):
        def move(i):
            e, r = divmod(i, repeats)
            t, w = divmod(r, pair)
            return e * repeats + ((t + j) % columns) * pair + w

        return fsdp_shift(a, move)

    def pair_swap(a):
        return fsdp_shift(a, lambda i: i ^ 1)

    def core_gather(a):
        return jnp.concatenate([a] + [core_shift(a, s) for s in range(1, ctx_count)], axis=0)

    block_count = deal.shape[1]
    block = group_len // block_count
    local_blocks = block_count // ctx_count
    dealt = jnp.argsort(deal[0]).astype(jnp.int32)
    perm = ((core - dealt // local_blocks) % ctx_count) * local_blocks + dealt % local_blocks
    cos, sin = rope_tables(group_len)

    def own_columns(w):
        return lax.dynamic_slice_in_dim(w, core * width, width, axis=1)

    packed = jnp.concatenate([own_columns(w) for w in (w_query, w_key, w_value, w_out)], axis=1)
    gathered = lax.all_gather(packed, "fsdp", axis=0, tiled=True)

    halves = 2
    part_slots = capacity // halves
    half = EXPERTS * part_slots
    ids = route_ids[0]
    flat = ids.reshape(-1)
    onehot = (flat[:, None] == jnp.arange(EXPERTS, dtype=jnp.int32)[None, :]).astype(jnp.int32)
    earlier = jnp.cumsum(onehot, axis=0) - onehot
    slot = jnp.sum(earlier * onehot, axis=1)
    place = (slot // part_slots) * half + flat * part_slots + slot % part_slots
    place = jnp.where(slot < capacity, place, -1).reshape(rows, TOPK)
    targets = jnp.arange(halves * half, dtype=jnp.int32)
    select = [(place[:, k : k + 1] == targets[None, :]).astype(bf16) for k in range(TOPK)]
    spread = [(targets[:, None] == place[None, :, k]).astype(bf16) for k in range(TOPK)]
    gates = gate_values[0]

    dy = cotangent[0].astype(f32)
    grad_pairs = jnp.concatenate([(dy * gates[:, k : k + 1]).astype(bf16) for k in range(TOPK)])
    spread_both = jnp.concatenate(spread, axis=1)
    grad_blocks = [
        dot(spread_both[h * half : (h + 1) * half], grad_pairs, 1, 0, bf16) for h in range(halves)
    ]

    inputs = tokens[0].astype(f32)
    normed_f, _, _ = normalize_parts(inputs, norm1_gain)
    normed = core_gather(normed_f.astype(bf16))

    per = D // (ctx_count * fsdp_count)
    mine = lax.axis_index("fsdp")
    my_column, my_side = (mine % repeats) // pair, mine % pair

    def feature_order(side_first):
        index = jnp.arange(D, dtype=jnp.int32)
        rest, j = index // per, index % per
        rest, c = rest // ctx_count, rest % ctx_count
        rest, e = rest // EXPERTS, rest % EXPERTS
        if side_first:
            w, t = rest // columns, rest % columns
        else:
            t, w = rest // pair, rest % pair
        t, w = (my_column + t) % columns, (my_side + w) % pair
        source = c * (D // ctx_count) + (e * repeats + t * pair + w) * per + j
        shuffle = (jnp.arange(D, dtype=jnp.int32)[:, None] == source[None, :]).astype(bf16)
        return dot(normed, shuffle, 1, 0, bf16)

    normed_side, normed_column = feature_order(True), feature_order(False)

    def weight_part(w):
        count = w.shape[0] // ctx_count
        return lax.dynamic_slice_in_dim(w, core * count, count, axis=0)

    weight_parts = [weight_part(w) for w in (w_gate, w_up, w_down)]
    gathered, *tied = after(gathered, normed_side, normed_column, *grad_blocks, *weight_parts)
    normed_side, normed_column = tied[:2]
    grad_blocks, weight_parts = tied[2 : 2 + halves], tied[2 + halves :]
    full_q, full_k, full_v, out_columns = (
        gathered[:, i * width : (i + 1) * width] for i in range(4)
    )

    lines = [[r + e * repeats for e in range(EXPERTS)] for r in range(repeats)]

    def swap_experts(a, width=D):
        blocks = a.reshape(EXPERTS, -1, width)
        return lax.all_to_all(blocks, "fsdp", 0, 0, axis_index_groups=lines, tiled=True)

    def to_columns(a):
        return [a] + [column_shift(a, j) for j in range(1, columns)]

    grads_first = swap_experts(grad_blocks[0]).reshape(half, D)

    sides = [[i, i ^ 1] for i in range(0, fsdp_count, 2)]
    sides = [sorted(group) for group in sides]
    swapped = [
        lax.all_gather(part, "fsdp", axis=0, tiled=True, axis_index_groups=sides)
        for part in weight_parts
    ]

    def pair_weights(part):
        if ctx_count == 2:
            again = core_shift(part, 1)
            count = part.shape[0] // pair
            rows_of = []
            for i in range(pair):
                a, b = part[i * count : (i + 1) * count], again[i * count : (i + 1) * count]
                rows_of += [jnp.where(core == 0, a, b), jnp.where(core == 0, b, a)]
            return jnp.concatenate(rows_of, axis=0)
        every = lax.all_gather(part, "ctx", axis=0, tiled=False)
        return every.reshape(ctx_count, pair, -1, D).transpose(1, 0, 2, 3).reshape(-1, D)

    pre = [dot(normed, w, 1, 0) for w in (full_q, full_k, full_v)]
    context, q, k, v, log_total = attention_forward(perm, block, pre, cos, sin)

    def out_rows(c):
        return lax.dynamic_slice_in_dim(out_columns, (c % ctx_count) * width, width, axis=0)

    if ctx_count == 2:
        own_part, other = out_rows(core), core_shift(out_rows(core + 1), 1)
        w_o = jnp.concatenate(
            [jnp.where(core == 0, own_part, other), jnp.where(core == 0, other, own_part)], axis=1
        )
    else:
        w_o = lax.all_to_all(out_columns.reshape(ctx_count, width, width), "ctx", 0, 0)
        w_o = w_o.transpose(1, 0, 2).reshape(width, D)
    away = [dot(context[s * rows : (s + 1) * rows], w_o, 1, 0, bf16) for s in range(1, ctx_count)]
    attention = dot(context[:rows], w_o, 1, 0)
    for s in range(1, ctx_count):
        attention = attention + core_shift(away[s - 1], -s).astype(f32)
    hidden_in = inputs + attention
    normed_two_f, unit_two, inverse_two = normalize_parts(hidden_in, norm2_gain)
    normed_two = normed_two_f.astype(bf16)

    spread_any = spread[0] + spread[1]
    slot_blocks = [
        dot(spread_any[h * half : (h + 1) * half], normed_two, 1, 0, bf16) for h in range(halves)
    ]
    grads_first, waiting, _ = after(grads_first, grad_blocks[1], away[0])
    grads_second = swap_experts(waiting).reshape(half, D)
    grad_parts = to_columns(grads_first)
    got = after(grads_second, *slot_blocks, *swapped[:2], *grad_parts[1:])
    grads_second, slots_a, slots_b, *swapped_two = got[:5]
    grad_parts[1:] = got[5:]
    grad_parts += to_columns(grads_second)
    first = swap_experts(slots_a).reshape(half, D)
    wg, wu = (pair_weights(w) for w in swapped_two)
    got = after(first, slots_b, swapped[2], wg, wu, *grad_parts[columns + 1 :])
    first, slots_b, swapped_down, wg, wu = got[:5]
    grad_parts[columns + 1 :] = got[5:]
    second = swap_experts(slots_b).reshape(half, D)
    wd = pair_weights(swapped_down)
    weights = (wg, wu, wd)
    parts = halves * columns

    def hidden_part(index, slots, state):
        return expert_hidden(index, parts, slots, grad_parts[index], weights, state)

    def part_rows(index):
        return slice(index * half, (index + 1) * half)

    def grad_rows(index, state):
        part = part_rows(index)
        return (dot(state[1][part], wg, 1, 0) + dot(state[2][part], wu, 1, 0)).astype(bf16)

    def columns_home(pieces):
        return [column_shift(part, -(j + 1)) for j, part in enumerate(pieces)]

    def add_parts(own, returned):
        total = own.astype(f32)
        for part in returned:
            total = total + part.astype(f32)
        return total.astype(bf16)

    slot_parts = to_columns(first)
    state, back, came = (), {}, []
    home_first = None
    for h in range(halves):
        for j in range(columns):
            index = h * columns + j
            state = hidden_part(index, slot_parts[index], state)
            if index == 0:
                second, *got = after(second, *state, *slot_parts[1:])
                state, slot_parts[1:] = got[:3], got[3:]
                slot_parts += to_columns(second)
            if h == 1 and j == 0:
                tied = after(*state, *came[0])
                home_first = add_parts(back[0], tied[3:])
                *state, home_first = after(*tied[:3], home_first)
                home_first = swap_experts(home_first)
        for j in [*range(1, columns), 0]:
            index = h * columns + j
            back[index] = grad_rows(index, state)
            back[index], *state = after(back[index], *state)
        came.append(columns_home([back[h * columns + j] for j in range(1, columns)]))
    hidden, grad_gate, grad_up = state
    all_slots = jnp.concatenate(slot_parts, axis=0)
    all_grads = jnp.concatenate(grad_parts, axis=0)

    def core_sum(part):
        total = lax.dynamic_slice_in_dim(part, core * width, width, axis=1).astype(f32)
        for s in range(1, ctx_count):
            start = ((core + s) % ctx_count) * width
            total = total + core_shift(
                lax.dynamic_slice_in_dim(part, start, width, axis=1), s
            ).astype(f32)
        return total.astype(bf16)

    def side_sum(total):
        return lax.psum_scatter(
            total, "fsdp", scatter_dimension=0, tiled=True, axis_index_groups=sides
        ).astype(f32)

    hidden_t = after(hidden, *(back[i] for i in range(parts)))[0]
    down_part = dot(hidden_t, all_grads, 0, 0, bf16)
    down_part, gate_t, home_first, *came[1] = after(down_part, grad_gate, home_first, *came[1])
    home_second = swap_experts(add_parts(back[columns], came[1]))
    gate_part = dot(gate_t, all_slots, 0, 0, bf16)
    down_total = core_sum(down_part)
    gate_part, down_total, hidden_t = after(gate_part, down_total, hidden)
    down_grad = side_sum(down_total)

    gate_total = core_sum(gate_part)
    outs, away_out = [None] * parts, []
    for j in [*range(1, columns), 0]:
        for h in range(halves):
            outs[h * columns + j] = dot(hidden_t[part_rows(h * columns + j)], wd, 1, 0, bf16)
        if j:
            *tied, hidden_t = after(*(o for o in outs if o is not None), hidden_t)
    away_out = [columns_home(outs[h * columns + 1 : (h + 1) * columns]) for h in range(halves)]
    gate_total, home_second, *outs = after(gate_total, home_second, *outs)
    gate_grad = side_sum(gate_total)
    grad_slot_in = jnp.concatenate([home_first, home_second], axis=0).reshape(halves * half, D)

    grad_normed_two = dot(select[0] + select[1], grad_slot_in, 1, 0)
    grad_norm_two, norm2_part = norm_backward(grad_normed_two, unit_two, inverse_two, norm2_gain)
    grad_hidden_in = dy + grad_norm_two
    grad_attention = core_gather(grad_hidden_in.astype(bf16))
    def reduce_blocks(blocks, shift):
        total = blocks[0].astype(f32)
        for d in range(1, len(blocks)):
            total = total + shift(blocks[d].astype(bf16), d).astype(f32)
        return total.astype(bf16)

    def cut(a, n):
        size = a.shape[0] // n
        return [a[i * size : (i + 1) * size] for i in range(n)]

    def side_shift(a, d):
        return pair_swap(a)

    def first_blocks(left, grad, n):
        size = D // n
        return [dot(left[:, i * size : (i + 1) * size], grad, 0, 0, bf16) for i in range(n)]

    def expert_sum(total):
        blocks = swap_experts(total, total.shape[1])
        return jnp.sum(blocks.reshape(EXPERTS, -1, total.shape[1]).astype(f32), axis=0)

    def row_blocks(a, n, own):
        split = a.reshape(EXPERTS, n, -1, a.shape[1])
        return [
            lax.dynamic_slice_in_dim(split, (own + d) % n, 1, axis=1).reshape(-1, a.shape[1])
            for d in range(n)
        ]

    out_part = dot(context, grad_attention, 0, 0, bf16)
    blocks_o = row_blocks(out_part, columns, my_column)
    grad_attention, *blocks_o = after(grad_attention, *blocks_o)
    sum_o = reduce_blocks(blocks_o, column_shift)
    grad_context = dot(grad_attention, w_o, 1, 1, bf16)
    grad_q, grad_k, grad_v = attention_backward(
        perm, block, q, k, v, log_total, grad_context, cos, sin
    )
    grad_q, grad_k, grad_v, *away_out[0] = after(grad_q, grad_k, grad_v, *away_out[0])
    outs_first = swap_experts(add_parts(outs[0], away_out[0]))
    blocks_q = first_blocks(normed_side, grad_q, pair)
    blocks_k = first_blocks(normed_column, grad_k, columns)
    blocks_v = first_blocks(normed_side, grad_v, pair)
    up_t, *tied = after(grad_up, grad_q, grad_k, grad_v, *blocks_q, *blocks_k, *blocks_v)
    grad_q, grad_k, grad_v = tied[:3]
    tied = tied[3:]
    blocks_q, blocks_k, blocks_v = tied[:pair], tied[pair : pair + columns], tied[pair + columns :]
    sum_q = reduce_blocks(blocks_q, side_shift)
    sum_k = reduce_blocks(blocks_k, column_shift)
    sum_v = reduce_blocks(blocks_v, side_shift)
    up_part = dot(up_t, all_slots, 0, 0, bf16)

    def back_rows(s, out):
        part = slice(s * rows, (s + 1) * rows)
        total = dot(grad_q[part], full_q, 1, 1) + dot(grad_k[part], full_k, 1, 1)
        return (total + dot(grad_v[part], full_v, 1, 1)).astype(out)

    up_part, grad_q, grad_k, grad_v = after(up_part, grad_q, grad_k, grad_v)
    up_total = core_sum(up_part)
    back_away = [back_rows(s, bf16) for s in range(1, ctx_count)]
    grad_normed = back_rows(0, f32)

    sum_q, sum_o, grad_normed, up_total, outs_first, own, *away_out[1] = after(
        sum_q, sum_o, grad_normed, up_total, outs_first, outs[columns], *away_out[1]
    )
    up_grad = side_sum(up_total)
    outs_second = swap_experts(add_parts(own, away_out[1]))
    sum_q = reduce_blocks(cut(sum_q, columns), column_shift)
    sum_o = reduce_blocks(row_blocks(sum_o, pair, my_side), side_shift)
    for s in range(1, ctx_count):
        grad_normed = grad_normed + core_shift(back_away[s - 1], -s).astype(f32)
    _, unit_one, inverse_one = normalize_parts(inputs, norm1_gain)
    grad_norm_one, norm1_part = norm_backward(grad_normed, unit_one, inverse_one, norm1_gain)
    tokens_grad = (grad_hidden_in + grad_norm_one).astype(bf16)

    sum_k, sum_v, tokens_grad = after(sum_k, sum_v, tokens_grad)
    sum_k = reduce_blocks(cut(sum_k, pair), side_shift)
    sum_v = reduce_blocks(cut(sum_v, columns), column_shift)
    out_grad = expert_sum(sum_o)
    sums = jnp.stack([expert_sum(a) for a in (sum_q, sum_k, sum_v)]).reshape(
        3, ctx_count, per, width
    )

    def core_piece(c):
        return lax.dynamic_index_in_dim(sums, c % ctx_count, 1, keepdims=False)

    if ctx_count == 2:
        own_part, other = core_piece(core), core_shift(core_piece(core + 1), 1)
        qkv_own = jnp.concatenate(
            [jnp.where(core == 0, own_part, other), jnp.where(core == 0, other, own_part)], axis=2
        )
    else:
        qkv_own = lax.all_to_all(sums.astype(bf16), "ctx", 1, 1).astype(f32)
        qkv_own = qkv_own.transpose(0, 2, 1, 3).reshape(3, per, D)
    query_grad, key_grad, value_grad = qkv_own[0], qkv_own[1], qkv_own[2]

    gains = jnp.stack([norm1_part, norm2_part])
    step = 1
    while step < ctx_count:
        gains = gains + lax.ppermute(gains, "ctx", [(i, i ^ step) for i in range(ctx_count)])
        step *= 2
    step = 1
    while step < fsdp_count:
        gains = gains + fsdp_shift(gains, lambda i, step=step: i ^ step)
        step *= 2
    place_own = (core * fsdp_count + mine) * per
    gains_own = lax.dynamic_slice_in_dim(gains, place_own, per, axis=1)

    slot_out = jnp.concatenate([outs_first, outs_second], axis=0).reshape(halves * half, D)
    mixed = hidden_in
    for i in range(TOPK):
        mixed = mixed + dot(select[i], slot_out, 1, 0) * gates[:, i : i + 1]

    return (
        mixed.astype(bf16)[None],
        tokens_grad[None],
        gains_own[0],
        query_grad,
        key_grad,
        value_grad,
        out_grad,
        gains_own[1],
        gate_grad,
        up_grad,
        down_grad,
    )


def solution(mesh):
    in_specs = (
        P("fsdp", "ctx", None),
        P("fsdp", "ctx", None),
        P("fsdp", "ctx", None),
        P("fsdp", None),
        P(),
        P("fsdp", None),
        P("fsdp", None),
        P("fsdp", None),
        P("fsdp", None),
        P(),
        P("fsdp", None),
        P("fsdp", None),
        P("fsdp", None),
        P("fsdp", "ctx", None),
    )
    out_specs = (
        P("fsdp", "ctx", None),
        P("fsdp", "ctx", None),
        P(("ctx", "fsdp")),
        P(("ctx", "fsdp"), None),
        P(("ctx", "fsdp"), None),
        P(("ctx", "fsdp"), None),
        P(("ctx", "fsdp"), None),
        P(("ctx", "fsdp")),
        P("fsdp", "ctx"),
        P("fsdp", "ctx"),
        P("fsdp", "ctx"),
    )
    return jax.shard_map(shards, mesh=mesh, in_specs=in_specs, out_specs=out_specs, check_vma=False)
```

```python
import functools
import math

import jax
import jax.numpy as jnp
from jax import lax
from jax.experimental import pallas as pl
from jax.experimental.pallas import tpu as pltpu
from jax.sharding import PartitionSpec as P

D = 2048
HEADS = 16
HD = 128
EXPERTS = 4
TOPK = 2
PROMPT = 512
CONT = 256
TILE = 256

norm_eps = 1e-05
scale = 1.0 / math.sqrt(HD)
bf16 = jnp.bfloat16
f32 = jnp.float32


def dot(a, b, ca, cb, out=f32):
    r = lax.dot_general(a, b, (((ca,), (cb,)), ((), ())), preferred_element_type=f32)
    return r.astype(out)


def tile_keys(t):
    prompt_tiles = PROMPT // TILE
    if t < prompt_tiles:
        return list(range(t + 1))
    per = CONT // TILE
    first = prompt_tiles + ((t - prompt_tiles) // per) * per
    return list(range(prompt_tiles)) + list(range(first, t + 1))


def load_tile(ref, perm, t, block, cols):
    per = TILE // block
    parts = [
        ref[pl.ds(pl.multiple_of(perm[t * per + i] * block, block), block), cols]
        for i in range(per)
    ]
    return parts[0] if per == 1 else jnp.concatenate(parts, axis=0)


def store_tile(ref, perm, t, block, cols, value):
    per = TILE // block
    for i in range(per):
        ref[pl.ds(pl.multiple_of(perm[t * per + i] * block, block), block), cols] = value[
            i * block : (i + 1) * block
        ]


def spread_keys(ref, tiles):
    runs, start = [], tiles[0]
    for a, b in zip(tiles, tiles[1:] + [None]):
        if b != a + 1:
            runs.append((start, a + 1))
            start = b
    parts = [ref[lo * TILE : hi * TILE, :] for lo, hi in runs]
    return parts[0] if len(parts) == 1 else jnp.concatenate(parts, axis=0)


def causal_fill(scores, value):
    width = scores.shape[1] - TILE
    row = lax.broadcasted_iota(jnp.int32, (TILE, TILE), 0)
    col = lax.broadcasted_iota(jnp.int32, (TILE, TILE), 1)
    last = jnp.where(col <= row, scores[:, width:], value)
    return last if width == 0 else jnp.concatenate([scores[:, :width], last], axis=1)


def forward_kernel(
    block, perm, pre_q, pre_k, pre_v, cos_ref, sin_ref, ctx_ref, q_ref, k_ref, v_ref, log_ref
):
    tiles = pre_q.shape[0] // TILE
    for t in range(tiles):
        rows = slice(t * TILE, (t + 1) * TILE)
        cos, sin = cos_ref[rows, :], sin_ref[rows, :]
        q = load_tile(pre_q, perm, t, block, slice(None))
        q_ref[rows, :] = (q * cos + pltpu.roll(q, HD // 2, 1) * sin).astype(bf16)
        k = load_tile(pre_k, perm, t, block, slice(None))
        k_ref[rows, :] = (k * cos + pltpu.roll(k, HD // 2, 1) * sin).astype(bf16)
        v_ref[rows, :] = load_tile(pre_v, perm, t, block, slice(None)).astype(bf16)
    for t in range(tiles):
        rows = slice(t * TILE, (t + 1) * TILE)
        seen = tile_keys(t)
        keys, values = spread_keys(k_ref, seen), spread_keys(v_ref, seen)
        scores = dot(q_ref[rows, :], keys, 1, 1) * scale
        scores = causal_fill(scores, -1e30)
        top = jnp.max(scores, axis=1, keepdims=True)
        expo = jnp.exp(scores - top)
        total = jnp.sum(expo, axis=1, keepdims=True)
        probs = (expo * (1.0 / total)).astype(bf16)
        context = dot(probs, values, 1, 0).astype(bf16)
        store_tile(ctx_ref, perm, t, block, slice(None), context)
        log_ref[rows, :] = jnp.broadcast_to(top + jnp.log(total), (TILE, HD))


def backward_kernel(
    block,
    perm,
    q_ref,
    k_ref,
    v_ref,
    log_ref,
    do_ref,
    cos_ref,
    sin_ref,
    out_qk,
    out_v,
    dk_ref,
    dv_ref,
):
    tiles = q_ref.shape[0] // TILE
    dk_ref[...] = jnp.zeros_like(dk_ref)
    dv_ref[...] = jnp.zeros_like(dv_ref)
    for t in range(tiles):
        rows = slice(t * TILE, (t + 1) * TILE)
        seen = tile_keys(t)
        keys, values = spread_keys(k_ref, seen), spread_keys(v_ref, seen)
        query = q_ref[rows, :]
        grad = load_tile(do_ref, perm, t, block, slice(None))
        scores = dot(query, keys, 1, 1) * scale
        soft = causal_fill(jnp.exp(scores - log_ref[rows, 0:1]), 0.0)
        grad_prob = dot(grad, values, 1, 1)
        delta = jnp.sum(grad_prob * soft, axis=1, keepdims=True)
        grad_scores = (soft * (grad_prob - delta)).astype(bf16)
        values_back = dot(soft.astype(bf16), grad, 0, 0)
        keys_back = dot(grad_scores, query, 0, 0)
        for i, s in enumerate(seen):
            part, own = slice(i * TILE, (i + 1) * TILE), slice(s * TILE, (s + 1) * TILE)
            dv_ref[own, :] += values_back[part]
            dk_ref[own, :] += keys_back[part]
        back = dot(grad_scores, keys, 1, 0) * scale
        cos, sin = cos_ref[rows, :], sin_ref[rows, :]
        back = back * cos - pltpu.roll(back, HD // 2, 1) * sin
        store_tile(out_qk, perm, t, block, slice(0, HD), back.astype(bf16))
    for t in range(tiles):
        rows = slice(t * TILE, (t + 1) * TILE)
        cos, sin = cos_ref[rows, :], sin_ref[rows, :]
        back = dk_ref[rows, :] * scale
        back = back * cos - pltpu.roll(back, HD // 2, 1) * sin
        store_tile(out_qk, perm, t, block, slice(HD, 2 * HD), back.astype(bf16))
        store_tile(out_v, perm, t, block, slice(None), dv_ref[rows, :].astype(bf16))


def attention_forward(perm, block, pre, cos, sin):
    rows, heads = pre.shape[0], pre.shape[1] // (3 * HD)
    per_head = pl.BlockSpec((rows, HD), lambda h, p: (0, h))
    table = pl.BlockSpec((rows, HD), lambda h, p: (0, 0))
    head_array = jax.ShapeDtypeStruct((rows, heads * HD), bf16)
    return pl.pallas_call(
        functools.partial(forward_kernel, block),
        grid_spec=pltpu.PrefetchScalarGridSpec(
            num_scalar_prefetch=1,
            grid=(heads,),
            in_specs=[
                pl.BlockSpec((rows, HD), lambda h, p: (0, 2 * h)),
                pl.BlockSpec((rows, HD), lambda h, p: (0, 2 * h + 1)),
                pl.BlockSpec((rows, HD), lambda h, p: (0, 2 * heads + h)),
                table,
                table,
            ],
            out_specs=[per_head] * 5,
        ),
        out_shape=[head_array] * 4 + [jax.ShapeDtypeStruct((rows, heads * HD), f32)],
        name="attention_forward",
    )(perm, pre, pre, pre, cos, sin)


def attention_backward(perm, block, q, k, v, log_total, grad, cos, sin):
    rows, heads = q.shape[0], q.shape[1] // HD
    per_head = pl.BlockSpec((rows, HD), lambda h, p: (0, h))
    table = pl.BlockSpec((rows, HD), lambda h, p: (0, 0))
    return pl.pallas_call(
        functools.partial(backward_kernel, block),
        grid_spec=pltpu.PrefetchScalarGridSpec(
            num_scalar_prefetch=1,
            grid=(heads,),
            in_specs=[per_head] * 5 + [table, table],
            out_specs=[pl.BlockSpec((rows, 2 * HD), lambda h, p: (0, h)), per_head],
            scratch_shapes=[pltpu.VMEM((rows, HD), f32), pltpu.VMEM((rows, HD), f32)],
        ),
        out_shape=[
            jax.ShapeDtypeStruct((rows, 2 * heads * HD), bf16),
            jax.ShapeDtypeStruct((rows, heads * HD), bf16),
        ],
        name="attention_backward",
    )(perm, q, k, v, log_total, grad, cos, sin)


def expert_kernel(kept, x_ref, g_ref, wg_ref, wu_ref, wd_ref, *refs):
    hidden_ref, gate_ref, up_ref = refs[kept:]
    count = x_ref.shape[0] // 2
    for p in range(2):
        rows = slice(p * count, (p + 1) * count)
        gate = dot(x_ref[rows, :], wg_ref[...], 1, 1)
        up = dot(x_ref[rows, :], wu_ref[...], 1, 1)
        grad = dot(g_ref[rows, :], wd_ref[...], 1, 1)
        sigmoid = jax.nn.sigmoid(gate)
        silu = gate * sigmoid
        hidden_ref[rows, :] = (silu * up).astype(bf16)
        gate_ref[rows, :] = (grad * up * sigmoid * (1.0 + gate * (1.0 - sigmoid))).astype(bf16)
        up_ref[rows, :] = (grad * silu).astype(bf16)


def expert_hidden(part, parts, slots, grads, weights, kept):
    rows, units = slots.shape[0], weights[0].shape[0]
    tile = 256 if units % 256 == 0 else 128
    whole = pl.BlockSpec((rows, D), lambda i: (0, 0))
    weight = pl.BlockSpec((tile, D), lambda i: (i, 0))
    result = pl.BlockSpec((rows, tile), lambda i: (part, i))
    return pl.pallas_call(
        functools.partial(expert_kernel, len(kept)),
        grid=(units // tile,),
        in_specs=[whole] * 2 + [weight] * 3 + [pl.BlockSpec(memory_space=pl.ANY)] * len(kept),
        out_specs=[result] * 3,
        out_shape=[jax.ShapeDtypeStruct((parts * rows, units), bf16)] * 3,
        input_output_aliases={5 + i: i for i in range(len(kept))},
        name="expert_hidden",
    )(slots, grads, *weights, *kept)


def rows_kernel(count, *refs):
    total = dot(refs[0][...], refs[count][...], 1, 0)
    for i in range(1, count):
        total = total + dot(refs[i][...], refs[count + i][...], 1, 0)
    refs[-1][...] = total.astype(bf16)


def expert_rows(part, rows, left, right):
    units, tile = right[0].shape[0], 256
    return pl.pallas_call(
        functools.partial(rows_kernel, len(left)),
        grid=(D // tile,),
        in_specs=[pl.BlockSpec((rows, units), lambda n: (part, 0))] * len(left)
        + [pl.BlockSpec((units, tile), lambda n: (0, n))] * len(right),
        out_specs=pl.BlockSpec((rows, tile), lambda n: (0, n)),
        out_shape=jax.ShapeDtypeStruct((rows, D), bf16),
        name="expert_rows",
    )(*left, *right)


def join_kernel(where, own_ref, *refs):
    parts, out_ref, sems = refs[:-2], refs[-2], refs[-1]
    side, core = where[0], where[1]
    size, count = own_ref.shape[0], parts[0].shape[0]
    copies = [
        pltpu.make_async_copy(
            own_ref, out_ref.at[pl.ds(pl.multiple_of(side * size, 8), size)], sems.at[0]
        )
    ]
    for s, part in enumerate(parts):
        source = lax.rem(core - s + len(parts), len(parts))
        start = pl.multiple_of((1 - side) * size + source * count, 8)
        copies.append(
            pltpu.make_async_copy(part, out_ref.at[pl.ds(start, count)], sems.at[1 + s])
        )
    for copy in copies:
        copy.start()
    for copy in copies:
        copy.wait()


def join_weights(where, own, parts):
    anywhere = pl.BlockSpec(memory_space=pl.ANY)
    return pl.pallas_call(
        join_kernel,
        grid_spec=pltpu.PrefetchScalarGridSpec(
            num_scalar_prefetch=1,
            grid=(1,),
            in_specs=[anywhere] * (1 + len(parts)),
            out_specs=anywhere,
            scratch_shapes=[pltpu.SemaphoreType.DMA((1 + len(parts),))],
        ),
        out_shape=jax.ShapeDtypeStruct((2 * own.shape[0], own.shape[1]), own.dtype),
        name="join_weights",
    )(where, own, *parts)


def rope_tables(group_len):
    index = jnp.arange(group_len, dtype=jnp.int32)
    position = jnp.where(index < PROMPT, index, PROMPT + (index - PROMPT) % CONT).astype(f32)
    half = HD // 2
    frequency = jnp.exp(-math.log(10000.0) * jnp.arange(half, dtype=f32) / half)
    angles = position[:, None] * frequency[None, :]
    cosine, sine = jnp.cos(angles), jnp.sin(angles)
    return (
        jnp.concatenate([cosine, cosine], axis=1),
        jnp.concatenate([-sine, sine], axis=1),
    )


def after(*arrays):
    return lax.optimization_barrier(arrays)


def normalize_parts(values, gain):
    inverse = lax.rsqrt(jnp.mean(values * values, axis=-1, keepdims=True) + norm_eps)
    unit_rows = values * inverse
    return (unit_rows * gain, unit_rows, inverse)


def norm_backward(grad_outer, unit_rows, inverse, gain):
    grad_unit = grad_outer * gain
    grad_inner = inverse * (
        grad_unit - unit_rows * jnp.mean(grad_unit * unit_rows, axis=-1, keepdims=True)
    )
    return (grad_inner, jnp.sum(grad_outer * unit_rows, axis=0))


def shards(
    tokens,
    route_ids,
    gate_values,
    deal,
    norm1_gain,
    w_query,
    w_key,
    w_value,
    w_out,
    norm2_gain,
    w_gate,
    w_up,
    w_down,
    cotangent,
):
    rows = tokens.shape[1]
    ctx_count = lax.axis_size("ctx")
    fsdp_count = lax.axis_size("fsdp")
    group_len = rows * ctx_count
    capacity = 5 * rows * TOPK // (4 * EXPERTS)
    repeats = fsdp_count // EXPERTS
    pair = 2
    columns = repeats // pair
    core = lax.axis_index("ctx")
    expert = lax.axis_index("fsdp") // repeats
    width = D // ctx_count
    heads = HEADS // ctx_count

    def core_shift(a, s):
        return lax.ppermute(a, "ctx", [(i, (i + s) % ctx_count) for i in range(ctx_count)])

    def fsdp_shift(a, move):
        return lax.ppermute(a, "fsdp", [(i, move(i)) for i in range(fsdp_count)])

    def expert_shift(a, k):
        return fsdp_shift(a, lambda i: (i + k * repeats) % fsdp_count)

    def column_shift(a, j):
        def move(i):
            e, r = divmod(i, repeats)
            t, w = divmod(r, pair)
            return e * repeats + ((t + j) % columns) * pair + w

        return fsdp_shift(a, move)

    def pair_swap(a):
        return fsdp_shift(a, lambda i: i ^ 1)

    def core_gather(a):
        return jnp.concatenate([a] + [core_shift(a, s) for s in range(1, ctx_count)], axis=0)

    block_count = deal.shape[1]
    block = group_len // block_count
    local_blocks = block_count // ctx_count
    dealt = jnp.argsort(deal[0]).astype(jnp.int32)
    perm = ((core - dealt // local_blocks) % ctx_count) * local_blocks + dealt % local_blocks
    cos, sin = rope_tables(group_len)

    def own_columns(w):
        return lax.dynamic_slice_in_dim(w, core * width, width, axis=1)

    by_head = [own_columns(w).reshape(-1, heads, HD) for w in (w_query, w_key)]
    packed = jnp.concatenate(
        [jnp.stack(by_head, axis=2).reshape(-1, 2 * width), own_columns(w_value), own_columns(w_out)],
        axis=1,
    )
    gathered = lax.all_gather(packed, "fsdp", axis=0, tiled=True)

    halves = 2
    part_slots = capacity // halves
    half = EXPERTS * part_slots
    ids = route_ids[0]
    flat = ids.reshape(-1)
    onehot = (flat[:, None] == jnp.arange(EXPERTS, dtype=jnp.int32)[None, :]).astype(jnp.int32)
    earlier = jnp.cumsum(onehot, axis=0) - onehot
    slot = jnp.sum(earlier * onehot, axis=1)
    place = (slot // part_slots) * half + flat * part_slots + slot % part_slots
    place = jnp.where(slot < capacity, place, -1).reshape(rows, TOPK)
    targets = jnp.arange(halves * half, dtype=jnp.int32)
    select = [(place[:, k : k + 1] == targets[None, :]).astype(bf16) for k in range(TOPK)]
    spread = [(targets[:, None] == place[None, :, k]).astype(bf16) for k in range(TOPK)]
    gates = gate_values[0]

    dy = cotangent[0].astype(f32)
    grad_pairs = jnp.concatenate([(dy * gates[:, k : k + 1]).astype(bf16) for k in range(TOPK)])
    spread_both = jnp.concatenate(spread, axis=1)
    grad_blocks = [
        dot(spread_both[h * half : (h + 1) * half], grad_pairs, 1, 0, bf16) for h in range(halves)
    ]

    inputs = tokens[0].astype(f32)
    normed_f, _, _ = normalize_parts(inputs, norm1_gain)
    normed = core_gather(normed_f.astype(bf16))

    per = D // (ctx_count * fsdp_count)
    mine = lax.axis_index("fsdp")
    my_column, my_side = (mine % repeats) // pair, mine % pair

    def feature_order(relative):
        index = jnp.arange(D, dtype=jnp.int32)
        rest, j = index // per, index % per
        rest, c = rest // ctx_count, rest % ctx_count
        if relative:
            rest, e = rest // EXPERTS, rest % EXPERTS
            w, t = rest // columns, rest % columns
            t, w = (my_column + t) % columns, (my_side + w) % pair
            rest = e * repeats + t * pair + w
        source = c * (D // ctx_count) + rest * per + j
        shuffle = (jnp.arange(D, dtype=jnp.int32)[:, None] == source[None, :]).astype(bf16)
        return dot(normed, shuffle, 1, 0, bf16)

    normed_side, normed_mixed = feature_order(True), feature_order(False)

    def weight_part(w):
        count = w.shape[0] // ctx_count
        return lax.dynamic_slice_in_dim(w, core * count, count, axis=0)

    weight_parts = [weight_part(w) for w in (w_gate, w_up, w_down)]
    gathered, *tied = after(gathered, normed_side, normed_mixed, *grad_blocks, *weight_parts)
    normed_side, normed_mixed = tied[:2]
    grad_blocks, weight_parts = tied[2 : 2 + halves], tied[2 + halves :]
    full_qk, full_v = gathered[:, : 2 * width], gathered[:, 2 * width : 3 * width]
    out_columns = gathered[:, 3 * width :]
    full_qkv = gathered[:, : 3 * width]

    lines = [[r + e * repeats for e in range(EXPERTS)] for r in range(repeats)]

    def swap_experts(a, width=D):
        blocks = a.reshape(EXPERTS, -1, width)
        return lax.all_to_all(blocks, "fsdp", 0, 0, axis_index_groups=lines, tiled=True)

    def to_columns(a):
        return [a] + [column_shift(a, j) for j in range(1, columns)]

    grads_first = swap_experts(grad_blocks[0]).reshape(half, D)

    sides = [[i, i ^ 1] for i in range(0, fsdp_count, 2)]
    sides = [sorted(group) for group in sides]
    swapped = [
        lax.all_gather(part, "fsdp", axis=0, tiled=True, axis_index_groups=sides)
        for part in weight_parts
    ]

    where = jnp.stack([my_side, core]).astype(jnp.int32)

    def pair_weights(own, both):
        count = both.shape[0] // pair
        part = lax.dynamic_slice_in_dim(both, (1 - my_side) * count, count, axis=0)
        return join_weights(
            where, own, [part] + [core_shift(part, s) for s in range(1, ctx_count)]
        )

    pre = dot(normed, full_qkv, 1, 0)
    context, q, k, v, log_total = attention_forward(perm, block, pre, cos, sin)

    def out_rows(c):
        return lax.dynamic_slice_in_dim(out_columns, (c % ctx_count) * width, width, axis=0)

    if ctx_count == 2:
        own_part, other = out_rows(core), core_shift(out_rows(core + 1), 1)
        w_o = jnp.concatenate(
            [jnp.where(core == 0, own_part, other), jnp.where(core == 0, other, own_part)], axis=1
        )
    else:
        w_o = lax.all_to_all(out_columns.reshape(ctx_count, width, width), "ctx", 0, 0)
        w_o = w_o.transpose(1, 0, 2).reshape(width, D)
    away = [dot(context[s * rows : (s + 1) * rows], w_o, 1, 0, bf16) for s in range(1, ctx_count)]
    attention = dot(context[:rows], w_o, 1, 0)
    for s in range(1, ctx_count):
        attention = attention + core_shift(away[s - 1], -s).astype(f32)
    hidden_in = inputs + attention
    normed_two_f, unit_two, inverse_two = normalize_parts(hidden_in, norm2_gain)
    normed_two = normed_two_f.astype(bf16)

    spread_any = spread[0] + spread[1]
    slot_blocks = [
        dot(spread_any[h * half : (h + 1) * half], normed_two, 1, 0, bf16) for h in range(halves)
    ]
    grads_first, waiting, _ = after(grads_first, grad_blocks[1], away[0])
    grads_second = swap_experts(waiting).reshape(half, D)
    grad_parts = to_columns(grads_first)
    got = after(grads_second, *slot_blocks, *swapped[:2], *grad_parts[1:])
    grads_second, slots_a, slots_b, *swapped_two = got[:5]
    grad_parts[1:] = got[5:]
    grad_parts += to_columns(grads_second)
    first = swap_experts(slots_a).reshape(half, D)
    wg, wu = (pair_weights(*w) for w in zip((w_gate, w_up), swapped_two))
    got = after(first, slots_b, swapped[2], wg, wu, *grad_parts[columns + 1 :])
    first, slots_b, swapped_down, wg, wu = got[:5]
    grad_parts[columns + 1 :] = got[5:]
    second = swap_experts(slots_b).reshape(half, D)
    wd = pair_weights(w_down, swapped_down)
    weights = (wg, wu, wd)
    parts = halves * columns

    def hidden_part(index, slots, state):
        return expert_hidden(index, parts, slots, grad_parts[index], weights, state)

    def grad_rows(index, state):
        return expert_rows(index, half, state[1:], (wg, wu))

    def columns_home(pieces):
        return [column_shift(part, -(j + 1)) for j, part in enumerate(pieces)]

    def add_parts(own, returned):
        total = own.astype(f32)
        for part in returned:
            total = total + part.astype(f32)
        return total.astype(bf16)

    slot_parts = to_columns(first)
    state, back, came = (), {}, []
    home_first = None
    for h in range(halves):
        for j in range(columns):
            index = h * columns + j
            state = hidden_part(index, slot_parts[index], state)
            if index == 0:
                second, *got = after(second, *state, *slot_parts[1:])
                state, slot_parts[1:] = got[:3], got[3:]
                slot_parts += to_columns(second)
            if h == 1 and j == 0:
                tied = after(*state, *came[0])
                home_first = add_parts(back[0], tied[3:])
                *state, home_first = after(*tied[:3], home_first)
                home_first = swap_experts(home_first)
        for j in [*range(1, columns), 0]:
            index = h * columns + j
            back[index] = grad_rows(index, state)
            tied = after(back[index], *state, *slot_parts[(1 + h) * columns + 1 :])
            back[index], state = tied[0], tied[1:4]
            slot_parts[(1 + h) * columns + 1 :] = tied[4:]
            if h == 1 and j == columns - 1:
                home_first, *state = after(home_first, *state)
        came.append(columns_home([back[h * columns + j] for j in range(1, columns)]))
    hidden, grad_gate, grad_up = state
    all_slots = jnp.concatenate(slot_parts, axis=0)
    all_grads = jnp.concatenate(grad_parts, axis=0)

    def core_sum(part):
        total = lax.dynamic_slice_in_dim(part, core * width, width, axis=1).astype(f32)
        for s in range(1, ctx_count):
            start = ((core + s) % ctx_count) * width
            total = total + core_shift(
                lax.dynamic_slice_in_dim(part, start, width, axis=1), s
            ).astype(f32)
        return total.astype(bf16)

    def side_sum(total):
        return lax.psum_scatter(
            total, "fsdp", scatter_dimension=0, tiled=True, axis_index_groups=sides
        ).astype(f32)

    def out_rows_of(h, j, left):
        return expert_rows(h * columns + j, half, (left,), (wd,))

    hidden_t = after(hidden, *(back[i] for i in range(parts)))[0]
    down_part = dot(hidden_t, all_grads, 0, 0, bf16)
    down_part, hidden_t, gate_t, *got = after(down_part, hidden_t, grad_gate, *came[1])
    home_second = swap_experts(add_parts(back[columns], got))
    gate_part = dot(gate_t, all_slots, 0, 0, bf16)
    down_total = core_sum(down_part)
    gate_part, hidden_t = after(gate_part, hidden_t)
    away_first = [out_rows_of(0, j, hidden_t) for j in range(1, columns)]
    own_first = out_rows_of(0, 0, hidden_t)
    home_second, down_total, hidden_t, own_first, *away_first = after(
        home_second, down_total, hidden_t, own_first, *away_first
    )
    down_grad = side_sum(down_total)
    away_first = columns_home(away_first)

    def side_swap_sum(total):
        def side_rows(i):
            size = total.shape[0] // pair
            return lax.dynamic_slice_in_dim(total, (i % pair) * size, size, axis=0)

        return side_rows(my_side), pair_swap(side_rows(my_side + 1))

    gate_total = core_sum(gate_part)
    grad_slot_in = jnp.concatenate([home_first, home_second], axis=0).reshape(halves * half, D)

    grad_normed_two = dot(select[0] + select[1], grad_slot_in, 1, 0)
    grad_norm_two, norm2_part = norm_backward(grad_normed_two, unit_two, inverse_two, norm2_gain)
    grad_hidden_in = dy + grad_norm_two
    grad_attention = core_gather(grad_hidden_in.astype(bf16))
    def reduce_blocks(blocks, shift):
        total = blocks[0].astype(f32)
        for d in range(1, len(blocks)):
            total = total + shift(blocks[d].astype(bf16), d).astype(f32)
        return total.astype(bf16)

    def cut(a, n):
        size = a.shape[0] // n
        return [a[i * size : (i + 1) * size] for i in range(n)]

    def side_shift(a, d):
        return pair_swap(a)

    def first_blocks(left, grad, n):
        size = D // n
        return [dot(left[:, i * size : (i + 1) * size], grad, 0, 0, bf16) for i in range(n)]

    def expert_sum(total):
        blocks = swap_experts(total, total.shape[1])
        return jnp.sum(blocks.reshape(EXPERTS, -1, total.shape[1]).astype(f32), axis=0)

    def row_blocks(a, n, own):
        split = a.reshape(EXPERTS, n, -1, a.shape[1])
        return [
            lax.dynamic_slice_in_dim(split, (own + d) % n, 1, axis=1).reshape(-1, a.shape[1])
            for d in range(n)
        ]

    out_part = dot(context, grad_attention, 0, 0, bf16)
    blocks_o = row_blocks(out_part, columns, my_column)
    got = after(grad_attention, gate_total, *blocks_o)
    grad_attention, gate_total, blocks_o = got[0], got[1], got[2:]
    gate_own, gate_came = side_swap_sum(gate_total)
    came_o = [column_shift(block, d) for d, block in enumerate(blocks_o) if d]
    grad_context = dot(grad_attention, w_o, 1, 1, bf16)
    grad_qk, grad_v = attention_backward(
        perm, block, q, k, v, log_total, grad_context, cos, sin
    )
    qk_part = dot(normed_mixed, grad_qk, 0, 0, bf16)
    qk_sum = lax.psum_scatter(qk_part, "fsdp", scatter_dimension=0, tiled=True)
    got = after(qk_part, grad_qk, grad_v, hidden_t, grad_up, down_grad, *away_first)
    grad_qk, grad_v, hidden_t, up_t, down_grad, *away_first = got[1:]
    outs_first = swap_experts(add_parts(own_first, away_first))
    blocks_v = first_blocks(normed_side, grad_v, pair)
    hidden_t, grad_qk, grad_v, *blocks_v = after(hidden_t, grad_qk, grad_v, *blocks_v)
    away_second = [out_rows_of(1, j, hidden_t) for j in range(1, columns)]
    hidden_t, grad_qk, grad_v, *away_second = after(hidden_t, grad_qk, grad_v, *away_second)
    away_second = columns_home(away_second)

    def back_rows(s, out):
        part = slice(s * rows, (s + 1) * rows)
        return (dot(grad_qk[part], full_qk, 1, 1) + dot(grad_v[part], full_v, 1, 1)).astype(out)

    back_away = [back_rows(s, bf16) for s in range(1, ctx_count)]
    grad_normed = back_rows(0, f32)
    grad_normed, gate_own, gate_came, *came_o = after(grad_normed, gate_own, gate_came, *came_o)
    gate_grad = gate_own.astype(f32) + gate_came.astype(f32)
    sum_o = add_parts(blocks_o[0], came_o)
    sum_o = reduce_blocks(row_blocks(sum_o, pair, my_side), side_shift)
    for s in range(1, ctx_count):
        grad_normed = grad_normed + core_shift(back_away[s - 1], -s).astype(f32)
    _, unit_one, inverse_one = normalize_parts(inputs, norm1_gain)
    grad_norm_one, norm1_part = norm_backward(grad_normed, unit_one, inverse_one, norm1_gain)
    tokens_grad = (grad_hidden_in + grad_norm_one).astype(bf16)
    up_t, norm1_part, tokens_grad, *away_second = after(
        up_t, norm1_part, tokens_grad, *away_second
    )

    up_part = dot(up_t, all_slots, 0, 0, bf16)
    came_v = [side_shift(block, d) for d, block in enumerate(blocks_v) if d]
    up_part, sum_o, outs_first, hidden_t, *came_v = after(
        up_part, sum_o, outs_first, hidden_t, *came_v
    )
    sum_v = reduce_blocks(cut(add_parts(blocks_v[0], came_v), columns), column_shift)
    out_grad = expert_sum(sum_o)
    up_total = core_sum(up_part)
    own_second = out_rows_of(1, 0, hidden_t)
    own_second, up_total, out_grad, sum_v, qk_sum = after(
        own_second, up_total, out_grad, sum_v, qk_sum
    )
    up_own, up_came = side_swap_sum(up_total)

    gains = jnp.stack([norm1_part, norm2_part]).reshape(2, ctx_count, fsdp_count, per)
    gains = lax.all_to_all(gains.transpose(2, 1, 0, 3), "fsdp", 0, 0, tiled=True)
    gains = jnp.sum(gains, axis=0)

    def gains_of(c):
        return lax.dynamic_index_in_dim(gains, c % ctx_count, 0, keepdims=False)

    gains_own = gains_of(core)
    for s in range(1, ctx_count):
        gains_own = gains_own + core_shift(gains_of(core + s), s)
    value_part = expert_sum(sum_v).reshape(ctx_count, per, width)
    outs_second = swap_experts(add_parts(own_second, away_second))
    up_grad = up_own.astype(f32) + up_came.astype(f32)
    qk_parts = qk_sum.astype(f32).reshape(ctx_count, per, heads, 2, HD)
    sums = jnp.stack(
        [
            qk_parts[:, :, :, 0].reshape(ctx_count, per, width),
            qk_parts[:, :, :, 1].reshape(ctx_count, per, width),
            value_part,
        ]
    )

    def core_piece(c):
        return lax.dynamic_index_in_dim(sums, c % ctx_count, 1, keepdims=False)

    if ctx_count == 2:
        own_part, other = core_piece(core), core_shift(core_piece(core + 1), 1)
        qkv_own = jnp.concatenate(
            [jnp.where(core == 0, own_part, other), jnp.where(core == 0, other, own_part)], axis=2
        )
    else:
        qkv_own = lax.all_to_all(sums.astype(bf16), "ctx", 1, 1).astype(f32)
        qkv_own = qkv_own.transpose(0, 2, 1, 3).reshape(3, per, D)
    query_grad, key_grad, value_grad = qkv_own[0], qkv_own[1], qkv_own[2]

    slot_out = jnp.concatenate([outs_first, outs_second], axis=0).reshape(halves * half, D)
    mixed = hidden_in
    for i in range(TOPK):
        mixed = mixed + dot(select[i], slot_out, 1, 0) * gates[:, i : i + 1]

    return (
        mixed.astype(bf16)[None],
        tokens_grad[None],
        gains_own[0],
        query_grad,
        key_grad,
        value_grad,
        out_grad,
        gains_own[1],
        gate_grad,
        up_grad,
        down_grad,
    )


def solution(mesh):
    in_specs = (
        P("fsdp", "ctx", None),
        P("fsdp", "ctx", None),
        P("fsdp", "ctx", None),
        P("fsdp", None),
        P(),
        P("fsdp", None),
        P("fsdp", None),
        P("fsdp", None),
        P("fsdp", None),
        P(),
        P("fsdp", None),
        P("fsdp", None),
        P("fsdp", None),
        P("fsdp", "ctx", None),
    )
    out_specs = (
        P("fsdp", "ctx", None),
        P("fsdp", "ctx", None),
        P(("ctx", "fsdp")),
        P(("ctx", "fsdp"), None),
        P(("ctx", "fsdp"), None),
        P(("ctx", "fsdp"), None),
        P(("ctx", "fsdp"), None),
        P(("ctx", "fsdp")),
        P("fsdp", "ctx"),
        P("fsdp", "ctx"),
        P("fsdp", "ctx"),
    )
    return jax.shard_map(shards, mesh=mesh, in_specs=in_specs, out_specs=out_specs, check_vma=False)
```

```python
import functools
import math

import jax
import jax.numpy as jnp
from jax import lax
from jax.experimental import pallas as pl
from jax.experimental.layout import Layout, with_layout_constraint
from jax.experimental.pallas import tpu as pltpu
from jax.sharding import PartitionSpec as P

D = 2048
HEADS = 16
HD = 128
EXPERTS = 4
TOPK = 2
PROMPT = 512
CONT = 256
TILE = 256

norm_eps = 1e-05
scale = 1.0 / math.sqrt(HD)
bf16 = jnp.bfloat16
f32 = jnp.float32


def dot(a, b, ca, cb, out=f32):
    r = lax.dot_general(a, b, (((ca,), (cb,)), ((), ())), preferred_element_type=f32)
    return r.astype(out)


def tile_keys(t):
    prompt_tiles = PROMPT // TILE
    if t < prompt_tiles:
        return list(range(t + 1))
    per = CONT // TILE
    first = prompt_tiles + ((t - prompt_tiles) // per) * per
    return list(range(prompt_tiles)) + list(range(first, t + 1))


def load_tile(ref, perm, t, block, cols):
    per = TILE // block
    parts = [
        ref[pl.ds(pl.multiple_of(perm[t * per + i] * block, block), block), cols]
        for i in range(per)
    ]
    return parts[0] if per == 1 else jnp.concatenate(parts, axis=0)


def store_tile(ref, perm, t, block, cols, value):
    per = TILE // block
    for i in range(per):
        ref[pl.ds(pl.multiple_of(perm[t * per + i] * block, block), block), cols] = value[
            i * block : (i + 1) * block
        ]


def spread_keys(ref, tiles):
    runs, start = [], tiles[0]
    for a, b in zip(tiles, tiles[1:] + [None]):
        if b != a + 1:
            runs.append((start, a + 1))
            start = b
    parts = [ref[lo * TILE : hi * TILE, :] for lo, hi in runs]
    return parts[0] if len(parts) == 1 else jnp.concatenate(parts, axis=0)


def causal_fill(scores, value):
    width = scores.shape[1] - TILE
    row = lax.broadcasted_iota(jnp.int32, (TILE, TILE), 0)
    col = lax.broadcasted_iota(jnp.int32, (TILE, TILE), 1)
    last = jnp.where(col <= row, scores[:, width:], value)
    return last if width == 0 else jnp.concatenate([scores[:, :width], last], axis=1)


def forward_kernel(
    block, perm, pre_q, pre_k, pre_v, cos_ref, sin_ref, ctx_ref, q_ref, k_ref, v_ref, log_ref
):
    tiles = pre_q.shape[0] // TILE
    for t in range(tiles):
        rows = slice(t * TILE, (t + 1) * TILE)
        cos, sin = cos_ref[rows, :], sin_ref[rows, :]
        q = load_tile(pre_q, perm, t, block, slice(None))
        q_ref[rows, :] = (q * cos + pltpu.roll(q, HD // 2, 1) * sin).astype(bf16)
        k = load_tile(pre_k, perm, t, block, slice(None))
        k_ref[rows, :] = (k * cos + pltpu.roll(k, HD // 2, 1) * sin).astype(bf16)
        v_ref[rows, :] = load_tile(pre_v, perm, t, block, slice(None)).astype(bf16)
    for t in range(tiles):
        rows = slice(t * TILE, (t + 1) * TILE)
        seen = tile_keys(t)
        keys, values = spread_keys(k_ref, seen), spread_keys(v_ref, seen)
        scores = dot(q_ref[rows, :], keys, 1, 1) * scale
        scores = causal_fill(scores, -1e30)
        top = jnp.max(scores, axis=1, keepdims=True)
        expo = jnp.exp(scores - top)
        total = jnp.sum(expo, axis=1, keepdims=True)
        probs = (expo * (1.0 / total)).astype(bf16)
        context = dot(probs, values, 1, 0).astype(bf16)
        store_tile(ctx_ref, perm, t, block, slice(None), context)
        log_ref[rows, :] = jnp.broadcast_to(top + jnp.log(total), (TILE, HD))


def backward_kernel(
    block,
    perm,
    q_ref,
    k_ref,
    v_ref,
    log_ref,
    do_ref,
    cos_ref,
    sin_ref,
    out_qk,
    out_v,
    dk_ref,
    dv_ref,
):
    tiles = q_ref.shape[0] // TILE
    dk_ref[...] = jnp.zeros_like(dk_ref)
    dv_ref[...] = jnp.zeros_like(dv_ref)
    for t in range(tiles):
        rows = slice(t * TILE, (t + 1) * TILE)
        seen = tile_keys(t)
        keys, values = spread_keys(k_ref, seen), spread_keys(v_ref, seen)
        query = q_ref[rows, :]
        grad = load_tile(do_ref, perm, t, block, slice(None))
        scores = dot(query, keys, 1, 1) * scale
        soft = causal_fill(jnp.exp(scores - log_ref[rows, 0:1]), 0.0)
        grad_prob = dot(grad, values, 1, 1)
        delta = jnp.sum(grad_prob * soft, axis=1, keepdims=True)
        grad_scores = (soft * (grad_prob - delta)).astype(bf16)
        values_back = dot(soft.astype(bf16), grad, 0, 0)
        keys_back = dot(grad_scores, query, 0, 0)
        for i, s in enumerate(seen):
            part, own = slice(i * TILE, (i + 1) * TILE), slice(s * TILE, (s + 1) * TILE)
            dv_ref[own, :] += values_back[part]
            dk_ref[own, :] += keys_back[part]
        back = dot(grad_scores, keys, 1, 0) * scale
        cos, sin = cos_ref[rows, :], sin_ref[rows, :]
        back = back * cos - pltpu.roll(back, HD // 2, 1) * sin
        store_tile(out_qk, perm, t, block, slice(0, HD), back.astype(bf16))
    for t in range(tiles):
        rows = slice(t * TILE, (t + 1) * TILE)
        cos, sin = cos_ref[rows, :], sin_ref[rows, :]
        back = dk_ref[rows, :] * scale
        back = back * cos - pltpu.roll(back, HD // 2, 1) * sin
        store_tile(out_qk, perm, t, block, slice(HD, 2 * HD), back.astype(bf16))
        store_tile(out_v, perm, t, block, slice(None), dv_ref[rows, :].astype(bf16))


def attention_forward(perm, block, pre, cos, sin):
    rows, heads = pre.shape[0], pre.shape[1] // (3 * HD)
    per_head = pl.BlockSpec((rows, HD), lambda h, p: (0, h))
    table = pl.BlockSpec((rows, HD), lambda h, p: (0, 0))
    head_array = jax.ShapeDtypeStruct((rows, heads * HD), bf16)
    return pl.pallas_call(
        functools.partial(forward_kernel, block),
        grid_spec=pltpu.PrefetchScalarGridSpec(
            num_scalar_prefetch=1,
            grid=(heads,),
            in_specs=[
                pl.BlockSpec((rows, HD), lambda h, p: (0, 2 * h)),
                pl.BlockSpec((rows, HD), lambda h, p: (0, 2 * h + 1)),
                pl.BlockSpec((rows, HD), lambda h, p: (0, 2 * heads + h)),
                table,
                table,
            ],
            out_specs=[per_head] * 5,
        ),
        out_shape=[head_array] * 4 + [jax.ShapeDtypeStruct((rows, heads * HD), f32)],
        name="attention_forward",
    )(perm, pre, pre, pre, cos, sin)


def attention_backward(perm, block, q, k, v, log_total, grad, cos, sin):
    rows, heads = q.shape[0], q.shape[1] // HD
    per_head = pl.BlockSpec((rows, HD), lambda h, p: (0, h))
    table = pl.BlockSpec((rows, HD), lambda h, p: (0, 0))
    return pl.pallas_call(
        functools.partial(backward_kernel, block),
        grid_spec=pltpu.PrefetchScalarGridSpec(
            num_scalar_prefetch=1,
            grid=(heads,),
            in_specs=[per_head] * 5 + [table, table],
            out_specs=[pl.BlockSpec((rows, 2 * HD), lambda h, p: (0, h)), per_head],
            scratch_shapes=[pltpu.VMEM((rows, HD), f32), pltpu.VMEM((rows, HD), f32)],
        ),
        out_shape=[
            jax.ShapeDtypeStruct((rows, 2 * heads * HD), bf16),
            jax.ShapeDtypeStruct((rows, heads * HD), bf16),
        ],
        name="attention_backward",
    )(perm, q, k, v, log_total, grad, cos, sin)


def expert_kernel(kept, x_ref, g_ref, wg_ref, wu_ref, wd_ref, *refs):
    hidden_ref, gate_ref, up_ref = refs[kept:]
    count = x_ref.shape[0] // 2
    for p in range(2):
        rows = slice(p * count, (p + 1) * count)
        gate = dot(x_ref[rows, :], wg_ref[...], 1, 1)
        up = dot(x_ref[rows, :], wu_ref[...], 1, 1)
        grad = dot(g_ref[rows, :], wd_ref[...], 1, 1)
        sigmoid = jax.nn.sigmoid(gate)
        silu = gate * sigmoid
        hidden_ref[rows, :] = (silu * up).astype(bf16)
        gate_ref[rows, :] = (grad * up * sigmoid * (1.0 + gate * (1.0 - sigmoid))).astype(bf16)
        up_ref[rows, :] = (grad * silu).astype(bf16)


def expert_hidden(part, parts, slots, grads, weights, kept):
    rows, units = slots.shape[0], weights[0].shape[0]
    tile = 256 if units % 256 == 0 else 128
    whole = pl.BlockSpec((rows, D), lambda i: (0, 0))
    weight = pl.BlockSpec((tile, D), lambda i: (i, 0))
    result = pl.BlockSpec((rows, tile), lambda i: (part, i))
    return pl.pallas_call(
        functools.partial(expert_kernel, len(kept)),
        grid=(units // tile,),
        in_specs=[whole] * 2 + [weight] * 3 + [pl.BlockSpec(memory_space=pl.ANY)] * len(kept),
        out_specs=[result] * 3,
        out_shape=[jax.ShapeDtypeStruct((parts * rows, units), bf16)] * 3,
        input_output_aliases={5 + i: i for i in range(len(kept))},
        name="expert_hidden",
    )(slots, grads, *weights, *kept)


def rows_kernel(count, *refs):
    total = dot(refs[0][...], refs[count][...], 1, 0)
    for i in range(1, count):
        total = total + dot(refs[i][...], refs[count + i][...], 1, 0)
    refs[-1][...] = total.astype(bf16)


def expert_rows(part, rows, left, right):
    units, tile = right[0].shape[0], 256
    return pl.pallas_call(
        functools.partial(rows_kernel, len(left)),
        grid=(D // tile,),
        in_specs=[pl.BlockSpec((rows, units), lambda n: (part, 0))] * len(left)
        + [pl.BlockSpec((units, tile), lambda n: (0, n))] * len(right),
        out_specs=pl.BlockSpec((rows, tile), lambda n: (0, n)),
        out_shape=jax.ShapeDtypeStruct((rows, D), bf16),
        name="expert_rows",
    )(*left, *right)


def join_kernel(own_blocks, part_blocks, where, own_ref, *refs):
    parts, out_ref = refs[:-1], refs[-1]
    i = pl.program_id(0)
    inside = i - where[0] * own_blocks

    @pl.when((inside >= 0) & (inside < own_blocks))
    def _():
        out_ref[...] = own_ref[...]

    for s, part in enumerate(parts):
        place = i - where[1 + s]

        @pl.when((place >= 0) & (place < part_blocks))
        def _(part=part):
            out_ref[...] = part[...]


def join_weights(side, starts, own, parts):
    size, count = own.shape[0], parts[0].shape[0]
    tile = count // 2 if count % 32 == 0 else count
    own_blocks, part_blocks = size // tile, count // tile
    where = jnp.stack([side] + [start * part_blocks for start in starts]).astype(jnp.int32)

    def part_spec(s):
        return pl.BlockSpec(
            (tile, D), lambda i, w: (jnp.clip(i - w[1 + s], 0, part_blocks - 1), 0)
        )

    return pl.pallas_call(
        functools.partial(join_kernel, own_blocks, part_blocks),
        grid_spec=pltpu.PrefetchScalarGridSpec(
            num_scalar_prefetch=1,
            grid=(2 * own_blocks,),
            in_specs=[
                pl.BlockSpec(
                    (tile, D),
                    lambda i, w: (jnp.clip(i - w[0] * own_blocks, 0, own_blocks - 1), 0),
                )
            ]
            + [part_spec(s) for s in range(len(parts))],
            out_specs=pl.BlockSpec((tile, D), lambda i, w: (i, 0)),
        ),
        out_shape=jax.ShapeDtypeStruct((2 * size, D), own.dtype),
        name="join_weights",
    )(where, own, *parts)


def rope_tables(group_len):
    index = jnp.arange(group_len, dtype=jnp.int32)
    position = jnp.where(index < PROMPT, index, PROMPT + (index - PROMPT) % CONT).astype(f32)
    half = HD // 2
    frequency = jnp.exp(-math.log(10000.0) * jnp.arange(half, dtype=f32) / half)
    angles = position[:, None] * frequency[None, :]
    cosine, sine = jnp.cos(angles), jnp.sin(angles)
    return (
        jnp.concatenate([cosine, cosine], axis=1),
        jnp.concatenate([-sine, sine], axis=1),
    )


def after(*arrays):
    return lax.optimization_barrier(arrays)


def normalize_parts(values, gain):
    inverse = lax.rsqrt(jnp.mean(values * values, axis=-1, keepdims=True) + norm_eps)
    unit_rows = values * inverse
    return (unit_rows * gain, unit_rows, inverse)


def norm_backward(grad_outer, unit_rows, inverse, gain):
    grad_unit = grad_outer * gain
    grad_inner = inverse * (
        grad_unit - unit_rows * jnp.mean(grad_unit * unit_rows, axis=-1, keepdims=True)
    )
    return (grad_inner, jnp.sum(grad_outer * unit_rows, axis=0))


def shards(
    tokens,
    route_ids,
    gate_values,
    deal,
    norm1_gain,
    w_query,
    w_key,
    w_value,
    w_out,
    norm2_gain,
    w_gate,
    w_up,
    w_down,
    cotangent,
):
    rows = tokens.shape[1]
    ctx_count = lax.axis_size("ctx")
    fsdp_count = lax.axis_size("fsdp")
    group_len = rows * ctx_count
    capacity = 5 * rows * TOPK // (4 * EXPERTS)
    repeats = fsdp_count // EXPERTS
    pair = 2
    columns = repeats // pair
    core = lax.axis_index("ctx")
    expert = lax.axis_index("fsdp") // repeats
    width = D // ctx_count
    heads = HEADS // ctx_count

    def core_shift(a, s):
        return lax.ppermute(a, "ctx", [(i, (i + s) % ctx_count) for i in range(ctx_count)])

    def fsdp_shift(a, move):
        return lax.ppermute(a, "fsdp", [(i, move(i)) for i in range(fsdp_count)])

    def expert_shift(a, k):
        return fsdp_shift(a, lambda i: (i + k * repeats) % fsdp_count)

    def column_shift(a, j):
        def move(i):
            e, r = divmod(i, repeats)
            t, w = divmod(r, pair)
            return e * repeats + ((t + j) % columns) * pair + w

        return fsdp_shift(a, move)

    def pair_swap(a):
        return fsdp_shift(a, lambda i: i ^ 1)

    def core_gather(a):
        return jnp.concatenate([a] + [core_shift(a, s) for s in range(1, ctx_count)], axis=0)

    block_count = deal.shape[1]
    block = group_len // block_count
    local_blocks = block_count // ctx_count
    dealt = jnp.argsort(deal[0]).astype(jnp.int32)
    perm = ((core - dealt // local_blocks) % ctx_count) * local_blocks + dealt % local_blocks
    cos, sin = rope_tables(group_len)

    def own_columns(w):
        return lax.dynamic_slice_in_dim(w, core * width, width, axis=1)

    by_head = [own_columns(w).reshape(-1, heads, HD) for w in (w_query, w_key)]
    packed = jnp.concatenate(
        [jnp.stack(by_head, axis=2).reshape(-1, 2 * width), own_columns(w_value), own_columns(w_out)],
        axis=1,
    )
    packed = with_layout_constraint(packed, Layout(major_to_minor=(0, 1)))
    gathered = lax.all_gather(packed, "fsdp", axis=0, tiled=True)
    gathered = with_layout_constraint(gathered, Layout(major_to_minor=(0, 1)))

    halves = 2
    part_slots = capacity // halves
    half = EXPERTS * part_slots
    ids = route_ids[0]
    flat = ids.reshape(-1)
    onehot = (flat[:, None] == jnp.arange(EXPERTS, dtype=jnp.int32)[None, :]).astype(jnp.int32)
    earlier = jnp.cumsum(onehot, axis=0) - onehot
    slot = jnp.sum(earlier * onehot, axis=1)
    place = (slot // part_slots) * half + flat * part_slots + slot % part_slots
    place = jnp.where(slot < capacity, place, -1).reshape(rows, TOPK)
    targets = jnp.arange(halves * half, dtype=jnp.int32)
    select = [(place[:, k : k + 1] == targets[None, :]).astype(bf16) for k in range(TOPK)]
    spread = [(targets[:, None] == place[None, :, k]).astype(bf16) for k in range(TOPK)]
    gates = gate_values[0]

    dy = cotangent[0].astype(f32)
    grad_pairs = jnp.concatenate([(dy * gates[:, k : k + 1]).astype(bf16) for k in range(TOPK)])
    spread_both = jnp.concatenate(spread, axis=1)
    grad_blocks = [
        dot(spread_both[h * half : (h + 1) * half], grad_pairs, 1, 0, bf16) for h in range(halves)
    ]

    inputs = tokens[0].astype(f32)
    normed_f, _, _ = normalize_parts(inputs, norm1_gain)
    normed = core_gather(normed_f.astype(bf16))

    per = D // (ctx_count * fsdp_count)
    mine = lax.axis_index("fsdp")
    my_column, my_side = (mine % repeats) // pair, mine % pair

    def feature_order(relative):
        index = jnp.arange(D, dtype=jnp.int32)
        rest, j = index // per, index % per
        rest, c = rest // ctx_count, rest % ctx_count
        if relative:
            rest, e = rest // EXPERTS, rest % EXPERTS
            w, t = rest // columns, rest % columns
            t, w = (my_column + t) % columns, (my_side + w) % pair
            rest = e * repeats + t * pair + w
        source = c * (D // ctx_count) + rest * per + j
        shuffle = (jnp.arange(D, dtype=jnp.int32)[:, None] == source[None, :]).astype(bf16)
        return dot(normed, shuffle, 1, 0, bf16)

    normed_side, normed_mixed = feature_order(True), feature_order(False)

    def weight_part(w):
        count = w.shape[0] // ctx_count
        return lax.dynamic_slice_in_dim(w, core * count, count, axis=0)

    weight_parts = [weight_part(w) for w in (w_gate, w_up, w_down)]
    gathered, *tied = after(gathered, normed_side, normed_mixed, *grad_blocks, *weight_parts)
    normed_side, normed_mixed = tied[:2]
    grad_blocks, weight_parts = tied[2 : 2 + halves], tied[2 + halves :]
    full_qk, full_v = gathered[:, : 2 * width], gathered[:, 2 * width : 3 * width]
    out_columns = gathered[:, 3 * width :]
    full_qkv = gathered[:, : 3 * width]

    lines = [[r + e * repeats for e in range(EXPERTS)] for r in range(repeats)]

    def swap_experts(a, width=D):
        blocks = a.reshape(EXPERTS, -1, width)
        return lax.all_to_all(blocks, "fsdp", 0, 0, axis_index_groups=lines, tiled=True)

    def to_columns(a):
        return [a] + [column_shift(a, j) for j in range(1, columns)]

    grads_first = swap_experts(grad_blocks[0]).reshape(half, D)

    sides = [[i, i ^ 1] for i in range(0, fsdp_count, 2)]
    sides = [sorted(group) for group in sides]
    swapped = [
        lax.all_gather(part, "fsdp", axis=0, tiled=True, axis_index_groups=sides)
        for part in weight_parts
    ]

    starts = [(1 - my_side) * ctx_count + (core - s) % ctx_count for s in range(ctx_count)]

    def pair_weights(own, both):
        count = both.shape[0] // pair
        part = lax.dynamic_slice_in_dim(both, (1 - my_side) * count, count, axis=0)
        return join_weights(
            my_side, starts, own, [part] + [core_shift(part, s) for s in range(1, ctx_count)]
        )

    pre = dot(normed, full_qkv, 1, 0)
    context, q, k, v, log_total = attention_forward(perm, block, pre, cos, sin)

    def out_rows(c):
        return lax.dynamic_slice_in_dim(out_columns, (c % ctx_count) * width, width, axis=0)

    if ctx_count == 2:
        own_part, other = out_rows(core), core_shift(out_rows(core + 1), 1)
        w_o = jnp.concatenate(
            [jnp.where(core == 0, own_part, other), jnp.where(core == 0, other, own_part)], axis=1
        )
    else:
        w_o = lax.all_to_all(out_columns.reshape(ctx_count, width, width), "ctx", 0, 0)
        w_o = w_o.transpose(1, 0, 2).reshape(width, D)
    away = [dot(context[s * rows : (s + 1) * rows], w_o, 1, 0, bf16) for s in range(1, ctx_count)]
    attention = dot(context[:rows], w_o, 1, 0)
    for s in range(1, ctx_count):
        attention = attention + core_shift(away[s - 1], -s).astype(f32)
    hidden_in = inputs + attention
    normed_two_f, unit_two, inverse_two = normalize_parts(hidden_in, norm2_gain)
    normed_two = normed_two_f.astype(bf16)

    spread_any = spread[0] + spread[1]
    slot_blocks = [
        dot(spread_any[h * half : (h + 1) * half], normed_two, 1, 0, bf16) for h in range(halves)
    ]
    grads_first, waiting, _ = after(grads_first, grad_blocks[1], away[0])
    grads_second = swap_experts(waiting).reshape(half, D)
    grad_parts = to_columns(grads_first)
    got = after(grads_second, *slot_blocks, *swapped[:2], *grad_parts[1:])
    grads_second, slots_a, slots_b, *swapped_two = got[:5]
    grad_parts[1:] = got[5:]
    grad_parts += to_columns(grads_second)
    first = swap_experts(slots_a).reshape(half, D)
    wg, wu = (pair_weights(*w) for w in zip((w_gate, w_up), swapped_two))
    got = after(first, slots_b, swapped[2], wg, wu, *grad_parts[columns + 1 :])
    first, slots_b, swapped_down, wg, wu = got[:5]
    grad_parts[columns + 1 :] = got[5:]
    second = swap_experts(slots_b).reshape(half, D)
    wd = pair_weights(w_down, swapped_down)
    weights = (wg, wu, wd)
    parts = halves * columns

    def hidden_part(index, slots, state):
        return expert_hidden(index, parts, slots, grad_parts[index], weights, state)

    def grad_rows(index, state):
        return expert_rows(index, half, state[1:], (wg, wu))

    def columns_home(pieces):
        return [column_shift(part, -(j + 1)) for j, part in enumerate(pieces)]

    def add_parts(own, returned):
        total = own.astype(f32)
        for part in returned:
            total = total + part.astype(f32)
        return total.astype(bf16)

    slot_parts = to_columns(first)
    state, back, came = (), {}, []
    home_first = None
    for h in range(halves):
        for j in range(columns):
            index = h * columns + j
            state = hidden_part(index, slot_parts[index], state)
            if index == 0:
                second, *got = after(second, *state, *slot_parts[1:])
                state, slot_parts[1:] = got[:3], got[3:]
                slot_parts += to_columns(second)
            if h == 1 and j == 0:
                tied = after(*state, *came[0])
                home_first = add_parts(back[0], tied[3:])
                *state, home_first = after(*tied[:3], home_first)
                home_first = swap_experts(home_first)
        for j in [*range(1, columns), 0]:
            index = h * columns + j
            back[index] = grad_rows(index, state)
            tied = after(back[index], *state, *slot_parts[(1 + h) * columns + 1 :])
            back[index], state = tied[0], tied[1:4]
            slot_parts[(1 + h) * columns + 1 :] = tied[4:]
            if h == 1 and j == columns - 1:
                home_first, *state = after(home_first, *state)
        came.append(columns_home([back[h * columns + j] for j in range(1, columns)]))
    hidden, grad_gate, grad_up = state
    all_slots = jnp.concatenate(slot_parts, axis=0)
    all_grads = jnp.concatenate(grad_parts, axis=0)

    def core_sum(part):
        total = lax.dynamic_slice_in_dim(part, core * width, width, axis=1).astype(f32)
        for s in range(1, ctx_count):
            start = ((core + s) % ctx_count) * width
            total = total + core_shift(
                lax.dynamic_slice_in_dim(part, start, width, axis=1), s
            ).astype(f32)
        return total.astype(bf16)

    def side_sum(total):
        return lax.psum_scatter(
            total, "fsdp", scatter_dimension=0, tiled=True, axis_index_groups=sides
        ).astype(f32)

    def out_rows_of(h, j, left):
        return expert_rows(h * columns + j, half, (left,), (wd,))

    hidden_t = after(hidden, *(back[i] for i in range(parts)))[0]
    down_part = dot(hidden_t, all_grads, 0, 0, bf16)
    down_part, hidden_t, gate_t, *got = after(down_part, hidden_t, grad_gate, *came[1])
    home_second = swap_experts(add_parts(back[columns], got))
    gate_part = dot(gate_t, all_slots, 0, 0, bf16)
    down_total = core_sum(down_part)
    gate_part, hidden_t = after(gate_part, hidden_t)
    away_first = [out_rows_of(0, j, hidden_t) for j in range(1, columns)]
    own_first = out_rows_of(0, 0, hidden_t)
    home_second, down_total, hidden_t, own_first, *away_first = after(
        home_second, down_total, hidden_t, own_first, *away_first
    )
    down_grad = side_sum(down_total)
    away_first = columns_home(away_first)

    def side_swap_sum(total):
        def side_rows(i):
            size = total.shape[0] // pair
            return lax.dynamic_slice_in_dim(total, (i % pair) * size, size, axis=0)

        return side_rows(my_side), pair_swap(side_rows(my_side + 1))

    gate_total = core_sum(gate_part)
    grad_slot_in = jnp.concatenate([home_first, home_second], axis=0).reshape(halves * half, D)

    grad_normed_two = dot(select[0] + select[1], grad_slot_in, 1, 0)
    grad_norm_two, norm2_part = norm_backward(grad_normed_two, unit_two, inverse_two, norm2_gain)
    grad_hidden_in = dy + grad_norm_two
    grad_attention = core_gather(grad_hidden_in.astype(bf16))
    def reduce_blocks(blocks, shift):
        total = blocks[0].astype(f32)
        for d in range(1, len(blocks)):
            total = total + shift(blocks[d].astype(bf16), d).astype(f32)
        return total.astype(bf16)

    def cut(a, n):
        size = a.shape[0] // n
        return [a[i * size : (i + 1) * size] for i in range(n)]

    def side_shift(a, d):
        return pair_swap(a)

    def first_blocks(left, grad, n):
        size = D // n
        return [dot(left[:, i * size : (i + 1) * size], grad, 0, 0, bf16) for i in range(n)]

    def expert_sum(total):
        blocks = swap_experts(total, total.shape[1])
        return jnp.sum(blocks.reshape(EXPERTS, -1, total.shape[1]).astype(f32), axis=0)

    def row_blocks(a, n, own):
        split = a.reshape(EXPERTS, n, -1, a.shape[1])
        return [
            lax.dynamic_slice_in_dim(split, (own + d) % n, 1, axis=1).reshape(-1, a.shape[1])
            for d in range(n)
        ]

    out_part = dot(context, grad_attention, 0, 0, bf16)
    blocks_o = row_blocks(out_part, columns, my_column)
    got = after(grad_attention, gate_total, *blocks_o)
    grad_attention, gate_total, blocks_o = got[0], got[1], got[2:]
    gate_own, gate_came = side_swap_sum(gate_total)
    came_o = [column_shift(block, d) for d, block in enumerate(blocks_o) if d]
    grad_context = dot(grad_attention, w_o, 1, 1, bf16)
    grad_qk, grad_v = attention_backward(
        perm, block, q, k, v, log_total, grad_context, cos, sin
    )
    qk_part = dot(normed_mixed, grad_qk, 0, 0, bf16)
    qk_sum = lax.psum_scatter(qk_part, "fsdp", scatter_dimension=0, tiled=True)
    got = after(qk_part, grad_qk, grad_v, hidden_t, grad_up, down_grad, *away_first)
    grad_qk, grad_v, hidden_t, up_t, down_grad, *away_first = got[1:]
    outs_first = swap_experts(add_parts(own_first, away_first))
    blocks_v = first_blocks(normed_side, grad_v, pair)
    hidden_t, grad_qk, grad_v, *blocks_v = after(hidden_t, grad_qk, grad_v, *blocks_v)
    away_second = [out_rows_of(1, j, hidden_t) for j in range(1, columns)]
    hidden_t, grad_qk, grad_v, *away_second = after(hidden_t, grad_qk, grad_v, *away_second)
    away_second = columns_home(away_second)

    def back_rows(s, out):
        part = slice(s * rows, (s + 1) * rows)
        return (dot(grad_qk[part], full_qk, 1, 1) + dot(grad_v[part], full_v, 1, 1)).astype(out)

    back_away = [back_rows(s, bf16) for s in range(1, ctx_count)]
    grad_normed = back_rows(0, f32)
    grad_normed, gate_own, gate_came, *came_o = after(grad_normed, gate_own, gate_came, *came_o)
    gate_grad = gate_own.astype(f32) + gate_came.astype(f32)
    sum_o = add_parts(blocks_o[0], came_o)
    sum_o = reduce_blocks(row_blocks(sum_o, pair, my_side), side_shift)
    for s in range(1, ctx_count):
        grad_normed = grad_normed + core_shift(back_away[s - 1], -s).astype(f32)
    _, unit_one, inverse_one = normalize_parts(inputs, norm1_gain)
    grad_norm_one, norm1_part = norm_backward(grad_normed, unit_one, inverse_one, norm1_gain)
    tokens_grad = (grad_hidden_in + grad_norm_one).astype(bf16)
    up_t, norm1_part, tokens_grad, *away_second = after(
        up_t, norm1_part, tokens_grad, *away_second
    )

    up_part = dot(up_t, all_slots, 0, 0, bf16)
    came_v = [side_shift(block, d) for d, block in enumerate(blocks_v) if d]
    up_part, sum_o, outs_first, hidden_t, *came_v = after(
        up_part, sum_o, outs_first, hidden_t, *came_v
    )
    sum_v = reduce_blocks(cut(add_parts(blocks_v[0], came_v), columns), column_shift)
    out_grad = expert_sum(sum_o)
    up_total = core_sum(up_part)
    own_second = out_rows_of(1, 0, hidden_t)
    own_second, up_total, out_grad, sum_v, qk_sum = after(
        own_second, up_total, out_grad, sum_v, qk_sum
    )
    up_own, up_came = side_swap_sum(up_total)

    gains = jnp.stack([norm1_part, norm2_part]).reshape(2, ctx_count, fsdp_count, per)
    gains = lax.all_to_all(gains.transpose(2, 1, 0, 3), "fsdp", 0, 0, tiled=True)
    gains = jnp.sum(gains, axis=0)

    def gains_of(c):
        return lax.dynamic_index_in_dim(gains, c % ctx_count, 0, keepdims=False)

    gains_own = gains_of(core)
    for s in range(1, ctx_count):
        gains_own = gains_own + core_shift(gains_of(core + s), s)
    value_part = expert_sum(sum_v).reshape(ctx_count, per, width)
    outs_second = swap_experts(add_parts(own_second, away_second))
    up_grad = up_own.astype(f32) + up_came.astype(f32)
    qk_parts = qk_sum.astype(f32).reshape(ctx_count, per, heads, 2, HD)
    sums = jnp.stack(
        [
            qk_parts[:, :, :, 0].reshape(ctx_count, per, width),
            qk_parts[:, :, :, 1].reshape(ctx_count, per, width),
            value_part,
        ]
    )

    def core_piece(c):
        return lax.dynamic_index_in_dim(sums, c % ctx_count, 1, keepdims=False)

    if ctx_count == 2:
        own_part, other = core_piece(core), core_shift(core_piece(core + 1), 1)
        qkv_own = jnp.concatenate(
            [jnp.where(core == 0, own_part, other), jnp.where(core == 0, other, own_part)], axis=2
        )
    else:
        qkv_own = lax.all_to_all(sums.astype(bf16), "ctx", 1, 1).astype(f32)
        qkv_own = qkv_own.transpose(0, 2, 1, 3).reshape(3, per, D)
    query_grad, key_grad, value_grad = qkv_own[0], qkv_own[1], qkv_own[2]

    slot_out = jnp.concatenate([outs_first, outs_second], axis=0).reshape(halves * half, D)
    mixed = hidden_in
    for i in range(TOPK):
        mixed = mixed + dot(select[i], slot_out, 1, 0) * gates[:, i : i + 1]

    return (
        mixed.astype(bf16)[None],
        tokens_grad[None],
        gains_own[0],
        query_grad,
        key_grad,
        value_grad,
        out_grad,
        gains_own[1],
        gate_grad,
        up_grad,
        down_grad,
    )


def solution(mesh):
    in_specs = (
        P("fsdp", "ctx", None),
        P("fsdp", "ctx", None),
        P("fsdp", "ctx", None),
        P("fsdp", None),
        P(),
        P("fsdp", None),
        P("fsdp", None),
        P("fsdp", None),
        P("fsdp", None),
        P(),
        P("fsdp", None),
        P("fsdp", None),
        P("fsdp", None),
        P("fsdp", "ctx", None),
    )
    out_specs = (
        P("fsdp", "ctx", None),
        P("fsdp", "ctx", None),
        P(("ctx", "fsdp")),
        P(("ctx", "fsdp"), None),
        P(("ctx", "fsdp"), None),
        P(("ctx", "fsdp"), None),
        P(("ctx", "fsdp"), None),
        P(("ctx", "fsdp")),
        P("fsdp", "ctx"),
        P("fsdp", "ctx"),
        P("fsdp", "ctx"),
    )
    return jax.shard_map(shards, mesh=mesh, in_specs=in_specs, out_specs=out_specs, check_vma=False)
```

```python
import functools
import math

import jax
import jax.numpy as jnp
from jax import lax
from jax.experimental import pallas as pl
from jax.experimental.layout import Layout, with_layout_constraint
from jax.experimental.pallas import tpu as pltpu
from jax.sharding import PartitionSpec as P

D = 2048
HEADS = 16
HD = 128
EXPERTS = 4
TOPK = 2
PROMPT = 512
CONT = 256
TILE = 256

norm_eps = 1e-05
scale = 1.0 / math.sqrt(HD)
bf16 = jnp.bfloat16
f32 = jnp.float32


def dot(a, b, ca, cb, out=f32):
    r = lax.dot_general(a, b, (((ca,), (cb,)), ((), ())), preferred_element_type=f32)
    return r.astype(out)


def tile_keys(t):
    prompt_tiles = PROMPT // TILE
    if t < prompt_tiles:
        return list(range(t + 1))
    per = CONT // TILE
    first = prompt_tiles + ((t - prompt_tiles) // per) * per
    return list(range(prompt_tiles)) + list(range(first, t + 1))


def load_tile(ref, perm, t, block, cols):
    per = TILE // block
    parts = [
        ref[pl.ds(pl.multiple_of(perm[t * per + i] * block, block), block), cols]
        for i in range(per)
    ]
    return parts[0] if per == 1 else jnp.concatenate(parts, axis=0)


def store_tile(ref, perm, t, block, cols, value):
    per = TILE // block
    for i in range(per):
        ref[pl.ds(pl.multiple_of(perm[t * per + i] * block, block), block), cols] = value[
            i * block : (i + 1) * block
        ]


def spread_keys(ref, tiles):
    runs, start = [], tiles[0]
    for a, b in zip(tiles, tiles[1:] + [None]):
        if b != a + 1:
            runs.append((start, a + 1))
            start = b
    parts = [ref[lo * TILE : hi * TILE, :] for lo, hi in runs]
    return parts[0] if len(parts) == 1 else jnp.concatenate(parts, axis=0)


def causal_fill(scores, value):
    width = scores.shape[1] - TILE
    row = lax.broadcasted_iota(jnp.int32, (TILE, TILE), 0)
    col = lax.broadcasted_iota(jnp.int32, (TILE, TILE), 1)
    last = jnp.where(col <= row, scores[:, width:], value)
    return last if width == 0 else jnp.concatenate([scores[:, :width], last], axis=1)


def forward_kernel(
    block, perm, pre_q, pre_k, pre_v, cos_ref, sin_ref, ctx_ref, q_ref, k_ref, v_ref, log_ref
):
    tiles = pre_q.shape[0] // TILE
    for t in range(tiles):
        rows = slice(t * TILE, (t + 1) * TILE)
        cos, sin = cos_ref[rows, :], sin_ref[rows, :]
        q = load_tile(pre_q, perm, t, block, slice(None))
        q_ref[rows, :] = (q * cos + pltpu.roll(q, HD // 2, 1) * sin).astype(bf16)
        k = load_tile(pre_k, perm, t, block, slice(None))
        k_ref[rows, :] = (k * cos + pltpu.roll(k, HD // 2, 1) * sin).astype(bf16)
        v_ref[rows, :] = load_tile(pre_v, perm, t, block, slice(None)).astype(bf16)
    for t in range(tiles):
        rows = slice(t * TILE, (t + 1) * TILE)
        seen = tile_keys(t)
        keys, values = spread_keys(k_ref, seen), spread_keys(v_ref, seen)
        scores = dot(q_ref[rows, :], keys, 1, 1) * scale
        scores = causal_fill(scores, -1e30)
        top = jnp.max(scores, axis=1, keepdims=True)
        expo = jnp.exp(scores - top)
        total = jnp.sum(expo, axis=1, keepdims=True)
        probs = (expo * (1.0 / total)).astype(bf16)
        context = dot(probs, values, 1, 0).astype(bf16)
        store_tile(ctx_ref, perm, t, block, slice(None), context)
        log_ref[rows, :] = jnp.broadcast_to(top + jnp.log(total), (TILE, HD))


def backward_kernel(
    block,
    perm,
    q_ref,
    k_ref,
    v_ref,
    log_ref,
    do_ref,
    cos_ref,
    sin_ref,
    out_qk,
    out_v,
    dk_ref,
    dv_ref,
):
    tiles = q_ref.shape[0] // TILE
    dk_ref[...] = jnp.zeros_like(dk_ref)
    dv_ref[...] = jnp.zeros_like(dv_ref)
    for t in range(tiles):
        rows = slice(t * TILE, (t + 1) * TILE)
        seen = tile_keys(t)
        keys, values = spread_keys(k_ref, seen), spread_keys(v_ref, seen)
        query = q_ref[rows, :]
        grad = load_tile(do_ref, perm, t, block, slice(None))
        scores = dot(query, keys, 1, 1) * scale
        soft = causal_fill(jnp.exp(scores - log_ref[rows, 0:1]), 0.0)
        grad_prob = dot(grad, values, 1, 1)
        delta = jnp.sum(grad_prob * soft, axis=1, keepdims=True)
        grad_scores = (soft * (grad_prob - delta)).astype(bf16)
        values_back = dot(soft.astype(bf16), grad, 0, 0)
        keys_back = dot(grad_scores, query, 0, 0)
        for i, s in enumerate(seen):
            part, own = slice(i * TILE, (i + 1) * TILE), slice(s * TILE, (s + 1) * TILE)
            dv_ref[own, :] += values_back[part]
            dk_ref[own, :] += keys_back[part]
        back = dot(grad_scores, keys, 1, 0) * scale
        cos, sin = cos_ref[rows, :], sin_ref[rows, :]
        back = back * cos - pltpu.roll(back, HD // 2, 1) * sin
        store_tile(out_qk, perm, t, block, slice(0, HD), back.astype(bf16))
    for t in range(tiles):
        rows = slice(t * TILE, (t + 1) * TILE)
        cos, sin = cos_ref[rows, :], sin_ref[rows, :]
        back = dk_ref[rows, :] * scale
        back = back * cos - pltpu.roll(back, HD // 2, 1) * sin
        store_tile(out_qk, perm, t, block, slice(HD, 2 * HD), back.astype(bf16))
        store_tile(out_v, perm, t, block, slice(None), dv_ref[rows, :].astype(bf16))


def attention_forward(perm, block, pre, cos, sin):
    rows, heads = pre.shape[0], pre.shape[1] // (3 * HD)
    per_head = pl.BlockSpec((rows, HD), lambda h, p: (0, h))
    table = pl.BlockSpec((rows, HD), lambda h, p: (0, 0))
    head_array = jax.ShapeDtypeStruct((rows, heads * HD), bf16)
    return pl.pallas_call(
        functools.partial(forward_kernel, block),
        grid_spec=pltpu.PrefetchScalarGridSpec(
            num_scalar_prefetch=1,
            grid=(heads,),
            in_specs=[
                pl.BlockSpec((rows, HD), lambda h, p: (0, 2 * h)),
                pl.BlockSpec((rows, HD), lambda h, p: (0, 2 * h + 1)),
                pl.BlockSpec((rows, HD), lambda h, p: (0, 2 * heads + h)),
                table,
                table,
            ],
            out_specs=[per_head] * 5,
        ),
        out_shape=[head_array] * 4 + [jax.ShapeDtypeStruct((rows, heads * HD), f32)],
        name="attention_forward",
    )(perm, pre, pre, pre, cos, sin)


def attention_backward(perm, block, q, k, v, log_total, grad, cos, sin):
    rows, heads = q.shape[0], q.shape[1] // HD
    per_head = pl.BlockSpec((rows, HD), lambda h, p: (0, h))
    table = pl.BlockSpec((rows, HD), lambda h, p: (0, 0))
    return pl.pallas_call(
        functools.partial(backward_kernel, block),
        grid_spec=pltpu.PrefetchScalarGridSpec(
            num_scalar_prefetch=1,
            grid=(heads,),
            in_specs=[per_head] * 5 + [table, table],
            out_specs=[pl.BlockSpec((rows, 2 * HD), lambda h, p: (0, h)), per_head],
            scratch_shapes=[pltpu.VMEM((rows, HD), f32), pltpu.VMEM((rows, HD), f32)],
        ),
        out_shape=[
            jax.ShapeDtypeStruct((rows, 2 * heads * HD), bf16),
            jax.ShapeDtypeStruct((rows, heads * HD), bf16),
        ],
        name="attention_backward",
    )(perm, q, k, v, log_total, grad, cos, sin)


def expert_kernel(kept, x_ref, g_ref, wg_ref, wu_ref, wd_ref, *refs):
    hidden_ref, gate_ref, up_ref = refs[kept:]
    count = x_ref.shape[0] // 2
    for p in range(2):
        rows = slice(p * count, (p + 1) * count)
        gate = dot(x_ref[rows, :], wg_ref[...], 1, 1)
        up = dot(x_ref[rows, :], wu_ref[...], 1, 1)
        grad = dot(g_ref[rows, :], wd_ref[...], 1, 1)
        sigmoid = jax.nn.sigmoid(gate)
        silu = gate * sigmoid
        hidden_ref[rows, :] = (silu * up).astype(bf16)
        gate_ref[rows, :] = (grad * up * sigmoid * (1.0 + gate * (1.0 - sigmoid))).astype(bf16)
        up_ref[rows, :] = (grad * silu).astype(bf16)


def expert_hidden(part, parts, slots, grads, weights, kept):
    rows, units = slots.shape[0], weights[0].shape[0]
    tile = 256 if units % 256 == 0 else 128
    whole = pl.BlockSpec((rows, D), lambda i: (0, 0))
    weight = pl.BlockSpec((tile, D), lambda i: (i, 0))
    result = pl.BlockSpec((rows, tile), lambda i: (part, i))
    return pl.pallas_call(
        functools.partial(expert_kernel, len(kept)),
        grid=(units // tile,),
        in_specs=[whole] * 2 + [weight] * 3 + [pl.BlockSpec(memory_space=pl.ANY)] * len(kept),
        out_specs=[result] * 3,
        out_shape=[jax.ShapeDtypeStruct((parts * rows, units), bf16)] * 3,
        input_output_aliases={5 + i: i for i in range(len(kept))},
        name="expert_hidden",
    )(slots, grads, *weights, *kept)


def rows_kernel(count, *refs):
    total = dot(refs[0][...], refs[count][...], 1, 0)
    for i in range(1, count):
        total = total + dot(refs[i][...], refs[count + i][...], 1, 0)
    refs[-1][...] = total.astype(bf16)


def expert_rows(part, rows, left, right):
    units, tile = right[0].shape[0], 256
    return pl.pallas_call(
        functools.partial(rows_kernel, len(left)),
        grid=(D // tile,),
        in_specs=[pl.BlockSpec((rows, units), lambda n: (part, 0))] * len(left)
        + [pl.BlockSpec((units, tile), lambda n: (0, n))] * len(right),
        out_specs=pl.BlockSpec((rows, tile), lambda n: (0, n)),
        out_shape=jax.ShapeDtypeStruct((rows, D), bf16),
        name="expert_rows",
    )(*left, *right)


def join_kernel(own_blocks, part_blocks, where, own_ref, *refs):
    parts, out_ref = refs[:-1], refs[-1]
    i = pl.program_id(0)
    inside = i - where[0] * own_blocks

    @pl.when((inside >= 0) & (inside < own_blocks))
    def _():
        out_ref[...] = own_ref[...]

    for s, part in enumerate(parts):
        place = i - where[1 + s]

        @pl.when((place >= 0) & (place < part_blocks))
        def _(part=part):
            out_ref[...] = part[...]


def join_weights(side, starts, own, parts):
    size, count = own.shape[0], parts[0].shape[0]
    tile = count // 2 if count % 32 == 0 else count
    own_blocks, part_blocks = size // tile, count // tile
    where = jnp.stack([side] + [start * part_blocks for start in starts]).astype(jnp.int32)

    def part_spec(s):
        return pl.BlockSpec(
            (tile, D), lambda i, w: (jnp.clip(i - w[1 + s], 0, part_blocks - 1), 0)
        )

    return pl.pallas_call(
        functools.partial(join_kernel, own_blocks, part_blocks),
        grid_spec=pltpu.PrefetchScalarGridSpec(
            num_scalar_prefetch=1,
            grid=(2 * own_blocks,),
            in_specs=[
                pl.BlockSpec(
                    (tile, D),
                    lambda i, w: (jnp.clip(i - w[0] * own_blocks, 0, own_blocks - 1), 0),
                )
            ]
            + [part_spec(s) for s in range(len(parts))],
            out_specs=pl.BlockSpec((tile, D), lambda i, w: (i, 0)),
        ),
        out_shape=jax.ShapeDtypeStruct((2 * size, D), own.dtype),
        name="join_weights",
    )(where, own, *parts)


def rope_tables(group_len):
    index = jnp.arange(group_len, dtype=jnp.int32)
    position = jnp.where(index < PROMPT, index, PROMPT + (index - PROMPT) % CONT).astype(f32)
    half = HD // 2
    frequency = jnp.exp(-math.log(10000.0) * jnp.arange(half, dtype=f32) / half)
    angles = position[:, None] * frequency[None, :]
    cosine, sine = jnp.cos(angles), jnp.sin(angles)
    return (
        jnp.concatenate([cosine, cosine], axis=1),
        jnp.concatenate([-sine, sine], axis=1),
    )


def after(*arrays):
    return lax.optimization_barrier(arrays)


def normalize_parts(values, gain):
    inverse = lax.rsqrt(jnp.mean(values * values, axis=-1, keepdims=True) + norm_eps)
    unit_rows = values * inverse
    return (unit_rows * gain, unit_rows, inverse)


def norm_backward(grad_outer, unit_rows, inverse, gain):
    grad_unit = grad_outer * gain
    grad_inner = inverse * (
        grad_unit - unit_rows * jnp.mean(grad_unit * unit_rows, axis=-1, keepdims=True)
    )
    return (grad_inner, jnp.sum(grad_outer * unit_rows, axis=0))


def shards(
    tokens,
    route_ids,
    gate_values,
    deal,
    norm1_gain,
    w_query,
    w_key,
    w_value,
    w_out,
    norm2_gain,
    w_gate,
    w_up,
    w_down,
    cotangent,
):
    rows = tokens.shape[1]
    ctx_count = lax.axis_size("ctx")
    fsdp_count = lax.axis_size("fsdp")
    group_len = rows * ctx_count
    capacity = 5 * rows * TOPK // (4 * EXPERTS)
    repeats = fsdp_count // EXPERTS
    pair = 2
    columns = repeats // pair
    core = lax.axis_index("ctx")
    expert = lax.axis_index("fsdp") // repeats
    width = D // ctx_count
    heads = HEADS // ctx_count

    def core_shift(a, s):
        return lax.ppermute(a, "ctx", [(i, (i + s) % ctx_count) for i in range(ctx_count)])

    def fsdp_shift(a, move):
        return lax.ppermute(a, "fsdp", [(i, move(i)) for i in range(fsdp_count)])

    def expert_shift(a, k):
        return fsdp_shift(a, lambda i: (i + k * repeats) % fsdp_count)

    def column_shift(a, j):
        def move(i):
            e, r = divmod(i, repeats)
            t, w = divmod(r, pair)
            return e * repeats + ((t + j) % columns) * pair + w

        return fsdp_shift(a, move)

    def pair_swap(a):
        return fsdp_shift(a, lambda i: i ^ 1)

    def core_gather(a):
        return jnp.concatenate([a] + [core_shift(a, s) for s in range(1, ctx_count)], axis=0)

    block_count = deal.shape[1]
    block = group_len // block_count
    local_blocks = block_count // ctx_count
    dealt = jnp.argsort(deal[0]).astype(jnp.int32)
    perm = ((core - dealt // local_blocks) % ctx_count) * local_blocks + dealt % local_blocks
    cos, sin = rope_tables(group_len)

    def own_columns(w):
        return lax.dynamic_slice_in_dim(w, core * width, width, axis=1)

    by_head = [own_columns(w).reshape(-1, heads, HD) for w in (w_query, w_key)]
    packed = jnp.concatenate(
        [jnp.stack(by_head, axis=2).reshape(-1, 2 * width), own_columns(w_value), own_columns(w_out)],
        axis=1,
    )
    packed = with_layout_constraint(packed, Layout(major_to_minor=(0, 1)))
    gathered = lax.all_gather(packed, "fsdp", axis=0, tiled=True)
    gathered = with_layout_constraint(gathered, Layout(major_to_minor=(0, 1)))

    halves = 2
    part_slots = capacity // halves
    half = EXPERTS * part_slots
    ids = route_ids[0]
    flat = ids.reshape(-1)
    onehot = (flat[:, None] == jnp.arange(EXPERTS, dtype=jnp.int32)[None, :]).astype(jnp.int32)
    earlier = jnp.cumsum(onehot, axis=0) - onehot
    slot = jnp.sum(earlier * onehot, axis=1)
    place = (slot // part_slots) * half + flat * part_slots + slot % part_slots
    place = jnp.where(slot < capacity, place, -1).reshape(rows, TOPK)
    targets = jnp.arange(halves * half, dtype=jnp.int32)
    select = [(place[:, k : k + 1] == targets[None, :]).astype(bf16) for k in range(TOPK)]
    spread = [(targets[:, None] == place[None, :, k]).astype(bf16) for k in range(TOPK)]
    gates = gate_values[0]

    dy = cotangent[0].astype(f32)
    grad_pairs = jnp.concatenate([(dy * gates[:, k : k + 1]).astype(bf16) for k in range(TOPK)])
    spread_both = jnp.concatenate(spread, axis=1)
    grad_blocks = [
        dot(spread_both[h * half : (h + 1) * half], grad_pairs, 1, 0, bf16) for h in range(halves)
    ]

    inputs = tokens[0].astype(f32)
    normed_f, _, _ = normalize_parts(inputs, norm1_gain)
    normed = core_gather(normed_f.astype(bf16))

    per = D // (ctx_count * fsdp_count)
    mine = lax.axis_index("fsdp")
    my_column, my_side = (mine % repeats) // pair, mine % pair

    def feature_order(relative):
        index = jnp.arange(D, dtype=jnp.int32)
        rest, j = index // per, index % per
        rest, c = rest // ctx_count, rest % ctx_count
        if relative:
            rest, e = rest // EXPERTS, rest % EXPERTS
            w, t = rest // columns, rest % columns
            t, w = (my_column + t) % columns, (my_side + w) % pair
            rest = e * repeats + t * pair + w
        source = c * (D // ctx_count) + rest * per + j
        shuffle = (jnp.arange(D, dtype=jnp.int32)[:, None] == source[None, :]).astype(bf16)
        return dot(normed, shuffle, 1, 0, bf16)

    normed_side, normed_mixed = feature_order(True), feature_order(False)

    def weight_part(w):
        count = w.shape[0] // ctx_count
        return lax.dynamic_slice_in_dim(w, core * count, count, axis=0)

    weight_parts = [weight_part(w) for w in (w_gate, w_up, w_down)]
    gathered, *tied = after(gathered, normed_side, normed_mixed, *grad_blocks, *weight_parts)
    normed_side, normed_mixed = tied[:2]
    grad_blocks, weight_parts = tied[2 : 2 + halves], tied[2 + halves :]
    full_qk, full_v = gathered[:, : 2 * width], gathered[:, 2 * width : 3 * width]
    out_columns = gathered[:, 3 * width :]
    full_qkv = gathered[:, : 3 * width]

    lines = [[r + e * repeats for e in range(EXPERTS)] for r in range(repeats)]

    def swap_experts(a, width=D):
        blocks = a.reshape(EXPERTS, -1, width)
        return lax.all_to_all(blocks, "fsdp", 0, 0, axis_index_groups=lines, tiled=True)

    def to_columns(a):
        return [a] + [column_shift(a, j) for j in range(1, columns)]

    grads_first = swap_experts(grad_blocks[0]).reshape(half, D)

    sides = [[i, i ^ 1] for i in range(0, fsdp_count, 2)]
    sides = [sorted(group) for group in sides]
    swapped = [
        lax.all_gather(part, "fsdp", axis=0, tiled=True, axis_index_groups=sides)
        for part in weight_parts
    ]

    starts = [(1 - my_side) * ctx_count + (core - s) % ctx_count for s in range(ctx_count)]

    def pair_weights(own, both):
        count = both.shape[0] // pair
        part = lax.dynamic_slice_in_dim(both, (1 - my_side) * count, count, axis=0)
        return join_weights(
            my_side, starts, own, [part] + [core_shift(part, s) for s in range(1, ctx_count)]
        )

    pre = dot(normed, full_qkv, 1, 0)
    context, q, k, v, log_total = attention_forward(perm, block, pre, cos, sin)

    def out_rows(c):
        return lax.dynamic_slice_in_dim(out_columns, (c % ctx_count) * width, width, axis=0)

    if ctx_count == 2:
        own_part, other = out_rows(core), core_shift(out_rows(core + 1), 1)
        w_o = jnp.concatenate(
            [jnp.where(core == 0, own_part, other), jnp.where(core == 0, other, own_part)], axis=1
        )
    else:
        w_o = lax.all_to_all(out_columns.reshape(ctx_count, width, width), "ctx", 0, 0)
        w_o = w_o.transpose(1, 0, 2).reshape(width, D)
    away = [dot(context[s * rows : (s + 1) * rows], w_o, 1, 0, bf16) for s in range(1, ctx_count)]
    attention = dot(context[:rows], w_o, 1, 0)
    for s in range(1, ctx_count):
        attention = attention + core_shift(away[s - 1], -s).astype(f32)
    hidden_in = inputs + attention
    normed_two_f, unit_two, inverse_two = normalize_parts(hidden_in, norm2_gain)
    normed_two = normed_two_f.astype(bf16)

    spread_any = spread[0] + spread[1]
    slot_blocks = [
        dot(spread_any[h * half : (h + 1) * half], normed_two, 1, 0, bf16) for h in range(halves)
    ]
    grads_first, waiting, _ = after(grads_first, grad_blocks[1], away[0])
    grads_second = swap_experts(waiting).reshape(half, D)
    grad_parts = to_columns(grads_first)
    got = after(grads_second, *slot_blocks, *swapped[:2], *grad_parts[1:])
    grads_second, slots_a, slots_b, *swapped_two = got[:5]
    grad_parts[1:] = got[5:]
    grad_parts += to_columns(grads_second)
    first = swap_experts(slots_a).reshape(half, D)
    wg, wu = (pair_weights(*w) for w in zip((w_gate, w_up), swapped_two))
    got = after(first, slots_b, swapped[2], wg, wu, *grad_parts[columns + 1 :])
    first, slots_b, swapped_down, wg, wu = got[:5]
    grad_parts[columns + 1 :] = got[5:]
    second = swap_experts(slots_b).reshape(half, D)
    wd = pair_weights(w_down, swapped_down)
    weights = (wg, wu, wd)
    parts = halves * columns

    def hidden_part(index, slots, state):
        return expert_hidden(index, parts, slots, grad_parts[index], weights, state)

    def grad_rows(index, state):
        return expert_rows(index, half, state[1:], (wg, wu))

    def columns_home(pieces):
        return [column_shift(part, -(j + 1)) for j, part in enumerate(pieces)]

    def add_parts(own, returned):
        total = own.astype(f32)
        for part in returned:
            total = total + part.astype(f32)
        return total.astype(bf16)

    slot_parts = to_columns(first)
    back, came = {}, [None] * halves
    state = hidden_part(0, slot_parts[0], ())
    second, *got = after(second, *state, *slot_parts[1:])
    state, slot_parts[1:] = got[:3], got[3:]
    slot_parts += to_columns(second)
    for h in range(halves):
        for j in range(1, columns):
            index = h * columns + j
            state = hidden_part(index, slot_parts[index], state)
        for j in range(1, columns):
            index = h * columns + j
            back[index] = grad_rows(index, state)
            back[index], *state = after(back[index], *state)
        if h == 0:
            got = after(*state, *slot_parts[columns + 1 :])
            state, slot_parts[columns + 1 :] = got[:3], got[3:]
        came[h] = columns_home([back[h * columns + j] for j in range(1, columns)])
    back[0] = grad_rows(0, state)
    home_first, *got = after(back[0], *state, *came[0])
    state = got[:3]
    home_first = add_parts(home_first, got[3:])
    home_first, *state = after(home_first, *state)
    home_first = swap_experts(home_first)
    state = hidden_part(columns, slot_parts[columns], state)
    back[columns] = grad_rows(columns, state)
    back[columns], *state = after(back[columns], *state)
    hidden, grad_gate, grad_up = state
    all_slots = jnp.concatenate(slot_parts, axis=0)
    all_grads = jnp.concatenate(grad_parts, axis=0)

    def core_sum(part):
        total = lax.dynamic_slice_in_dim(part, core * width, width, axis=1).astype(f32)
        for s in range(1, ctx_count):
            start = ((core + s) % ctx_count) * width
            total = total + core_shift(
                lax.dynamic_slice_in_dim(part, start, width, axis=1), s
            ).astype(f32)
        return total.astype(bf16)

    def side_sum(total):
        return lax.psum_scatter(
            total, "fsdp", scatter_dimension=0, tiled=True, axis_index_groups=sides
        ).astype(f32)

    def out_rows_of(h, j, left):
        return expert_rows(h * columns + j, half, (left,), (wd,))

    home_second, hidden_t, *got = after(back[columns], hidden, *came[1])
    home_second = add_parts(home_second, got)
    home_second, hidden_t = after(home_second, hidden_t)
    home_second = swap_experts(home_second)
    down_part = dot(hidden_t, all_grads, 0, 0, bf16)
    down_part, hidden_t = after(down_part, hidden_t)
    away_first = [out_rows_of(0, j, hidden_t) for j in range(1, columns)]
    home_second, hidden_t, *away_first = after(home_second, hidden_t, *away_first)
    away_first = columns_home(away_first)
    down_total = core_sum(down_part)

    def side_swap_sum(total):
        def side_rows(i):
            size = total.shape[0] // pair
            return lax.dynamic_slice_in_dim(total, (i % pair) * size, size, axis=0)

        return side_rows(my_side), pair_swap(side_rows(my_side + 1))

    grad_slot_in = jnp.concatenate([home_first, home_second], axis=0).reshape(halves * half, D)

    grad_normed_two = dot(select[0] + select[1], grad_slot_in, 1, 0)
    grad_norm_two, norm2_part = norm_backward(grad_normed_two, unit_two, inverse_two, norm2_gain)
    grad_hidden_in = dy + grad_norm_two
    grad_attention = core_gather(grad_hidden_in.astype(bf16))
    def reduce_blocks(blocks, shift):
        total = blocks[0].astype(f32)
        for d in range(1, len(blocks)):
            total = total + shift(blocks[d].astype(bf16), d).astype(f32)
        return total.astype(bf16)

    def cut(a, n):
        size = a.shape[0] // n
        return [a[i * size : (i + 1) * size] for i in range(n)]

    def side_shift(a, d):
        return pair_swap(a)

    def first_blocks(left, grad, n):
        size = D // n
        return [dot(left[:, i * size : (i + 1) * size], grad, 0, 0, bf16) for i in range(n)]

    def expert_sum(total):
        blocks = swap_experts(total, total.shape[1])
        return jnp.sum(blocks.reshape(EXPERTS, -1, total.shape[1]).astype(f32), axis=0)

    def row_blocks(a, n, own):
        split = a.reshape(EXPERTS, n, -1, a.shape[1])
        return [
            lax.dynamic_slice_in_dim(split, (own + d) % n, 1, axis=1).reshape(-1, a.shape[1])
            for d in range(n)
        ]

    out_part = dot(context, grad_attention, 0, 0, bf16)
    blocks_o = row_blocks(out_part, columns, my_column)
    got = after(grad_attention, down_total, *blocks_o)
    grad_attention, down_total, blocks_o = got[0], got[1], got[2:]
    down_grad = side_sum(down_total)
    came_o = [column_shift(block, d) for d, block in enumerate(blocks_o) if d]
    grad_context = dot(grad_attention, w_o, 1, 1, bf16)
    grad_qk, grad_v = attention_backward(
        perm, block, q, k, v, log_total, grad_context, cos, sin
    )
    qk_part = dot(normed_mixed, grad_qk, 0, 0, bf16)
    qk_sum = lax.psum_scatter(qk_part, "fsdp", scatter_dimension=0, tiled=True)
    got = after(qk_part, grad_qk, grad_v, hidden_t, grad_gate, grad_up, *away_first)
    grad_qk, grad_v, hidden_t, gate_t, up_t, *away_first = got[1:]
    gate_part = dot(gate_t, all_slots, 0, 0, bf16)
    gate_part, grad_v, hidden_t = after(gate_part, grad_v, hidden_t)
    gate_total = core_sum(gate_part)
    outs_first = add_parts(out_rows_of(0, 0, hidden_t), away_first)
    away_second = [out_rows_of(1, j, hidden_t) for j in range(1, columns)]
    blocks_v = first_blocks(normed_side, grad_v, pair)
    got = after(outs_first, up_t, hidden_t, gate_total, *blocks_v, *away_second, *came_o)
    outs_first, up_t, hidden_t, gate_total = got[:4]
    blocks_v, came_o = got[4 : 4 + pair], got[3 + pair + columns :]
    away_second = columns_home(got[4 + pair : 3 + pair + columns])
    blocks_o = row_blocks(add_parts(blocks_o[0], came_o), pair, my_side)
    outs_first = swap_experts(outs_first)
    came_v = pair_swap(blocks_v[1])

    up_part = dot(up_t, all_slots, 0, 0, bf16)
    came_o = pair_swap(blocks_o[1])
    got = after(
        up_part, hidden_t, gate_total, outs_first, came_v, came_o, grad_qk, *away_second
    )
    up_part, hidden_t, gate_total, outs_first, came_v, came_o, grad_qk, *away_second = got
    gate_own, gate_came = side_swap_sum(gate_total)
    out_grad = expert_sum(add_parts(blocks_o[0], [came_o]))
    blocks_v = cut(add_parts(blocks_v[0], [came_v]), columns)
    came_v = [column_shift(block, d) for d, block in enumerate(blocks_v) if d]
    own_second = out_rows_of(1, 0, hidden_t)
    up_total = core_sum(up_part)
    outs_second, out_grad = after(add_parts(own_second, away_second), out_grad)
    outs_second = swap_experts(outs_second)
    got = after(up_total, grad_qk, gate_own, gate_came, outs_second, *came_v)
    up_total, grad_qk, gate_own, gate_came, outs_second, *came_v = got
    value_part = expert_sum(add_parts(blocks_v[0], came_v)).reshape(ctx_count, per, width)
    up_own, up_came = side_swap_sum(up_total)

    def back_rows(s, out):
        part = slice(s * rows, (s + 1) * rows)
        return (dot(grad_qk[part], full_qk, 1, 1) + dot(grad_v[part], full_v, 1, 1)).astype(out)

    back_away = [back_rows(s, bf16) for s in range(1, ctx_count)]
    grad_normed = back_rows(0, f32)
    grad_normed, qk_sum = after(grad_normed, qk_sum)
    gate_grad = gate_own.astype(f32) + gate_came.astype(f32)
    for s in range(1, ctx_count):
        grad_normed = grad_normed + core_shift(back_away[s - 1], -s).astype(f32)
    _, unit_one, inverse_one = normalize_parts(inputs, norm1_gain)
    grad_norm_one, norm1_part = norm_backward(grad_normed, unit_one, inverse_one, norm1_gain)
    tokens_grad = (grad_hidden_in + grad_norm_one).astype(bf16)
    up_own, up_came, value_part, norm1_part, tokens_grad = after(
        up_own, up_came, value_part, norm1_part, tokens_grad
    )

    gains = jnp.stack([norm1_part, norm2_part]).reshape(2, ctx_count, fsdp_count, per)
    gains = lax.all_to_all(gains.transpose(2, 1, 0, 3), "fsdp", 0, 0, tiled=True)
    gains = jnp.sum(gains, axis=0)

    def gains_of(c):
        return lax.dynamic_index_in_dim(gains, c % ctx_count, 0, keepdims=False)

    gains_own = gains_of(core)
    for s in range(1, ctx_count):
        gains_own = gains_own + core_shift(gains_of(core + s), s)
    up_grad = up_own.astype(f32) + up_came.astype(f32)
    qk_parts = qk_sum.astype(f32).reshape(ctx_count, per, heads, 2, HD)
    sums = jnp.stack(
        [
            qk_parts[:, :, :, 0].reshape(ctx_count, per, width),
            qk_parts[:, :, :, 1].reshape(ctx_count, per, width),
            value_part,
        ]
    )

    def core_piece(c):
        return lax.dynamic_index_in_dim(sums, c % ctx_count, 1, keepdims=False)

    if ctx_count == 2:
        own_part, other = core_piece(core), core_shift(core_piece(core + 1), 1)
        qkv_own = jnp.concatenate(
            [jnp.where(core == 0, own_part, other), jnp.where(core == 0, other, own_part)], axis=2
        )
    else:
        qkv_own = lax.all_to_all(sums.astype(bf16), "ctx", 1, 1).astype(f32)
        qkv_own = qkv_own.transpose(0, 2, 1, 3).reshape(3, per, D)
    query_grad, key_grad, value_grad = qkv_own[0], qkv_own[1], qkv_own[2]

    slot_out = jnp.concatenate([outs_first, outs_second], axis=0).reshape(halves * half, D)
    mixed = hidden_in
    for i in range(TOPK):
        mixed = mixed + dot(select[i], slot_out, 1, 0) * gates[:, i : i + 1]

    return (
        mixed.astype(bf16)[None],
        tokens_grad[None],
        gains_own[0],
        query_grad,
        key_grad,
        value_grad,
        out_grad,
        gains_own[1],
        gate_grad,
        up_grad,
        down_grad,
    )


def solution(mesh):
    in_specs = (
        P("fsdp", "ctx", None),
        P("fsdp", "ctx", None),
        P("fsdp", "ctx", None),
        P("fsdp", None),
        P(),
        P("fsdp", None),
        P("fsdp", None),
        P("fsdp", None),
        P("fsdp", None),
        P(),
        P("fsdp", None),
        P("fsdp", None),
        P("fsdp", None),
        P("fsdp", "ctx", None),
    )
    out_specs = (
        P("fsdp", "ctx", None),
        P("fsdp", "ctx", None),
        P(("ctx", "fsdp")),
        P(("ctx", "fsdp"), None),
        P(("ctx", "fsdp"), None),
        P(("ctx", "fsdp"), None),
        P(("ctx", "fsdp"), None),
        P(("ctx", "fsdp")),
        P("fsdp", "ctx"),
        P("fsdp", "ctx"),
        P("fsdp", "ctx"),
    )
    return jax.shard_map(shards, mesh=mesh, in_specs=in_specs, out_specs=out_specs, check_vma=False)
```

```python
import functools
import math

import jax
import jax.numpy as jnp
from jax import lax
from jax.experimental import pallas as pl
from jax.experimental.layout import Layout, with_layout_constraint
from jax.experimental.pallas import tpu as pltpu
from jax.sharding import PartitionSpec as P

D = 2048
HEADS = 16
HD = 128
EXPERTS = 4
TOPK = 2
PROMPT = 512
CONT = 256
TILE = 256

norm_eps = 1e-05
scale = 1.0 / math.sqrt(HD)
bf16 = jnp.bfloat16
f32 = jnp.float32


def dot(a, b, ca, cb, out=f32):
    r = lax.dot_general(a, b, (((ca,), (cb,)), ((), ())), preferred_element_type=f32)
    return r.astype(out)


def tile_keys(t):
    prompt_tiles = PROMPT // TILE
    if t < prompt_tiles:
        return list(range(t + 1))
    per = CONT // TILE
    first = prompt_tiles + ((t - prompt_tiles) // per) * per
    return list(range(prompt_tiles)) + list(range(first, t + 1))


def load_tile(ref, perm, t, block, cols):
    per = TILE // block
    parts = [
        ref[pl.ds(pl.multiple_of(perm[t * per + i] * block, block), block), cols]
        for i in range(per)
    ]
    return parts[0] if per == 1 else jnp.concatenate(parts, axis=0)


def store_tile(ref, perm, t, block, cols, value):
    per = TILE // block
    for i in range(per):
        ref[pl.ds(pl.multiple_of(perm[t * per + i] * block, block), block), cols] = value[
            i * block : (i + 1) * block
        ]


def spread_keys(ref, tiles):
    runs, start = [], tiles[0]
    for a, b in zip(tiles, tiles[1:] + [None]):
        if b != a + 1:
            runs.append((start, a + 1))
            start = b
    parts = [ref[lo * TILE : hi * TILE, :] for lo, hi in runs]
    return parts[0] if len(parts) == 1 else jnp.concatenate(parts, axis=0)


def causal_fill(scores, value):
    width = scores.shape[1] - TILE
    row = lax.broadcasted_iota(jnp.int32, (TILE, TILE), 0)
    col = lax.broadcasted_iota(jnp.int32, (TILE, TILE), 1)
    last = jnp.where(col <= row, scores[:, width:], value)
    return last if width == 0 else jnp.concatenate([scores[:, :width], last], axis=1)


def forward_kernel(
    block, perm, pre_q, pre_k, pre_v, cos_ref, sin_ref, ctx_ref, q_ref, k_ref, v_ref, log_ref
):
    tiles = pre_q.shape[0] // TILE
    for t in range(tiles):
        rows = slice(t * TILE, (t + 1) * TILE)
        cos, sin = cos_ref[rows, :], sin_ref[rows, :]
        q = load_tile(pre_q, perm, t, block, slice(None))
        q_ref[rows, :] = (q * cos + pltpu.roll(q, HD // 2, 1) * sin).astype(bf16)
        k = load_tile(pre_k, perm, t, block, slice(None))
        k_ref[rows, :] = (k * cos + pltpu.roll(k, HD // 2, 1) * sin).astype(bf16)
        v_ref[rows, :] = load_tile(pre_v, perm, t, block, slice(None)).astype(bf16)
    for t in range(tiles):
        rows = slice(t * TILE, (t + 1) * TILE)
        seen = tile_keys(t)
        keys, values = spread_keys(k_ref, seen), spread_keys(v_ref, seen)
        scores = dot(q_ref[rows, :], keys, 1, 1) * scale
        scores = causal_fill(scores, -1e30)
        top = jnp.max(scores, axis=1, keepdims=True)
        expo = jnp.exp(scores - top)
        total = jnp.sum(expo, axis=1, keepdims=True)
        probs = (expo * (1.0 / total)).astype(bf16)
        context = dot(probs, values, 1, 0).astype(bf16)
        store_tile(ctx_ref, perm, t, block, slice(None), context)
        log_ref[rows, :] = jnp.broadcast_to(top + jnp.log(total), (TILE, HD))


def backward_kernel(
    block,
    perm,
    q_ref,
    k_ref,
    v_ref,
    log_ref,
    do_ref,
    cos_ref,
    sin_ref,
    out_ref,
    dk_ref,
    dv_ref,
):
    tiles = q_ref.shape[0] // TILE
    dk_ref[...] = jnp.zeros_like(dk_ref)
    dv_ref[...] = jnp.zeros_like(dv_ref)
    for t in range(tiles):
        rows = slice(t * TILE, (t + 1) * TILE)
        seen = tile_keys(t)
        keys, values = spread_keys(k_ref, seen), spread_keys(v_ref, seen)
        query = q_ref[rows, :]
        grad = load_tile(do_ref, perm, t, block, slice(None))
        scores = dot(query, keys, 1, 1) * scale
        soft = causal_fill(jnp.exp(scores - log_ref[rows, 0:1]), 0.0)
        grad_prob = dot(grad, values, 1, 1)
        delta = jnp.sum(grad_prob * soft, axis=1, keepdims=True)
        grad_scores = (soft * (grad_prob - delta)).astype(bf16)
        values_back = dot(soft.astype(bf16), grad, 0, 0)
        keys_back = dot(grad_scores, query, 0, 0)
        for i, s in enumerate(seen):
            part, own = slice(i * TILE, (i + 1) * TILE), slice(s * TILE, (s + 1) * TILE)
            dv_ref[own, :] += values_back[part]
            dk_ref[own, :] += keys_back[part]
        back = dot(grad_scores, keys, 1, 0) * scale
        cos, sin = cos_ref[rows, :], sin_ref[rows, :]
        back = back * cos - pltpu.roll(back, HD // 2, 1) * sin
        store_tile(out_ref, perm, t, block, slice(0, HD), back.astype(bf16))
    for t in range(tiles):
        rows = slice(t * TILE, (t + 1) * TILE)
        cos, sin = cos_ref[rows, :], sin_ref[rows, :]
        back = dk_ref[rows, :] * scale
        back = back * cos - pltpu.roll(back, HD // 2, 1) * sin
        store_tile(out_ref, perm, t, block, slice(HD, 2 * HD), back.astype(bf16))
        store_tile(out_ref, perm, t, block, slice(2 * HD, 3 * HD), dv_ref[rows, :].astype(bf16))


def attention_forward(perm, block, pre, cos, sin):
    rows, heads = pre.shape[0], pre.shape[1] // (3 * HD)
    per_head = pl.BlockSpec((rows, HD), lambda h, p: (0, h))
    table = pl.BlockSpec((rows, HD), lambda h, p: (0, 0))
    head_array = jax.ShapeDtypeStruct((rows, heads * HD), bf16)
    return pl.pallas_call(
        functools.partial(forward_kernel, block),
        grid_spec=pltpu.PrefetchScalarGridSpec(
            num_scalar_prefetch=1,
            grid=(heads,),
            in_specs=[
                pl.BlockSpec((rows, HD), lambda h, p: (0, 3 * h)),
                pl.BlockSpec((rows, HD), lambda h, p: (0, 3 * h + 1)),
                pl.BlockSpec((rows, HD), lambda h, p: (0, 3 * h + 2)),
                table,
                table,
            ],
            out_specs=[per_head] * 5,
        ),
        out_shape=[head_array] * 4 + [jax.ShapeDtypeStruct((rows, heads * HD), f32)],
        name="attention_forward",
    )(perm, pre, pre, pre, cos, sin)


def attention_backward(perm, block, q, k, v, log_total, grad, cos, sin):
    rows, heads = q.shape[0], q.shape[1] // HD
    per_head = pl.BlockSpec((rows, HD), lambda h, p: (0, h))
    table = pl.BlockSpec((rows, HD), lambda h, p: (0, 0))
    return pl.pallas_call(
        functools.partial(backward_kernel, block),
        grid_spec=pltpu.PrefetchScalarGridSpec(
            num_scalar_prefetch=1,
            grid=(heads,),
            in_specs=[per_head] * 5 + [table, table],
            out_specs=pl.BlockSpec((rows, 3 * HD), lambda h, p: (0, h)),
            scratch_shapes=[pltpu.VMEM((rows, HD), f32), pltpu.VMEM((rows, HD), f32)],
        ),
        out_shape=jax.ShapeDtypeStruct((rows, 3 * heads * HD), bf16),
        name="attention_backward",
    )(perm, q, k, v, log_total, grad, cos, sin)


def expert_kernel(kept, x_ref, g_ref, wg_ref, wu_ref, wd_ref, *refs):
    hidden_ref, gate_ref, up_ref = refs[kept:]
    count = x_ref.shape[0] // 2
    for p in range(2):
        rows = slice(p * count, (p + 1) * count)
        gate = dot(x_ref[rows, :], wg_ref[...], 1, 1)
        up = dot(x_ref[rows, :], wu_ref[...], 1, 1)
        grad = dot(g_ref[rows, :], wd_ref[...], 1, 1)
        sigmoid = jax.nn.sigmoid(gate)
        silu = gate * sigmoid
        hidden_ref[rows, :] = (silu * up).astype(bf16)
        gate_ref[rows, :] = (grad * up * sigmoid * (1.0 + gate * (1.0 - sigmoid))).astype(bf16)
        up_ref[rows, :] = (grad * silu).astype(bf16)


def expert_hidden(part, parts, slots, grads, weights, kept):
    rows, units = slots.shape[0], weights[0].shape[0]
    tile = 256 if units % 256 == 0 else 128
    whole = pl.BlockSpec((rows, D), lambda i: (0, 0))
    weight = pl.BlockSpec((tile, D), lambda i: (i, 0))
    result = pl.BlockSpec((rows, tile), lambda i: (part, i))
    return pl.pallas_call(
        functools.partial(expert_kernel, len(kept)),
        grid=(units // tile,),
        in_specs=[whole] * 2 + [weight] * 3 + [pl.BlockSpec(memory_space=pl.ANY)] * len(kept),
        out_specs=[result] * 3,
        out_shape=[jax.ShapeDtypeStruct((parts * rows, units), bf16)] * 3,
        input_output_aliases={5 + i: i for i in range(len(kept))},
        name="expert_hidden",
    )(slots, grads, *weights, *kept)


def rows_kernel(count, *refs):
    total = dot(refs[0][...], refs[count][...], 1, 0)
    for i in range(1, count):
        total = total + dot(refs[i][...], refs[count + i][...], 1, 0)
    refs[-1][...] = total.astype(bf16)


def expert_rows(part, rows, left, right):
    units, tile = right[0].shape[0], 256
    return pl.pallas_call(
        functools.partial(rows_kernel, len(left)),
        grid=(D // tile,),
        in_specs=[pl.BlockSpec((rows, units), lambda n: (part, 0))] * len(left)
        + [pl.BlockSpec((units, tile), lambda n: (0, n))] * len(right),
        out_specs=pl.BlockSpec((rows, tile), lambda n: (0, n)),
        out_shape=jax.ShapeDtypeStruct((rows, D), bf16),
        name="expert_rows",
    )(*left, *right)


def join_kernel(own_blocks, part_blocks, where, own_ref, *refs):
    parts, out_ref = refs[:-1], refs[-1]
    i = pl.program_id(0)
    inside = i - where[0] * own_blocks

    @pl.when((inside >= 0) & (inside < own_blocks))
    def _():
        out_ref[...] = own_ref[...]

    for s, part in enumerate(parts):
        place = i - where[1 + s]

        @pl.when((place >= 0) & (place < part_blocks))
        def _(part=part):
            out_ref[...] = part[...]


def join_weights(side, starts, own, parts):
    size, count = own.shape[0], parts[0].shape[0]
    tile = count // 2 if count % 32 == 0 else count
    own_blocks, part_blocks = size // tile, count // tile
    where = jnp.stack([side] + [start * part_blocks for start in starts]).astype(jnp.int32)

    def part_spec(s):
        return pl.BlockSpec(
            (tile, D), lambda i, w: (jnp.clip(i - w[1 + s], 0, part_blocks - 1), 0)
        )

    return pl.pallas_call(
        functools.partial(join_kernel, own_blocks, part_blocks),
        grid_spec=pltpu.PrefetchScalarGridSpec(
            num_scalar_prefetch=1,
            grid=(2 * own_blocks,),
            in_specs=[
                pl.BlockSpec(
                    (tile, D),
                    lambda i, w: (jnp.clip(i - w[0] * own_blocks, 0, own_blocks - 1), 0),
                )
            ]
            + [part_spec(s) for s in range(len(parts))],
            out_specs=pl.BlockSpec((tile, D), lambda i, w: (i, 0)),
        ),
        out_shape=jax.ShapeDtypeStruct((2 * size, D), own.dtype),
        name="join_weights",
    )(where, own, *parts)


def rope_tables(group_len):
    index = jnp.arange(group_len, dtype=jnp.int32)
    position = jnp.where(index < PROMPT, index, PROMPT + (index - PROMPT) % CONT).astype(f32)
    half = HD // 2
    frequency = jnp.exp(-math.log(10000.0) * jnp.arange(half, dtype=f32) / half)
    angles = position[:, None] * frequency[None, :]
    cosine, sine = jnp.cos(angles), jnp.sin(angles)
    return (
        jnp.concatenate([cosine, cosine], axis=1),
        jnp.concatenate([-sine, sine], axis=1),
    )


def after(*arrays):
    return lax.optimization_barrier(arrays)


def normalize_parts(values, gain):
    inverse = lax.rsqrt(jnp.mean(values * values, axis=-1, keepdims=True) + norm_eps)
    unit_rows = values * inverse
    return (unit_rows * gain, unit_rows, inverse)


def norm_backward(grad_outer, unit_rows, inverse, gain):
    grad_unit = grad_outer * gain
    grad_inner = inverse * (
        grad_unit - unit_rows * jnp.mean(grad_unit * unit_rows, axis=-1, keepdims=True)
    )
    return (grad_inner, jnp.sum(grad_outer * unit_rows, axis=0))


def shards(
    tokens,
    route_ids,
    gate_values,
    deal,
    norm1_gain,
    w_query,
    w_key,
    w_value,
    w_out,
    norm2_gain,
    w_gate,
    w_up,
    w_down,
    cotangent,
):
    rows = tokens.shape[1]
    ctx_count = lax.axis_size("ctx")
    fsdp_count = lax.axis_size("fsdp")
    group_len = rows * ctx_count
    capacity = 5 * rows * TOPK // (4 * EXPERTS)
    repeats = fsdp_count // EXPERTS
    pair = 2
    columns = repeats // pair
    core = lax.axis_index("ctx")
    expert = lax.axis_index("fsdp") // repeats
    width = D // ctx_count
    heads = HEADS // ctx_count

    def core_shift(a, s):
        return lax.ppermute(a, "ctx", [(i, (i + s) % ctx_count) for i in range(ctx_count)])

    def fsdp_shift(a, move):
        return lax.ppermute(a, "fsdp", [(i, move(i)) for i in range(fsdp_count)])

    def expert_shift(a, k):
        return fsdp_shift(a, lambda i: (i + k * repeats) % fsdp_count)

    def column_shift(a, j):
        def move(i):
            e, r = divmod(i, repeats)
            t, w = divmod(r, pair)
            return e * repeats + ((t + j) % columns) * pair + w

        return fsdp_shift(a, move)

    def pair_swap(a):
        return fsdp_shift(a, lambda i: i ^ 1)

    def core_gather(a):
        return jnp.concatenate([a] + [core_shift(a, s) for s in range(1, ctx_count)], axis=0)

    block_count = deal.shape[1]
    block = group_len // block_count
    local_blocks = block_count // ctx_count
    dealt = jnp.argsort(deal[0]).astype(jnp.int32)
    perm = ((core - dealt // local_blocks) % ctx_count) * local_blocks + dealt % local_blocks
    cos, sin = rope_tables(group_len)

    def own_columns(w):
        return lax.dynamic_slice_in_dim(w, core * width, width, axis=1)

    by_head = [own_columns(w).reshape(-1, heads, HD) for w in (w_query, w_key, w_value)]
    packed = jnp.concatenate(
        [jnp.stack(by_head, axis=2).reshape(-1, 3 * width), own_columns(w_out)], axis=1
    )
    packed = with_layout_constraint(packed, Layout(major_to_minor=(0, 1)))
    gathered = lax.all_gather(packed, "fsdp", axis=0, tiled=True)
    gathered = with_layout_constraint(gathered, Layout(major_to_minor=(0, 1)))

    halves = 2
    part_slots = capacity // halves
    half = EXPERTS * part_slots
    ids = route_ids[0]
    flat = ids.reshape(-1)
    onehot = (flat[:, None] == jnp.arange(EXPERTS, dtype=jnp.int32)[None, :]).astype(jnp.int32)
    earlier = jnp.cumsum(onehot, axis=0) - onehot
    slot = jnp.sum(earlier * onehot, axis=1)
    place = (slot // part_slots) * half + flat * part_slots + slot % part_slots
    place = jnp.where(slot < capacity, place, -1).reshape(rows, TOPK)
    targets = jnp.arange(halves * half, dtype=jnp.int32)
    select = [(place[:, k : k + 1] == targets[None, :]).astype(bf16) for k in range(TOPK)]
    spread = [(targets[:, None] == place[None, :, k]).astype(bf16) for k in range(TOPK)]
    gates = gate_values[0]

    dy = cotangent[0].astype(f32)
    grad_pairs = jnp.concatenate([(dy * gates[:, k : k + 1]).astype(bf16) for k in range(TOPK)])
    spread_both = jnp.concatenate(spread, axis=1)
    grad_blocks = [
        dot(spread_both[h * half : (h + 1) * half], grad_pairs, 1, 0, bf16) for h in range(halves)
    ]

    inputs = tokens[0].astype(f32)
    normed_f, _, _ = normalize_parts(inputs, norm1_gain)
    normed = core_gather(normed_f.astype(bf16))

    per = D // (ctx_count * fsdp_count)
    mine = lax.axis_index("fsdp")
    my_column, my_side = (mine % repeats) // pair, mine % pair

    index = jnp.arange(D, dtype=jnp.int32)
    source = (index // per % ctx_count) * (D // ctx_count)
    source = source + index // (per * ctx_count) * per + index % per
    shuffle = (index[:, None] == source[None, :]).astype(bf16)
    normed_mixed = dot(normed, shuffle, 1, 0, bf16)

    def weight_part(w):
        count = w.shape[0] // ctx_count
        return lax.dynamic_slice_in_dim(w, core * count, count, axis=0)

    weight_parts = [weight_part(w) for w in (w_gate, w_up, w_down)]
    gathered, normed_mixed, *tied = after(gathered, normed_mixed, *grad_blocks, *weight_parts)
    grad_blocks, weight_parts = tied[:halves], tied[halves:]
    out_columns = gathered[:, 3 * width :]
    full_qkv = gathered[:, : 3 * width]

    lines = [[r + e * repeats for e in range(EXPERTS)] for r in range(repeats)]

    def swap_experts(a, width=D):
        blocks = a.reshape(EXPERTS, -1, width)
        return lax.all_to_all(blocks, "fsdp", 0, 0, axis_index_groups=lines, tiled=True)

    def to_columns(a):
        return [a] + [column_shift(a, j) for j in range(1, columns)]

    grads_first = swap_experts(grad_blocks[0]).reshape(half, D)

    sides = [[i, i ^ 1] for i in range(0, fsdp_count, 2)]
    sides = [sorted(group) for group in sides]
    swapped = [
        lax.all_gather(part, "fsdp", axis=0, tiled=True, axis_index_groups=sides)
        for part in weight_parts
    ]

    starts = [(1 - my_side) * ctx_count + (core - s) % ctx_count for s in range(ctx_count)]

    def pair_weights(own, both):
        count = both.shape[0] // pair
        part = lax.dynamic_slice_in_dim(both, (1 - my_side) * count, count, axis=0)
        return join_weights(
            my_side, starts, own, [part] + [core_shift(part, s) for s in range(1, ctx_count)]
        )

    pre = dot(normed, full_qkv, 1, 0)
    context, q, k, v, log_total = attention_forward(perm, block, pre, cos, sin)

    def out_rows(c):
        return lax.dynamic_slice_in_dim(out_columns, (c % ctx_count) * width, width, axis=0)

    if ctx_count == 2:
        own_part, other = out_rows(core), core_shift(out_rows(core + 1), 1)
        w_o = jnp.concatenate(
            [jnp.where(core == 0, own_part, other), jnp.where(core == 0, other, own_part)], axis=1
        )
    else:
        w_o = lax.all_to_all(out_columns.reshape(ctx_count, width, width), "ctx", 0, 0)
        w_o = w_o.transpose(1, 0, 2).reshape(width, D)
    away = [dot(context[s * rows : (s + 1) * rows], w_o, 1, 0, bf16) for s in range(1, ctx_count)]
    attention = dot(context[:rows], w_o, 1, 0)
    for s in range(1, ctx_count):
        attention = attention + core_shift(away[s - 1], -s).astype(f32)
    hidden_in = inputs + attention
    normed_two_f, unit_two, inverse_two = normalize_parts(hidden_in, norm2_gain)
    normed_two = normed_two_f.astype(bf16)

    spread_any = spread[0] + spread[1]
    slot_blocks = [
        dot(spread_any[h * half : (h + 1) * half], normed_two, 1, 0, bf16) for h in range(halves)
    ]
    grads_first, waiting, _ = after(grads_first, grad_blocks[1], away[0])
    grads_second = swap_experts(waiting).reshape(half, D)
    grad_parts = to_columns(grads_first)
    got = after(grads_second, *slot_blocks, *swapped[:2], *grad_parts[1:])
    grads_second, slots_a, slots_b, *swapped_two = got[:5]
    grad_parts[1:] = got[5:]
    grad_parts += to_columns(grads_second)
    first = swap_experts(slots_a).reshape(half, D)
    wg, wu = (pair_weights(*w) for w in zip((w_gate, w_up), swapped_two))
    got = after(first, slots_b, swapped[2], wg, wu, *grad_parts[columns + 1 :])
    first, slots_b, swapped_down, wg, wu = got[:5]
    grad_parts[columns + 1 :] = got[5:]
    second = swap_experts(slots_b).reshape(half, D)
    wd = pair_weights(w_down, swapped_down)
    weights = (wg, wu, wd)
    parts = halves * columns

    def hidden_part(index, slots, state):
        return expert_hidden(index, parts, slots, grad_parts[index], weights, state)

    def grad_rows(index, state):
        return expert_rows(index, half, state[1:], (wg, wu))

    def columns_home(pieces):
        return [column_shift(part, -(j + 1)) for j, part in enumerate(pieces)]

    def add_parts(own, returned):
        total = own.astype(f32)
        for part in returned:
            total = total + part.astype(f32)
        return total.astype(bf16)

    slot_parts = to_columns(first)
    back, came = {}, [None] * halves
    state = hidden_part(0, slot_parts[0], ())
    second, *got = after(second, *state, *slot_parts[1:])
    state, slot_parts[1:] = got[:3], got[3:]
    slot_parts += to_columns(second)
    for h in range(halves):
        for j in range(1, columns):
            index = h * columns + j
            state = hidden_part(index, slot_parts[index], state)
        for j in range(1, columns):
            index = h * columns + j
            back[index] = grad_rows(index, state)
            back[index], *state = after(back[index], *state)
        if h == 0:
            got = after(*state, *slot_parts[columns + 1 :])
            state, slot_parts[columns + 1 :] = got[:3], got[3:]
        came[h] = columns_home([back[h * columns + j] for j in range(1, columns)])
    back[0] = grad_rows(0, state)
    home_first, *got = after(back[0], *state, *came[0])
    state = got[:3]
    home_first = add_parts(home_first, got[3:])
    home_first, *state = after(home_first, *state)
    home_first = swap_experts(home_first)
    state = hidden_part(columns, slot_parts[columns], state)
    back[columns] = grad_rows(columns, state)
    back[columns], home_first, *state = after(back[columns], home_first, *state)
    hidden, grad_gate, grad_up = state
    all_slots = jnp.concatenate(slot_parts, axis=0)
    all_grads = jnp.concatenate(grad_parts, axis=0)

    def core_sum(part):
        total = lax.dynamic_slice_in_dim(part, core * width, width, axis=1).astype(f32)
        for s in range(1, ctx_count):
            start = ((core + s) % ctx_count) * width
            total = total + core_shift(
                lax.dynamic_slice_in_dim(part, start, width, axis=1), s
            ).astype(f32)
        return total.astype(bf16)

    def side_sum(total):
        return lax.psum_scatter(
            total, "fsdp", scatter_dimension=0, tiled=True, axis_index_groups=sides
        ).astype(f32)

    def out_rows_of(h, j, left):
        return expert_rows(h * columns + j, half, (left,), (wd,))

    home_second, hidden_t, *got = after(back[columns], hidden, *came[1])
    home_second = add_parts(home_second, got)
    home_second, hidden_t = after(home_second, hidden_t)
    home_second = swap_experts(home_second)
    down_part = dot(hidden_t, all_grads, 0, 0, bf16)
    down_part, hidden_t = after(down_part, hidden_t)
    away_first = [out_rows_of(0, j, hidden_t) for j in range(1, columns)]
    home_second, hidden_t, *away_first = after(home_second, hidden_t, *away_first)
    away_first = columns_home(away_first)
    down_total = core_sum(down_part)

    def side_swap_sum(total):
        def side_rows(i):
            size = total.shape[0] // pair
            return lax.dynamic_slice_in_dim(total, (i % pair) * size, size, axis=0)

        return side_rows(my_side), pair_swap(side_rows(my_side + 1))

    grad_slot_in = jnp.concatenate([home_first, home_second], axis=0).reshape(halves * half, D)

    grad_normed_two = dot(select[0] + select[1], grad_slot_in, 1, 0)
    grad_norm_two, norm2_part = norm_backward(grad_normed_two, unit_two, inverse_two, norm2_gain)
    grad_hidden_in = dy + grad_norm_two
    grad_attention = core_gather(grad_hidden_in.astype(bf16))
    def reduce_blocks(blocks, shift):
        total = blocks[0].astype(f32)
        for d in range(1, len(blocks)):
            total = total + shift(blocks[d].astype(bf16), d).astype(f32)
        return total.astype(bf16)

    def cut(a, n):
        size = a.shape[0] // n
        return [a[i * size : (i + 1) * size] for i in range(n)]

    def expert_sum(total):
        blocks = swap_experts(total, total.shape[1])
        return jnp.sum(blocks.reshape(EXPERTS, -1, total.shape[1]).astype(f32), axis=0)

    def row_blocks(a, n, own):
        split = a.reshape(EXPERTS, n, -1, a.shape[1])
        return [
            lax.dynamic_slice_in_dim(split, (own + d) % n, 1, axis=1).reshape(-1, a.shape[1])
            for d in range(n)
        ]

    out_part = dot(context, grad_attention, 0, 0, bf16)
    blocks_o = row_blocks(out_part, columns, my_column)
    got = after(grad_attention, down_total, *blocks_o)
    grad_attention, down_total, blocks_o = got[0], got[1], got[2:]
    down_grad = side_sum(down_total)
    came_o = [column_shift(block, d) for d, block in enumerate(blocks_o) if d]
    grad_context = dot(grad_attention, w_o, 1, 1, bf16)
    grad_qkv = attention_backward(
        perm, block, q, k, v, log_total, grad_context, cos, sin
    )
    qkv_part = dot(normed_mixed, grad_qkv, 0, 0, bf16)
    qkv_sum = lax.psum_scatter(qkv_part, "fsdp", scatter_dimension=0, tiled=True)

    got = after(qkv_part, grad_qkv, hidden_t, grad_gate, grad_up, *away_first)
    grad_qkv, hidden_t, gate_t, up_t, *away_first = got[1:]
    gate_part = dot(gate_t, all_slots, 0, 0, bf16)
    gate_part, hidden_t = after(gate_part, hidden_t)
    outs_first = add_parts(out_rows_of(0, 0, hidden_t), away_first)
    away_second = [out_rows_of(1, j, hidden_t) for j in range(1, columns)]
    gate_total = core_sum(gate_part)
    got = after(outs_first, gate_total, up_t, *away_second, *came_o)
    outs_first, gate_total, up_t = got[:3]
    away_second, came_o = columns_home(got[3 : 2 + columns]), got[2 + columns :]
    outs_first = swap_experts(outs_first)
    gate_own, gate_came = side_swap_sum(gate_total)
    blocks_o = row_blocks(add_parts(blocks_o[0], came_o), pair, my_side)
    up_t, *blocks_o = after(up_t, *blocks_o)
    came_o = pair_swap(blocks_o[1])

    up_part = dot(up_t, all_slots, 0, 0, bf16)
    got = after(up_part, hidden_t, grad_qkv, outs_first, came_o, gate_came, *away_second)
    up_part, hidden_t, grad_qkv, outs_first, came_o, gate_came, *away_second = got
    gate_grad = gate_own.astype(f32) + gate_came.astype(f32)
    outs_second = add_parts(out_rows_of(1, 0, hidden_t), away_second)
    up_total = core_sum(up_part)
    outs_second, up_total, grad_qkv = after(outs_second, up_total, grad_qkv)
    outs_second = swap_experts(outs_second)
    up_own, up_came = side_swap_sum(up_total)

    def back_rows(s, out):
        return dot(grad_qkv[s * rows : (s + 1) * rows], full_qkv, 1, 1, out)

    back_away = [back_rows(s, bf16) for s in range(1, ctx_count)]
    grad_normed = back_rows(0, f32)
    for s in range(1, ctx_count):
        grad_normed = grad_normed + core_shift(back_away[s - 1], -s).astype(f32)
    _, unit_one, inverse_one = normalize_parts(inputs, norm1_gain)
    grad_norm_one, norm1_part = norm_backward(grad_normed, unit_one, inverse_one, norm1_gain)
    tokens_grad = (grad_hidden_in + grad_norm_one).astype(bf16)
    tokens_grad, norm1_part, outs_second, up_own, up_came, qkv_sum = after(
        tokens_grad, norm1_part, outs_second, up_own, up_came, qkv_sum
    )
    out_grad = expert_sum(add_parts(blocks_o[0], [came_o]))

    gains = jnp.stack([norm1_part, norm2_part]).reshape(2, ctx_count, fsdp_count, per)
    gains = lax.all_to_all(gains.transpose(2, 1, 0, 3), "fsdp", 0, 0, tiled=True)
    gains = jnp.sum(gains, axis=0)

    def gains_of(c):
        return lax.dynamic_index_in_dim(gains, c % ctx_count, 0, keepdims=False)

    gains_own = gains_of(core)
    for s in range(1, ctx_count):
        gains_own = gains_own + core_shift(gains_of(core + s), s)
    up_grad = up_own.astype(f32) + up_came.astype(f32)
    sums = qkv_sum.reshape(ctx_count, per, heads, 3, HD).astype(f32)
    sums = sums.transpose(3, 0, 1, 2, 4).reshape(3, ctx_count, per, width)

    def core_piece(c):
        return lax.dynamic_index_in_dim(sums, c % ctx_count, 1, keepdims=False)

    if ctx_count == 2:
        own_part, other = core_piece(core), core_shift(core_piece(core + 1), 1)
        qkv_own = jnp.concatenate(
            [jnp.where(core == 0, own_part, other), jnp.where(core == 0, other, own_part)], axis=2
        )
    else:
        qkv_own = lax.all_to_all(sums.astype(bf16), "ctx", 1, 1).astype(f32)
        qkv_own = qkv_own.transpose(0, 2, 1, 3).reshape(3, per, D)
    query_grad, key_grad, value_grad = qkv_own[0], qkv_own[1], qkv_own[2]

    slot_out = jnp.concatenate([outs_first, outs_second], axis=0).reshape(halves * half, D)
    mixed = hidden_in
    for i in range(TOPK):
        mixed = mixed + dot(select[i], slot_out, 1, 0) * gates[:, i : i + 1]

    return (
        mixed.astype(bf16)[None],
        tokens_grad[None],
        gains_own[0],
        query_grad,
        key_grad,
        value_grad,
        out_grad,
        gains_own[1],
        gate_grad,
        up_grad,
        down_grad,
    )


def solution(mesh):
    in_specs = (
        P("fsdp", "ctx", None),
        P("fsdp", "ctx", None),
        P("fsdp", "ctx", None),
        P("fsdp", None),
        P(),
        P("fsdp", None),
        P("fsdp", None),
        P("fsdp", None),
        P("fsdp", None),
        P(),
        P("fsdp", None),
        P("fsdp", None),
        P("fsdp", None),
        P("fsdp", "ctx", None),
    )
    out_specs = (
        P("fsdp", "ctx", None),
        P("fsdp", "ctx", None),
        P(("ctx", "fsdp")),
        P(("ctx", "fsdp"), None),
        P(("ctx", "fsdp"), None),
        P(("ctx", "fsdp"), None),
        P(("ctx", "fsdp"), None),
        P(("ctx", "fsdp")),
        P("fsdp", "ctx"),
        P("fsdp", "ctx"),
        P("fsdp", "ctx"),
    )
    return jax.shard_map(shards, mesh=mesh, in_specs=in_specs, out_specs=out_specs, check_vma=False)
```

```python
import functools
import math

import jax
import jax.numpy as jnp
from jax import lax
from jax.experimental import pallas as pl
from jax.experimental.layout import Layout, with_layout_constraint
from jax.experimental.pallas import tpu as pltpu
from jax.sharding import PartitionSpec as P

D = 2048
HEADS = 16
HD = 128
EXPERTS = 4
TOPK = 2
PROMPT = 512
CONT = 256
TILE = 256

norm_eps = 1e-05
scale = 1.0 / math.sqrt(HD)
bf16 = jnp.bfloat16
f32 = jnp.float32


def dot(a, b, ca, cb, out=f32):
    r = lax.dot_general(a, b, (((ca,), (cb,)), ((), ())), preferred_element_type=f32)
    return r.astype(out)


def tile_keys(t):
    prompt_tiles = PROMPT // TILE
    if t < prompt_tiles:
        return list(range(t + 1))
    per = CONT // TILE
    first = prompt_tiles + ((t - prompt_tiles) // per) * per
    return list(range(prompt_tiles)) + list(range(first, t + 1))


def load_tile(ref, perm, t, block, cols):
    per = TILE // block
    parts = [
        ref[pl.ds(pl.multiple_of(perm[t * per + i] * block, block), block), cols]
        for i in range(per)
    ]
    return parts[0] if per == 1 else jnp.concatenate(parts, axis=0)


def store_tile(ref, perm, t, block, cols, value):
    per = TILE // block
    for i in range(per):
        ref[pl.ds(pl.multiple_of(perm[t * per + i] * block, block), block), cols] = value[
            i * block : (i + 1) * block
        ]


def spread_keys(ref, tiles):
    runs, start = [], tiles[0]
    for a, b in zip(tiles, tiles[1:] + [None]):
        if b != a + 1:
            runs.append((start, a + 1))
            start = b
    parts = [ref[lo * TILE : hi * TILE, :] for lo, hi in runs]
    return parts[0] if len(parts) == 1 else jnp.concatenate(parts, axis=0)


def causal_fill(scores, value):
    width = scores.shape[1] - TILE
    row = lax.broadcasted_iota(jnp.int32, (TILE, TILE), 0)
    col = lax.broadcasted_iota(jnp.int32, (TILE, TILE), 1)
    last = jnp.where(col <= row, scores[:, width:], value)
    return last if width == 0 else jnp.concatenate([scores[:, :width], last], axis=1)


def forward_kernel(
    block, perm, pre_q, pre_k, pre_v, cos_ref, sin_ref, ctx_ref, q_ref, k_ref, v_ref, log_ref
):
    tiles = pre_q.shape[0] // TILE
    for t in range(tiles):
        rows = slice(t * TILE, (t + 1) * TILE)
        cos, sin = cos_ref[rows, :], sin_ref[rows, :]
        q = load_tile(pre_q, perm, t, block, slice(None))
        q_ref[rows, :] = (q * cos + pltpu.roll(q, HD // 2, 1) * sin).astype(bf16)
        k = load_tile(pre_k, perm, t, block, slice(None))
        k_ref[rows, :] = (k * cos + pltpu.roll(k, HD // 2, 1) * sin).astype(bf16)
        v_ref[rows, :] = load_tile(pre_v, perm, t, block, slice(None)).astype(bf16)
    for t in range(tiles):
        rows = slice(t * TILE, (t + 1) * TILE)
        seen = tile_keys(t)
        keys, values = spread_keys(k_ref, seen), spread_keys(v_ref, seen)
        scores = dot(q_ref[rows, :], keys, 1, 1) * scale
        scores = causal_fill(scores, -1e30)
        top = jnp.max(scores, axis=1, keepdims=True)
        expo = jnp.exp(scores - top)
        total = jnp.sum(expo, axis=1, keepdims=True)
        probs = (expo * (1.0 / total)).astype(bf16)
        context = dot(probs, values, 1, 0).astype(bf16)
        store_tile(ctx_ref, perm, t, block, slice(None), context)
        log_ref[rows, :] = jnp.broadcast_to(top + jnp.log(total), (TILE, HD))


def backward_kernel(
    block,
    perm,
    q_ref,
    k_ref,
    v_ref,
    log_ref,
    do_ref,
    cos_ref,
    sin_ref,
    out_ref,
    dk_ref,
    dv_ref,
):
    tiles = q_ref.shape[0] // TILE
    dk_ref[...] = jnp.zeros_like(dk_ref)
    dv_ref[...] = jnp.zeros_like(dv_ref)
    for t in range(tiles):
        rows = slice(t * TILE, (t + 1) * TILE)
        seen = tile_keys(t)
        keys, values = spread_keys(k_ref, seen), spread_keys(v_ref, seen)
        query = q_ref[rows, :]
        grad = load_tile(do_ref, perm, t, block, slice(None))
        scores = dot(query, keys, 1, 1) * scale
        soft = causal_fill(jnp.exp(scores - log_ref[rows, 0:1]), 0.0)
        grad_prob = dot(grad, values, 1, 1)
        delta = jnp.sum(grad_prob * soft, axis=1, keepdims=True)
        grad_scores = (soft * (grad_prob - delta)).astype(bf16)
        values_back = dot(soft.astype(bf16), grad, 0, 0)
        keys_back = dot(grad_scores, query, 0, 0)
        for i, s in enumerate(seen):
            part, own = slice(i * TILE, (i + 1) * TILE), slice(s * TILE, (s + 1) * TILE)
            dv_ref[own, :] += values_back[part]
            dk_ref[own, :] += keys_back[part]
        back = dot(grad_scores, keys, 1, 0) * scale
        cos, sin = cos_ref[rows, :], sin_ref[rows, :]
        back = back * cos - pltpu.roll(back, HD // 2, 1) * sin
        store_tile(out_ref, perm, t, block, slice(0, HD), back.astype(bf16))
    for t in range(tiles):
        rows = slice(t * TILE, (t + 1) * TILE)
        cos, sin = cos_ref[rows, :], sin_ref[rows, :]
        back = dk_ref[rows, :] * scale
        back = back * cos - pltpu.roll(back, HD // 2, 1) * sin
        store_tile(out_ref, perm, t, block, slice(HD, 2 * HD), back.astype(bf16))
        store_tile(out_ref, perm, t, block, slice(2 * HD, 3 * HD), dv_ref[rows, :].astype(bf16))


def attention_forward(perm, block, pre, cos, sin):
    rows, heads = pre.shape[0], pre.shape[1] // (3 * HD)
    per_head = pl.BlockSpec((rows, HD), lambda h, p: (0, h))
    table = pl.BlockSpec((rows, HD), lambda h, p: (0, 0))
    head_array = jax.ShapeDtypeStruct((rows, heads * HD), bf16)
    return pl.pallas_call(
        functools.partial(forward_kernel, block),
        grid_spec=pltpu.PrefetchScalarGridSpec(
            num_scalar_prefetch=1,
            grid=(heads,),
            in_specs=[
                pl.BlockSpec((rows, HD), lambda h, p: (0, 3 * h)),
                pl.BlockSpec((rows, HD), lambda h, p: (0, 3 * h + 1)),
                pl.BlockSpec((rows, HD), lambda h, p: (0, 3 * h + 2)),
                table,
                table,
            ],
            out_specs=[per_head] * 5,
        ),
        out_shape=[head_array] * 4 + [jax.ShapeDtypeStruct((rows, heads * HD), f32)],
        name="attention_forward",
    )(perm, pre, pre, pre, cos, sin)


def attention_backward(perm, block, q, k, v, log_total, grad, cos, sin):
    rows, heads = q.shape[0], q.shape[1] // HD
    per_head = pl.BlockSpec((rows, HD), lambda h, p: (0, h))
    table = pl.BlockSpec((rows, HD), lambda h, p: (0, 0))
    return pl.pallas_call(
        functools.partial(backward_kernel, block),
        grid_spec=pltpu.PrefetchScalarGridSpec(
            num_scalar_prefetch=1,
            grid=(heads,),
            in_specs=[per_head] * 5 + [table, table],
            out_specs=pl.BlockSpec((rows, 3 * HD), lambda h, p: (0, h)),
            scratch_shapes=[pltpu.VMEM((rows, HD), f32), pltpu.VMEM((rows, HD), f32)],
        ),
        out_shape=jax.ShapeDtypeStruct((rows, 3 * heads * HD), bf16),
        name="attention_backward",
    )(perm, q, k, v, log_total, grad, cos, sin)


def expert_kernel(kept, x_ref, g_ref, wg_ref, wu_ref, wd_ref, *refs):
    hidden_ref, gate_ref, up_ref = refs[kept:]
    count = x_ref.shape[0] // 2
    for p in range(2):
        rows = slice(p * count, (p + 1) * count)
        gate = dot(x_ref[rows, :], wg_ref[...], 1, 1)
        up = dot(x_ref[rows, :], wu_ref[...], 1, 1)
        grad = dot(g_ref[rows, :], wd_ref[...], 1, 1)
        sigmoid = jax.nn.sigmoid(gate)
        silu = gate * sigmoid
        hidden_ref[rows, :] = (silu * up).astype(bf16)
        gate_ref[rows, :] = (grad * up * sigmoid * (1.0 + gate * (1.0 - sigmoid))).astype(bf16)
        up_ref[rows, :] = (grad * silu).astype(bf16)


def expert_hidden(part, parts, slots, grads, weights, kept):
    rows, units = slots.shape[0], weights[0].shape[0]
    tile = 256 if units % 256 == 0 else 128
    whole = pl.BlockSpec((rows, D), lambda i: (0, 0))
    weight = pl.BlockSpec((tile, D), lambda i: (i, 0))
    result = pl.BlockSpec((rows, tile), lambda i: (part, i))
    return pl.pallas_call(
        functools.partial(expert_kernel, len(kept)),
        grid=(units // tile,),
        in_specs=[whole] * 2 + [weight] * 3 + [pl.BlockSpec(memory_space=pl.ANY)] * len(kept),
        out_specs=[result] * 3,
        out_shape=[jax.ShapeDtypeStruct((parts * rows, units), bf16)] * 3,
        input_output_aliases={5 + i: i for i in range(len(kept))},
        name="expert_hidden",
    )(slots, grads, *weights, *kept)


def rows_kernel(count, *refs):
    total = dot(refs[0][...], refs[count][...], 1, 0)
    for i in range(1, count):
        total = total + dot(refs[i][...], refs[count + i][...], 1, 0)
    refs[-1][...] = total.astype(bf16)


def expert_rows(part, rows, left, right):
    units, tile = right[0].shape[0], 256
    return pl.pallas_call(
        functools.partial(rows_kernel, len(left)),
        grid=(D // tile,),
        in_specs=[pl.BlockSpec((rows, units), lambda n: (part, 0))] * len(left)
        + [pl.BlockSpec((units, tile), lambda n: (0, n))] * len(right),
        out_specs=pl.BlockSpec((rows, tile), lambda n: (0, n)),
        out_shape=jax.ShapeDtypeStruct((rows, D), bf16),
        name="expert_rows",
    )(*left, *right)


def join_kernel(own_blocks, part_blocks, where, own_ref, *refs):
    parts, out_ref = refs[:-1], refs[-1]
    i = pl.program_id(0)
    inside = i - where[0] * own_blocks

    @pl.when((inside >= 0) & (inside < own_blocks))
    def _():
        out_ref[...] = own_ref[...]

    for s, part in enumerate(parts):
        place = i - where[1 + s]

        @pl.when((place >= 0) & (place < part_blocks))
        def _(part=part):
            out_ref[...] = part[...]


def join_weights(side, starts, own, parts):
    size, count = own.shape[0], parts[0].shape[0]
    tile = count // 2 if count % 32 == 0 else count
    own_blocks, part_blocks = size // tile, count // tile
    where = jnp.stack([side] + [start * part_blocks for start in starts]).astype(jnp.int32)

    def part_spec(s):
        return pl.BlockSpec(
            (tile, D), lambda i, w: (jnp.clip(i - w[1 + s], 0, part_blocks - 1), 0)
        )

    return pl.pallas_call(
        functools.partial(join_kernel, own_blocks, part_blocks),
        grid_spec=pltpu.PrefetchScalarGridSpec(
            num_scalar_prefetch=1,
            grid=(2 * own_blocks,),
            in_specs=[
                pl.BlockSpec(
                    (tile, D),
                    lambda i, w: (jnp.clip(i - w[0] * own_blocks, 0, own_blocks - 1), 0),
                )
            ]
            + [part_spec(s) for s in range(len(parts))],
            out_specs=pl.BlockSpec((tile, D), lambda i, w: (i, 0)),
        ),
        out_shape=jax.ShapeDtypeStruct((2 * size, D), own.dtype),
        name="join_weights",
    )(where, own, *parts)


def rope_tables(group_len):
    index = jnp.arange(group_len, dtype=jnp.int32)
    position = jnp.where(index < PROMPT, index, PROMPT + (index - PROMPT) % CONT).astype(f32)
    half = HD // 2
    frequency = jnp.exp(-math.log(10000.0) * jnp.arange(half, dtype=f32) / half)
    angles = position[:, None] * frequency[None, :]
    cosine, sine = jnp.cos(angles), jnp.sin(angles)
    return (
        jnp.concatenate([cosine, cosine], axis=1),
        jnp.concatenate([-sine, sine], axis=1),
    )


def after(*arrays):
    return lax.optimization_barrier(arrays)


def normalize_parts(values, gain):
    inverse = lax.rsqrt(jnp.mean(values * values, axis=-1, keepdims=True) + norm_eps)
    unit_rows = values * inverse
    return (unit_rows * gain, unit_rows, inverse)


def norm_backward(grad_outer, unit_rows, inverse, gain):
    grad_unit = grad_outer * gain
    grad_inner = inverse * (
        grad_unit - unit_rows * jnp.mean(grad_unit * unit_rows, axis=-1, keepdims=True)
    )
    return (grad_inner, jnp.sum(grad_outer * unit_rows, axis=0))


def shards(
    tokens,
    route_ids,
    gate_values,
    deal,
    norm1_gain,
    w_query,
    w_key,
    w_value,
    w_out,
    norm2_gain,
    w_gate,
    w_up,
    w_down,
    cotangent,
):
    rows = tokens.shape[1]
    ctx_count = lax.axis_size("ctx")
    fsdp_count = lax.axis_size("fsdp")
    group_len = rows * ctx_count
    capacity = 5 * rows * TOPK // (4 * EXPERTS)
    repeats = fsdp_count // EXPERTS
    pair = 2
    columns = repeats // pair
    core = lax.axis_index("ctx")
    expert = lax.axis_index("fsdp") // repeats
    width = D // ctx_count
    heads = HEADS // ctx_count

    def core_shift(a, s):
        return lax.ppermute(a, "ctx", [(i, (i + s) % ctx_count) for i in range(ctx_count)])

    def fsdp_shift(a, move):
        return lax.ppermute(a, "fsdp", [(i, move(i)) for i in range(fsdp_count)])

    def expert_shift(a, k):
        return fsdp_shift(a, lambda i: (i + k * repeats) % fsdp_count)

    def column_shift(a, j):
        def move(i):
            e, r = divmod(i, repeats)
            t, w = divmod(r, pair)
            return e * repeats + ((t + j) % columns) * pair + w

        return fsdp_shift(a, move)

    def pair_swap(a):
        return fsdp_shift(a, lambda i: i ^ 1)

    def core_gather(a):
        return jnp.concatenate([a] + [core_shift(a, s) for s in range(1, ctx_count)], axis=0)

    block_count = deal.shape[1]
    block = group_len // block_count
    local_blocks = block_count // ctx_count
    dealt = jnp.argsort(deal[0]).astype(jnp.int32)
    perm = ((core - dealt // local_blocks) % ctx_count) * local_blocks + dealt % local_blocks
    cos, sin = rope_tables(group_len)

    def own_columns(w):
        return lax.dynamic_slice_in_dim(w, core * width, width, axis=1)

    by_head = [own_columns(w).reshape(-1, heads, HD) for w in (w_query, w_key, w_value)]
    packed = jnp.concatenate(
        [jnp.stack(by_head, axis=2).reshape(-1, 3 * width), own_columns(w_out)], axis=1
    )
    packed = with_layout_constraint(packed, Layout(major_to_minor=(0, 1)))
    gathered = lax.all_gather(packed, "fsdp", axis=0, tiled=True)
    gathered = with_layout_constraint(gathered, Layout(major_to_minor=(0, 1)))

    halves = 2
    part_slots = capacity // halves
    half = EXPERTS * part_slots
    ids = route_ids[0]
    flat = ids.reshape(-1)
    onehot = (flat[:, None] == jnp.arange(EXPERTS, dtype=jnp.int32)[None, :]).astype(jnp.int32)
    earlier = jnp.cumsum(onehot, axis=0) - onehot
    slot = jnp.sum(earlier * onehot, axis=1)
    place = (slot // part_slots) * half + flat * part_slots + slot % part_slots
    place = jnp.where(slot < capacity, place, -1).reshape(rows, TOPK)
    targets = jnp.arange(halves * half, dtype=jnp.int32)
    select = [(place[:, k : k + 1] == targets[None, :]).astype(bf16) for k in range(TOPK)]
    spread = [(targets[:, None] == place[None, :, k]).astype(bf16) for k in range(TOPK)]
    gates = gate_values[0]

    dy = cotangent[0].astype(f32)
    grad_pairs = jnp.concatenate([(dy * gates[:, k : k + 1]).astype(bf16) for k in range(TOPK)])
    spread_both = jnp.concatenate(spread, axis=1)
    grad_blocks = [
        dot(spread_both[h * half : (h + 1) * half], grad_pairs, 1, 0, bf16) for h in range(halves)
    ]

    inputs = tokens[0].astype(f32)
    normed_f, _, _ = normalize_parts(inputs, norm1_gain)
    normed = core_gather(normed_f.astype(bf16))

    per = D // (ctx_count * fsdp_count)
    mine = lax.axis_index("fsdp")
    my_column, my_side = (mine % repeats) // pair, mine % pair

    index = jnp.arange(D, dtype=jnp.int32)
    source = (index // per % ctx_count) * (D // ctx_count)
    source = source + index // (per * ctx_count) * per + index % per
    shuffle = (index[:, None] == source[None, :]).astype(bf16)
    normed_mixed = dot(normed, shuffle, 1, 0, bf16)

    def weight_part(w):
        count = w.shape[0] // ctx_count
        return lax.dynamic_slice_in_dim(w, core * count, count, axis=0)

    weight_parts = [weight_part(w) for w in (w_gate, w_up, w_down)]
    gathered, normed_mixed, *tied = after(gathered, normed_mixed, *grad_blocks, *weight_parts)
    grad_blocks, weight_parts = tied[:halves], tied[halves:]
    out_columns = gathered[:, 3 * width :]
    full_qkv = gathered[:, : 3 * width]

    lines = [[r + e * repeats for e in range(EXPERTS)] for r in range(repeats)]

    def swap_experts(a, width=D):
        blocks = a.reshape(EXPERTS, -1, width)
        return lax.all_to_all(blocks, "fsdp", 0, 0, axis_index_groups=lines, tiled=True)

    def to_columns(a):
        return [a] + [column_shift(a, j) for j in range(1, columns)]

    grads_first = swap_experts(grad_blocks[0]).reshape(half, D)

    sides = [[i, i ^ 1] for i in range(0, fsdp_count, 2)]
    sides = [sorted(group) for group in sides]
    swapped = [
        lax.all_gather(part, "fsdp", axis=0, tiled=True, axis_index_groups=sides)
        for part in weight_parts
    ]

    starts = [(1 - my_side) * ctx_count + (core - s) % ctx_count for s in range(ctx_count)]

    def pair_weights(own, both):
        count = both.shape[0] // pair
        part = lax.dynamic_slice_in_dim(both, (1 - my_side) * count, count, axis=0)
        return join_weights(
            my_side, starts, own, [part] + [core_shift(part, s) for s in range(1, ctx_count)]
        )

    pre = dot(normed, full_qkv, 1, 0)
    context, q, k, v, log_total = attention_forward(perm, block, pre, cos, sin)

    def out_rows(c):
        return lax.dynamic_slice_in_dim(out_columns, (c % ctx_count) * width, width, axis=0)

    if ctx_count == 2:
        own_part, other = out_rows(core), core_shift(out_rows(core + 1), 1)
        w_o = jnp.concatenate(
            [jnp.where(core == 0, own_part, other), jnp.where(core == 0, other, own_part)], axis=1
        )
    else:
        w_o = lax.all_to_all(out_columns.reshape(ctx_count, width, width), "ctx", 0, 0)
        w_o = w_o.transpose(1, 0, 2).reshape(width, D)
    away = [dot(context[s * rows : (s + 1) * rows], w_o, 1, 0, bf16) for s in range(1, ctx_count)]
    attention = dot(context[:rows], w_o, 1, 0)
    for s in range(1, ctx_count):
        attention = attention + core_shift(away[s - 1], -s).astype(f32)
    hidden_in = inputs + attention
    normed_two_f, unit_two, inverse_two = normalize_parts(hidden_in, norm2_gain)
    normed_two = normed_two_f.astype(bf16)

    spread_any = spread[0] + spread[1]
    slot_blocks = [
        dot(spread_any[h * half : (h + 1) * half], normed_two, 1, 0, bf16) for h in range(halves)
    ]
    grads_first, waiting, _ = after(grads_first, grad_blocks[1], away[0])
    grads_second = swap_experts(waiting).reshape(half, D)
    grad_parts = to_columns(grads_first)
    got = after(grads_second, *slot_blocks, *swapped[:2], *grad_parts[1:])
    grads_second, slots_a, slots_b, *swapped_two = got[:5]
    grad_parts[1:] = got[5:]
    grad_parts += to_columns(grads_second)
    first = swap_experts(slots_a).reshape(half, D)
    wg, wu = (pair_weights(*w) for w in zip((w_gate, w_up), swapped_two))
    got = after(first, slots_b, swapped[2], wg, wu, *grad_parts[columns + 1 :])
    first, slots_b, swapped_down, wg, wu = got[:5]
    grad_parts[columns + 1 :] = got[5:]
    second = swap_experts(slots_b).reshape(half, D)
    wd = pair_weights(w_down, swapped_down)
    weights = (wg, wu, wd)
    parts = halves * columns

    def hidden_part(index, slots, state):
        return expert_hidden(index, parts, slots, grad_parts[index], weights, state)

    def grad_rows(index, state):
        return expert_rows(index, half, state[1:], (wg, wu))

    def columns_home(pieces):
        return [column_shift(part, -(j + 1)) for j, part in enumerate(pieces)]

    def add_parts(own, returned):
        total = own.astype(f32)
        for part in returned:
            total = total + part.astype(f32)
        return total.astype(bf16)

    slot_parts = to_columns(first)
    back, came = {}, [None] * halves
    state = hidden_part(0, slot_parts[0], ())
    second, *got = after(second, *state, *slot_parts[1:])
    state, slot_parts[1:] = got[:3], got[3:]
    slot_parts += to_columns(second)
    for h in range(halves):
        for j in range(1, columns):
            index = h * columns + j
            state = hidden_part(index, slot_parts[index], state)
        for j in range(1, columns):
            index = h * columns + j
            back[index] = grad_rows(index, state)
            back[index], *state = after(back[index], *state)
        if h == 0:
            got = after(*state, *slot_parts[columns + 1 :])
            state, slot_parts[columns + 1 :] = got[:3], got[3:]
        came[h] = columns_home([back[h * columns + j] for j in range(1, columns)])
    back[0] = grad_rows(0, state)
    home_first, *got = after(back[0], *state, *came[0])
    state = got[:3]
    home_first = add_parts(home_first, got[3:])
    home_first, *state = after(home_first, *state)
    home_first = swap_experts(home_first)
    state = hidden_part(columns, slot_parts[columns], state)
    back[columns] = grad_rows(columns, state)
    back[columns], home_first, *state = after(back[columns], home_first, *state)
    hidden, grad_gate, grad_up = state
    all_slots = jnp.concatenate(slot_parts, axis=0)
    all_grads = jnp.concatenate(grad_parts, axis=0)

    def core_sum(part):
        total = lax.dynamic_slice_in_dim(part, core * width, width, axis=1).astype(f32)
        for s in range(1, ctx_count):
            start = ((core + s) % ctx_count) * width
            total = total + core_shift(
                lax.dynamic_slice_in_dim(part, start, width, axis=1), s
            ).astype(f32)
        return total.astype(bf16)

    def side_sum(total):
        return lax.psum_scatter(
            total, "fsdp", scatter_dimension=0, tiled=True, axis_index_groups=sides
        ).astype(f32)

    def out_rows_of(h, j, left):
        return expert_rows(h * columns + j, half, (left,), (wd,))

    home_second, hidden_t, *got = after(back[columns], hidden, *came[1])
    home_second = add_parts(home_second, got)
    home_second, hidden_t = after(home_second, hidden_t)
    home_second = swap_experts(home_second)
    down_part = dot(hidden_t, all_grads, 0, 0, bf16)
    down_part, hidden_t = after(down_part, hidden_t)
    away_first = [out_rows_of(0, j, hidden_t) for j in range(1, columns)]
    home_second, hidden_t, *away_first = after(home_second, hidden_t, *away_first)
    away_first = columns_home(away_first)
    down_total = core_sum(down_part)

    def side_swap_sum(total):
        def side_rows(i):
            size = total.shape[0] // pair
            return lax.dynamic_slice_in_dim(total, (i % pair) * size, size, axis=0)

        return side_rows(my_side), pair_swap(side_rows(my_side + 1))

    grad_slot_in = jnp.concatenate([home_first, home_second], axis=0).reshape(halves * half, D)

    grad_normed_two = dot(select[0] + select[1], grad_slot_in, 1, 0)
    grad_norm_two, norm2_part = norm_backward(grad_normed_two, unit_two, inverse_two, norm2_gain)
    grad_hidden_in = dy + grad_norm_two
    grad_attention = core_gather(grad_hidden_in.astype(bf16))
    def reduce_blocks(blocks, shift):
        total = blocks[0].astype(f32)
        for d in range(1, len(blocks)):
            total = total + shift(blocks[d].astype(bf16), d).astype(f32)
        return total.astype(bf16)

    def cut(a, n):
        size = a.shape[0] // n
        return [a[i * size : (i + 1) * size] for i in range(n)]

    def expert_sum(total):
        blocks = swap_experts(total, total.shape[1])
        return jnp.sum(blocks.reshape(EXPERTS, -1, total.shape[1]).astype(f32), axis=0)

    def row_blocks(a, n, own):
        split = a.reshape(EXPERTS, n, -1, a.shape[1])
        return [
            lax.dynamic_slice_in_dim(split, (own + d) % n, 1, axis=1).reshape(-1, a.shape[1])
            for d in range(n)
        ]

    out_part = dot(context, grad_attention, 0, 0, bf16)
    blocks_o = row_blocks(out_part, columns, my_column)
    got = after(grad_attention, down_total, *blocks_o)
    grad_attention, down_total, blocks_o = got[0], got[1], got[2:]
    down_grad = side_sum(down_total)
    came_o = [column_shift(block, d) for d, block in enumerate(blocks_o) if d]
    grad_context = dot(grad_attention, w_o, 1, 1, bf16)
    grad_qkv = attention_backward(
        perm, block, q, k, v, log_total, grad_context, cos, sin
    )
    qkv_part = dot(normed_mixed, grad_qkv, 0, 0, bf16)
    qkv_sum = lax.psum_scatter(qkv_part, "fsdp", scatter_dimension=0, tiled=True)

    got = after(qkv_part, grad_qkv, hidden_t, grad_gate, grad_up, *away_first)
    grad_qkv, hidden_t, gate_t, up_t, *away_first = got[1:]
    gate_part = dot(gate_t, all_slots, 0, 0, bf16)
    gate_part, hidden_t, *came_o = after(gate_part, hidden_t, *came_o)
    blocks_o = row_blocks(add_parts(blocks_o[0], came_o), pair, my_side)
    hidden_t, *blocks_o = after(hidden_t, *blocks_o)
    came_o = pair_swap(blocks_o[1])
    outs_first = add_parts(out_rows_of(0, 0, hidden_t), away_first)
    away_second = [out_rows_of(1, j, hidden_t) for j in range(1, columns)]
    gate_total = core_sum(gate_part)
    outs_first, gate_total, up_t, *away_second = after(outs_first, gate_total, up_t, *away_second)
    away_second = columns_home(away_second)
    outs_first = swap_experts(outs_first)
    gate_own, gate_came = side_swap_sum(gate_total)

    up_part = dot(up_t, all_slots, 0, 0, bf16)
    got = after(up_part, hidden_t, grad_qkv, outs_first, came_o, gate_came, *away_second)
    up_part, hidden_t, grad_qkv, outs_first, came_o, gate_came, *away_second = got
    out_grad = expert_sum(add_parts(blocks_o[0], [came_o]))
    outs_second = add_parts(out_rows_of(1, 0, hidden_t), away_second)
    up_total = core_sum(up_part)
    outs_second, up_total, grad_qkv, out_grad = after(outs_second, up_total, grad_qkv, out_grad)
    outs_second = swap_experts(outs_second)
    up_own, up_came = side_swap_sum(up_total)

    def back_rows(s, out):
        return dot(grad_qkv[s * rows : (s + 1) * rows], full_qkv, 1, 1, out)

    back_away = [back_rows(s, bf16) for s in range(1, ctx_count)]
    grad_normed = back_rows(0, f32)
    for s in range(1, ctx_count):
        grad_normed = grad_normed + core_shift(back_away[s - 1], -s).astype(f32)
    _, unit_one, inverse_one = normalize_parts(inputs, norm1_gain)
    grad_norm_one, norm1_part = norm_backward(grad_normed, unit_one, inverse_one, norm1_gain)
    tokens_grad = (grad_hidden_in + grad_norm_one).astype(bf16)
    got = after(tokens_grad, norm1_part, outs_second, up_own, up_came, qkv_sum, gate_own)
    tokens_grad, norm1_part, outs_second, up_own, up_came, qkv_sum, gate_own = got
    gate_grad = gate_own.astype(f32) + gate_came.astype(f32)

    gains = jnp.stack([norm1_part, norm2_part]).reshape(2, ctx_count, fsdp_count, per)
    gains = lax.all_to_all(gains.transpose(2, 1, 0, 3), "fsdp", 0, 0, tiled=True)
    gains = jnp.sum(gains, axis=0)

    def gains_of(c):
        return lax.dynamic_index_in_dim(gains, c % ctx_count, 0, keepdims=False)

    gains_own = gains_of(core)
    for s in range(1, ctx_count):
        gains_own = gains_own + core_shift(gains_of(core + s), s)
    up_grad = up_own.astype(f32) + up_came.astype(f32)
    sums = qkv_sum.reshape(ctx_count, per, heads, 3, HD).astype(f32)
    sums = sums.transpose(3, 0, 1, 2, 4).reshape(3, ctx_count, per, width)

    def core_piece(c):
        return lax.dynamic_index_in_dim(sums, c % ctx_count, 1, keepdims=False)

    if ctx_count == 2:
        own_part, other = core_piece(core), core_shift(core_piece(core + 1), 1)
        qkv_own = jnp.concatenate(
            [jnp.where(core == 0, own_part, other), jnp.where(core == 0, other, own_part)], axis=2
        )
    else:
        qkv_own = lax.all_to_all(sums.astype(bf16), "ctx", 1, 1).astype(f32)
        qkv_own = qkv_own.transpose(0, 2, 1, 3).reshape(3, per, D)
    query_grad, key_grad, value_grad = qkv_own[0], qkv_own[1], qkv_own[2]

    slot_out = jnp.concatenate([outs_first, outs_second], axis=0).reshape(halves * half, D)
    mixed = hidden_in
    for i in range(TOPK):
        mixed = mixed + dot(select[i], slot_out, 1, 0) * gates[:, i : i + 1]

    return (
        mixed.astype(bf16)[None],
        tokens_grad[None],
        gains_own[0],
        query_grad,
        key_grad,
        value_grad,
        out_grad,
        gains_own[1],
        gate_grad,
        up_grad,
        down_grad,
    )


def solution(mesh):
    in_specs = (
        P("fsdp", "ctx", None),
        P("fsdp", "ctx", None),
        P("fsdp", "ctx", None),
        P("fsdp", None),
        P(),
        P("fsdp", None),
        P("fsdp", None),
        P("fsdp", None),
        P("fsdp", None),
        P(),
        P("fsdp", None),
        P("fsdp", None),
        P("fsdp", None),
        P("fsdp", "ctx", None),
    )
    out_specs = (
        P("fsdp", "ctx", None),
        P("fsdp", "ctx", None),
        P(("ctx", "fsdp")),
        P(("ctx", "fsdp"), None),
        P(("ctx", "fsdp"), None),
        P(("ctx", "fsdp"), None),
        P(("ctx", "fsdp"), None),
        P(("ctx", "fsdp")),
        P("fsdp", "ctx"),
        P("fsdp", "ctx"),
        P("fsdp", "ctx"),
    )
    return jax.shard_map(shards, mesh=mesh, in_specs=in_specs, out_specs=out_specs, check_vma=False)
```

```python
import functools
import math

import jax
import jax.numpy as jnp
from jax import lax
from jax.experimental import pallas as pl
from jax.experimental.layout import Layout, with_layout_constraint
from jax.experimental.pallas import tpu as pltpu
from jax.sharding import PartitionSpec as P

D = 2048
HEADS = 16
HD = 128
EXPERTS = 4
TOPK = 2
PROMPT = 512
CONT = 256
TILE = 256

norm_eps = 1e-05
scale = 1.0 / math.sqrt(HD)
bf16 = jnp.bfloat16
f32 = jnp.float32


def dot(a, b, ca, cb, out=f32):
    r = lax.dot_general(a, b, (((ca,), (cb,)), ((), ())), preferred_element_type=f32)
    return r.astype(out)


def tile_keys(t):
    prompt_tiles = PROMPT // TILE
    if t < prompt_tiles:
        return list(range(t + 1))
    per = CONT // TILE
    first = prompt_tiles + ((t - prompt_tiles) // per) * per
    return list(range(prompt_tiles)) + list(range(first, t + 1))


def load_tile(ref, perm, t, block, cols):
    per = TILE // block
    parts = [
        ref[pl.ds(pl.multiple_of(perm[t * per + i] * block, block), block), cols]
        for i in range(per)
    ]
    return parts[0] if per == 1 else jnp.concatenate(parts, axis=0)


def store_tile(ref, perm, t, block, cols, value):
    per = TILE // block
    for i in range(per):
        ref[pl.ds(pl.multiple_of(perm[t * per + i] * block, block), block), cols] = value[
            i * block : (i + 1) * block
        ]


def spread_keys(ref, tiles):
    runs, start = [], tiles[0]
    for a, b in zip(tiles, tiles[1:] + [None]):
        if b != a + 1:
            runs.append((start, a + 1))
            start = b
    parts = [ref[lo * TILE : hi * TILE, :] for lo, hi in runs]
    return parts[0] if len(parts) == 1 else jnp.concatenate(parts, axis=0)


def causal_fill(scores, value):
    width = scores.shape[1] - TILE
    row = lax.broadcasted_iota(jnp.int32, (TILE, TILE), 0)
    col = lax.broadcasted_iota(jnp.int32, (TILE, TILE), 1)
    last = jnp.where(col <= row, scores[:, width:], value)
    return last if width == 0 else jnp.concatenate([scores[:, :width], last], axis=1)


def forward_kernel(
    block, perm, pre_q, pre_k, pre_v, cos_ref, sin_ref, ctx_ref, q_ref, k_ref, v_ref, log_ref
):
    tiles = pre_q.shape[0] // TILE
    for t in range(tiles):
        rows = slice(t * TILE, (t + 1) * TILE)
        cos, sin = cos_ref[rows, :], sin_ref[rows, :]
        q = load_tile(pre_q, perm, t, block, slice(None))
        q_ref[rows, :] = (q * cos + pltpu.roll(q, HD // 2, 1) * sin).astype(bf16)
        k = load_tile(pre_k, perm, t, block, slice(None))
        k_ref[rows, :] = (k * cos + pltpu.roll(k, HD // 2, 1) * sin).astype(bf16)
        v_ref[rows, :] = load_tile(pre_v, perm, t, block, slice(None)).astype(bf16)
    for t in range(tiles):
        rows = slice(t * TILE, (t + 1) * TILE)
        seen = tile_keys(t)
        keys, values = spread_keys(k_ref, seen), spread_keys(v_ref, seen)
        scores = dot(q_ref[rows, :], keys, 1, 1) * scale
        scores = causal_fill(scores, -1e30)
        top = jnp.max(scores, axis=1, keepdims=True)
        expo = jnp.exp(scores - top)
        total = jnp.sum(expo, axis=1, keepdims=True)
        probs = (expo * (1.0 / total)).astype(bf16)
        context = dot(probs, values, 1, 0).astype(bf16)
        store_tile(ctx_ref, perm, t, block, slice(None), context)
        log_ref[rows, :] = jnp.broadcast_to(top + jnp.log(total), (TILE, HD))


def backward_kernel(
    block,
    perm,
    q_ref,
    k_ref,
    v_ref,
    log_ref,
    do_ref,
    cos_ref,
    sin_ref,
    out_ref,
    dk_ref,
    dv_ref,
):
    tiles = q_ref.shape[0] // TILE
    dk_ref[...] = jnp.zeros_like(dk_ref)
    dv_ref[...] = jnp.zeros_like(dv_ref)
    for t in range(tiles):
        rows = slice(t * TILE, (t + 1) * TILE)
        seen = tile_keys(t)
        keys, values = spread_keys(k_ref, seen), spread_keys(v_ref, seen)
        query = q_ref[rows, :]
        grad = load_tile(do_ref, perm, t, block, slice(None))
        scores = dot(query, keys, 1, 1) * scale
        soft = causal_fill(jnp.exp(scores - log_ref[rows, 0:1]), 0.0)
        grad_prob = dot(grad, values, 1, 1)
        delta = jnp.sum(grad_prob * soft, axis=1, keepdims=True)
        grad_scores = (soft * (grad_prob - delta)).astype(bf16)
        values_back = dot(soft.astype(bf16), grad, 0, 0)
        keys_back = dot(grad_scores, query, 0, 0)
        for i, s in enumerate(seen):
            part, own = slice(i * TILE, (i + 1) * TILE), slice(s * TILE, (s + 1) * TILE)
            dv_ref[own, :] += values_back[part]
            dk_ref[own, :] += keys_back[part]
        back = dot(grad_scores, keys, 1, 0) * scale
        cos, sin = cos_ref[rows, :], sin_ref[rows, :]
        back = back * cos - pltpu.roll(back, HD // 2, 1) * sin
        store_tile(out_ref, perm, t, block, slice(0, HD), back.astype(bf16))
    for t in range(tiles):
        rows = slice(t * TILE, (t + 1) * TILE)
        cos, sin = cos_ref[rows, :], sin_ref[rows, :]
        back = dk_ref[rows, :] * scale
        back = back * cos - pltpu.roll(back, HD // 2, 1) * sin
        store_tile(out_ref, perm, t, block, slice(HD, 2 * HD), back.astype(bf16))
        store_tile(out_ref, perm, t, block, slice(2 * HD, 3 * HD), dv_ref[rows, :].astype(bf16))


def attention_forward(perm, block, pre, cos, sin):
    rows, heads = pre.shape[0], pre.shape[1] // (3 * HD)
    per_head = pl.BlockSpec((rows, HD), lambda h, p: (0, h))
    table = pl.BlockSpec((rows, HD), lambda h, p: (0, 0))
    head_array = jax.ShapeDtypeStruct((rows, heads * HD), bf16)
    return pl.pallas_call(
        functools.partial(forward_kernel, block),
        grid_spec=pltpu.PrefetchScalarGridSpec(
            num_scalar_prefetch=1,
            grid=(heads,),
            in_specs=[
                pl.BlockSpec((rows, HD), lambda h, p: (0, 3 * h)),
                pl.BlockSpec((rows, HD), lambda h, p: (0, 3 * h + 1)),
                pl.BlockSpec((rows, HD), lambda h, p: (0, 3 * h + 2)),
                table,
                table,
            ],
            out_specs=[per_head] * 5,
        ),
        out_shape=[head_array] * 4 + [jax.ShapeDtypeStruct((rows, heads * HD), f32)],
        name="attention_forward",
    )(perm, pre, pre, pre, cos, sin)


def attention_backward(perm, block, q, k, v, log_total, grad, cos, sin):
    rows, heads = q.shape[0], q.shape[1] // HD
    per_head = pl.BlockSpec((rows, HD), lambda h, p: (0, h))
    table = pl.BlockSpec((rows, HD), lambda h, p: (0, 0))
    return pl.pallas_call(
        functools.partial(backward_kernel, block),
        grid_spec=pltpu.PrefetchScalarGridSpec(
            num_scalar_prefetch=1,
            grid=(heads,),
            in_specs=[per_head] * 5 + [table, table],
            out_specs=pl.BlockSpec((rows, 3 * HD), lambda h, p: (0, h)),
            scratch_shapes=[pltpu.VMEM((rows, HD), f32), pltpu.VMEM((rows, HD), f32)],
        ),
        out_shape=jax.ShapeDtypeStruct((rows, 3 * heads * HD), bf16),
        name="attention_backward",
    )(perm, q, k, v, log_total, grad, cos, sin)


def expert_kernel(kept, x_ref, g_ref, wg_ref, wu_ref, wd_ref, *refs):
    hidden_ref, gate_ref, up_ref, back_ref, total_ref = refs[kept:]
    count = x_ref.shape[0] // 2

    @pl.when(pl.program_id(0) == 0)
    def _():
        total_ref[...] = jnp.zeros_like(total_ref)

    both = jnp.concatenate([wg_ref[...], wu_ref[...]], axis=0)
    for p in range(2):
        rows = slice(p * count, (p + 1) * count)
        gate = dot(x_ref[rows, :], wg_ref[...], 1, 1)
        up = dot(x_ref[rows, :], wu_ref[...], 1, 1)
        grad = dot(g_ref[rows, :], wd_ref[...], 1, 1)
        sigmoid = jax.nn.sigmoid(gate)
        silu = gate * sigmoid
        hidden_ref[rows, :] = (silu * up).astype(bf16)
        grad_gate = (grad * up * sigmoid * (1.0 + gate * (1.0 - sigmoid))).astype(bf16)
        grad_up = (grad * silu).astype(bf16)
        gate_ref[rows, :] = grad_gate
        up_ref[rows, :] = grad_up
        total_ref[rows, :] += dot(jnp.concatenate([grad_gate, grad_up], axis=1), both, 1, 0)

    @pl.when(pl.program_id(0) == pl.num_programs(0) - 1)
    def _():
        back_ref[...] = total_ref[...].astype(bf16)


def expert_hidden(part, parts, slots, grads, weights, kept):
    rows, units = slots.shape[0], weights[0].shape[0]
    tile = 256 if units % 256 == 0 else 128
    whole = pl.BlockSpec((rows, D), lambda i: (0, 0))
    weight = pl.BlockSpec((tile, D), lambda i: (i, 0))
    result = pl.BlockSpec((rows, tile), lambda i: (part, i))
    return pl.pallas_call(
        functools.partial(expert_kernel, len(kept)),
        grid=(units // tile,),
        in_specs=[whole] * 2 + [weight] * 3 + [pl.BlockSpec(memory_space=pl.ANY)] * len(kept),
        out_specs=[result] * 3 + [whole],
        out_shape=[jax.ShapeDtypeStruct((parts * rows, units), bf16)] * 3
        + [jax.ShapeDtypeStruct((rows, D), bf16)],
        scratch_shapes=[pltpu.VMEM((rows, D), f32)],
        input_output_aliases={5 + i: i for i in range(len(kept))},
        name="expert_hidden",
    )(slots, grads, *weights, *kept)


def rows_kernel(count, *refs):
    total = dot(refs[0][...], refs[count][...], 1, 0)
    for i in range(1, count):
        total = total + dot(refs[i][...], refs[count + i][...], 1, 0)
    refs[-1][...] = total.astype(bf16)


def expert_rows(part, rows, left, right):
    units, tile = right[0].shape[0], 256
    return pl.pallas_call(
        functools.partial(rows_kernel, len(left)),
        grid=(D // tile,),
        in_specs=[pl.BlockSpec((rows, units), lambda n: (part, 0))] * len(left)
        + [pl.BlockSpec((units, tile), lambda n: (0, n))] * len(right),
        out_specs=pl.BlockSpec((rows, tile), lambda n: (0, n)),
        out_shape=jax.ShapeDtypeStruct((rows, D), bf16),
        name="expert_rows",
    )(*left, *right)


def join_kernel(own_blocks, part_blocks, where, own_ref, *refs):
    parts, out_ref = refs[:-1], refs[-1]
    i = pl.program_id(0)
    inside = i - where[0] * own_blocks

    @pl.when((inside >= 0) & (inside < own_blocks))
    def _():
        out_ref[...] = own_ref[...]

    for s, part in enumerate(parts):
        place = i - where[1 + s]

        @pl.when((place >= 0) & (place < part_blocks))
        def _(part=part):
            out_ref[...] = part[...]


def join_weights(side, starts, own, parts):
    size, count = own.shape[0], parts[0].shape[0]
    tile = count // 2 if count % 32 == 0 else count
    own_blocks, part_blocks = size // tile, count // tile
    where = jnp.stack([side] + [start * part_blocks for start in starts]).astype(jnp.int32)

    def part_spec(s):
        return pl.BlockSpec(
            (tile, D), lambda i, w: (jnp.clip(i - w[1 + s], 0, part_blocks - 1), 0)
        )

    return pl.pallas_call(
        functools.partial(join_kernel, own_blocks, part_blocks),
        grid_spec=pltpu.PrefetchScalarGridSpec(
            num_scalar_prefetch=1,
            grid=(2 * own_blocks,),
            in_specs=[
                pl.BlockSpec(
                    (tile, D),
                    lambda i, w: (jnp.clip(i - w[0] * own_blocks, 0, own_blocks - 1), 0),
                )
            ]
            + [part_spec(s) for s in range(len(parts))],
            out_specs=pl.BlockSpec((tile, D), lambda i, w: (i, 0)),
        ),
        out_shape=jax.ShapeDtypeStruct((2 * size, D), own.dtype),
        name="join_weights",
    )(where, own, *parts)


def rope_tables(group_len):
    index = jnp.arange(group_len, dtype=jnp.int32)
    position = jnp.where(index < PROMPT, index, PROMPT + (index - PROMPT) % CONT).astype(f32)
    half = HD // 2
    frequency = jnp.exp(-math.log(10000.0) * jnp.arange(half, dtype=f32) / half)
    angles = position[:, None] * frequency[None, :]
    cosine, sine = jnp.cos(angles), jnp.sin(angles)
    return (
        jnp.concatenate([cosine, cosine], axis=1),
        jnp.concatenate([-sine, sine], axis=1),
    )


def after(*arrays):
    return lax.optimization_barrier(arrays)


def normalize_parts(values, gain):
    inverse = lax.rsqrt(jnp.mean(values * values, axis=-1, keepdims=True) + norm_eps)
    unit_rows = values * inverse
    return (unit_rows * gain, unit_rows, inverse)


def norm_backward(grad_outer, unit_rows, inverse, gain):
    grad_unit = grad_outer * gain
    grad_inner = inverse * (
        grad_unit - unit_rows * jnp.mean(grad_unit * unit_rows, axis=-1, keepdims=True)
    )
    return (grad_inner, jnp.sum(grad_outer * unit_rows, axis=0))


def shards(
    tokens,
    route_ids,
    gate_values,
    deal,
    norm1_gain,
    w_query,
    w_key,
    w_value,
    w_out,
    norm2_gain,
    w_gate,
    w_up,
    w_down,
    cotangent,
):
    rows = tokens.shape[1]
    ctx_count = lax.axis_size("ctx")
    fsdp_count = lax.axis_size("fsdp")
    group_len = rows * ctx_count
    capacity = 5 * rows * TOPK // (4 * EXPERTS)
    repeats = fsdp_count // EXPERTS
    pair = 2
    columns = repeats // pair
    core = lax.axis_index("ctx")
    expert = lax.axis_index("fsdp") // repeats
    width = D // ctx_count
    heads = HEADS // ctx_count

    def core_shift(a, s):
        return lax.ppermute(a, "ctx", [(i, (i + s) % ctx_count) for i in range(ctx_count)])

    def fsdp_shift(a, move):
        return lax.ppermute(a, "fsdp", [(i, move(i)) for i in range(fsdp_count)])

    def expert_shift(a, k):
        return fsdp_shift(a, lambda i: (i + k * repeats) % fsdp_count)

    def column_shift(a, j):
        def move(i):
            e, r = divmod(i, repeats)
            t, w = divmod(r, pair)
            return e * repeats + ((t + j) % columns) * pair + w

        return fsdp_shift(a, move)

    def pair_swap(a):
        return fsdp_shift(a, lambda i: i ^ 1)

    def core_gather(a):
        return jnp.concatenate([a] + [core_shift(a, s) for s in range(1, ctx_count)], axis=0)

    block_count = deal.shape[1]
    block = group_len // block_count
    local_blocks = block_count // ctx_count
    dealt = jnp.argsort(deal[0]).astype(jnp.int32)
    perm = ((core - dealt // local_blocks) % ctx_count) * local_blocks + dealt % local_blocks
    cos, sin = rope_tables(group_len)

    def own_columns(w):
        return lax.dynamic_slice_in_dim(w, core * width, width, axis=1)

    by_head = [own_columns(w).reshape(-1, heads, HD) for w in (w_query, w_key, w_value)]
    packed = jnp.concatenate(
        [jnp.stack(by_head, axis=2).reshape(-1, 3 * width), own_columns(w_out)], axis=1
    )
    packed = with_layout_constraint(packed, Layout(major_to_minor=(0, 1)))
    gathered = lax.all_gather(packed, "fsdp", axis=0, tiled=True)
    gathered = with_layout_constraint(gathered, Layout(major_to_minor=(0, 1)))

    halves = 2
    part_slots = capacity // halves
    half = EXPERTS * part_slots
    ids = route_ids[0]
    flat = ids.reshape(-1)
    onehot = (flat[:, None] == jnp.arange(EXPERTS, dtype=jnp.int32)[None, :]).astype(jnp.int32)
    earlier = jnp.cumsum(onehot, axis=0) - onehot
    slot = jnp.sum(earlier * onehot, axis=1)
    place = (slot // part_slots) * half + flat * part_slots + slot % part_slots
    place = jnp.where(slot < capacity, place, -1).reshape(rows, TOPK)
    targets = jnp.arange(halves * half, dtype=jnp.int32)
    select = [(place[:, k : k + 1] == targets[None, :]).astype(bf16) for k in range(TOPK)]
    spread = [(targets[:, None] == place[None, :, k]).astype(bf16) for k in range(TOPK)]
    gates = gate_values[0]

    dy = cotangent[0].astype(f32)
    grad_pairs = jnp.concatenate([(dy * gates[:, k : k + 1]).astype(bf16) for k in range(TOPK)])
    spread_both = jnp.concatenate(spread, axis=1)
    grad_blocks = [
        dot(spread_both[h * half : (h + 1) * half], grad_pairs, 1, 0, bf16) for h in range(halves)
    ]

    inputs = tokens[0].astype(f32)
    normed_f, _, _ = normalize_parts(inputs, norm1_gain)
    normed = core_gather(normed_f.astype(bf16))

    per = D // (ctx_count * fsdp_count)
    mine = lax.axis_index("fsdp")
    my_column, my_side = (mine % repeats) // pair, mine % pair

    index = jnp.arange(D, dtype=jnp.int32)
    source = (index // per % ctx_count) * (D // ctx_count)
    source = source + index // (per * ctx_count) * per + index % per
    shuffle = (index[:, None] == source[None, :]).astype(bf16)
    normed_mixed = dot(normed, shuffle, 1, 0, bf16)

    def weight_part(w):
        count = w.shape[0] // ctx_count
        return lax.dynamic_slice_in_dim(w, core * count, count, axis=0)

    weight_parts = [weight_part(w) for w in (w_gate, w_up, w_down)]
    gathered, normed_mixed, *tied = after(gathered, normed_mixed, *grad_blocks, *weight_parts)
    grad_blocks, weight_parts = tied[:halves], tied[halves:]
    out_columns = gathered[:, 3 * width :]
    full_qkv = gathered[:, : 3 * width]

    lines = [[r + e * repeats for e in range(EXPERTS)] for r in range(repeats)]

    def swap_experts(a, width=D):
        blocks = a.reshape(EXPERTS, -1, width)
        return lax.all_to_all(blocks, "fsdp", 0, 0, axis_index_groups=lines, tiled=True)

    def to_columns(a):
        return [a] + [column_shift(a, j) for j in range(1, columns)]

    grads_first = swap_experts(grad_blocks[0]).reshape(half, D)

    sides = [[i, i ^ 1] for i in range(0, fsdp_count, 2)]
    sides = [sorted(group) for group in sides]
    swapped = [
        lax.all_gather(part, "fsdp", axis=0, tiled=True, axis_index_groups=sides)
        for part in weight_parts
    ]

    starts = [(1 - my_side) * ctx_count + (core - s) % ctx_count for s in range(ctx_count)]

    def pair_weights(own, both):
        count = both.shape[0] // pair
        part = lax.dynamic_slice_in_dim(both, (1 - my_side) * count, count, axis=0)
        return join_weights(
            my_side, starts, own, [part] + [core_shift(part, s) for s in range(1, ctx_count)]
        )

    pre = dot(normed, full_qkv, 1, 0)
    context, q, k, v, log_total = attention_forward(perm, block, pre, cos, sin)

    def out_rows(c):
        return lax.dynamic_slice_in_dim(out_columns, (c % ctx_count) * width, width, axis=0)

    if ctx_count == 2:
        own_part, other = out_rows(core), core_shift(out_rows(core + 1), 1)
        w_o = jnp.concatenate(
            [jnp.where(core == 0, own_part, other), jnp.where(core == 0, other, own_part)], axis=1
        )
    else:
        w_o = lax.all_to_all(out_columns.reshape(ctx_count, width, width), "ctx", 0, 0)
        w_o = w_o.transpose(1, 0, 2).reshape(width, D)
    away = [dot(context[s * rows : (s + 1) * rows], w_o, 1, 0, bf16) for s in range(1, ctx_count)]
    attention = dot(context[:rows], w_o, 1, 0)
    for s in range(1, ctx_count):
        attention = attention + core_shift(away[s - 1], -s).astype(f32)
    hidden_in = inputs + attention
    normed_two_f, unit_two, inverse_two = normalize_parts(hidden_in, norm2_gain)
    normed_two = normed_two_f.astype(bf16)

    spread_any = spread[0] + spread[1]
    slot_blocks = [
        dot(spread_any[h * half : (h + 1) * half], normed_two, 1, 0, bf16) for h in range(halves)
    ]
    grads_first, waiting, _ = after(grads_first, grad_blocks[1], away[0])
    grads_second = swap_experts(waiting).reshape(half, D)
    grad_parts = to_columns(grads_first)
    got = after(grads_second, *slot_blocks, *swapped[:2], *grad_parts[1:])
    grads_second, slots_a, slots_b, *swapped_two = got[:5]
    grad_parts[1:] = got[5:]
    grad_parts += to_columns(grads_second)
    first = swap_experts(slots_a).reshape(half, D)
    wg, wu = (pair_weights(*w) for w in zip((w_gate, w_up), swapped_two))
    got = after(first, slots_b, swapped[2], wg, wu, *grad_parts[columns + 1 :])
    first, slots_b, swapped_down, wg, wu = got[:5]
    grad_parts[columns + 1 :] = got[5:]
    second = swap_experts(slots_b).reshape(half, D)
    wd = pair_weights(w_down, swapped_down)
    weights = (wg, wu, wd)
    parts = halves * columns

    def hidden_part(index, slots, state):
        *state, back = expert_hidden(index, parts, slots, grad_parts[index], weights, state)
        return state, back

    def columns_home(pieces):
        return [column_shift(part, -(j + 1)) for j, part in enumerate(pieces)]

    def add_parts(own, returned):
        total = own.astype(f32)
        for part in returned:
            total = total + part.astype(f32)
        return total.astype(bf16)

    slot_parts = to_columns(first)
    back, came = {}, [None] * halves
    state, back[0] = hidden_part(0, slot_parts[0], ())
    second, *got = after(second, *state, *slot_parts[1:])
    state, slot_parts[1:] = got[:3], got[3:]
    slot_parts += to_columns(second)
    for h in range(halves):
        for j in range(1, columns):
            index = h * columns + j
            state, back[index] = hidden_part(index, slot_parts[index], state)
            back[index], *state = after(back[index], *state)
        if h == 0:
            got = after(*state, *slot_parts[columns + 1 :])
            state, slot_parts[columns + 1 :] = got[:3], got[3:]
        came[h] = columns_home([back[h * columns + j] for j in range(1, columns)])
    home_first, *got = after(back[0], *state, *came[0])
    state = got[:3]
    home_first = add_parts(home_first, got[3:])
    home_first, *state = after(home_first, *state)
    home_first = swap_experts(home_first)
    state, back[columns] = hidden_part(columns, slot_parts[columns], state)
    back[columns], home_first, *state = after(back[columns], home_first, *state)
    hidden, grad_gate, grad_up = state
    all_slots = jnp.concatenate(slot_parts, axis=0)
    all_grads = jnp.concatenate(grad_parts, axis=0)

    def core_sum(part):
        total = lax.dynamic_slice_in_dim(part, core * width, width, axis=1).astype(f32)
        for s in range(1, ctx_count):
            start = ((core + s) % ctx_count) * width
            total = total + core_shift(
                lax.dynamic_slice_in_dim(part, start, width, axis=1), s
            ).astype(f32)
        return total.astype(bf16)

    def side_sum(total):
        return lax.psum_scatter(
            total, "fsdp", scatter_dimension=0, tiled=True, axis_index_groups=sides
        ).astype(f32)

    def out_rows_of(h, j, left):
        return expert_rows(h * columns + j, half, (left,), (wd,))

    home_second, hidden_t, *got = after(back[columns], hidden, *came[1])
    home_second = add_parts(home_second, got)
    home_second, hidden_t = after(home_second, hidden_t)
    home_second = swap_experts(home_second)
    down_part = dot(hidden_t, all_grads, 0, 0, bf16)
    down_part, hidden_t = after(down_part, hidden_t)
    away_first = [out_rows_of(0, j, hidden_t) for j in range(1, columns)]
    home_second, hidden_t, *away_first = after(home_second, hidden_t, *away_first)
    away_first = columns_home(away_first)
    down_total = core_sum(down_part)

    def side_swap_sum(total):
        def side_rows(i):
            size = total.shape[0] // pair
            return lax.dynamic_slice_in_dim(total, (i % pair) * size, size, axis=0)

        return side_rows(my_side), pair_swap(side_rows(my_side + 1))

    grad_slot_in = jnp.concatenate([home_first, home_second], axis=0).reshape(halves * half, D)

    grad_normed_two = dot(select[0] + select[1], grad_slot_in, 1, 0)
    grad_norm_two, norm2_part = norm_backward(grad_normed_two, unit_two, inverse_two, norm2_gain)
    grad_hidden_in = dy + grad_norm_two
    grad_attention = core_gather(grad_hidden_in.astype(bf16))
    def reduce_blocks(blocks, shift):
        total = blocks[0].astype(f32)
        for d in range(1, len(blocks)):
            total = total + shift(blocks[d].astype(bf16), d).astype(f32)
        return total.astype(bf16)

    def cut(a, n):
        size = a.shape[0] // n
        return [a[i * size : (i + 1) * size] for i in range(n)]

    def expert_sum(total):
        blocks = swap_experts(total, total.shape[1])
        return jnp.sum(blocks.reshape(EXPERTS, -1, total.shape[1]).astype(f32), axis=0)

    def row_blocks(a, n, own):
        split = a.reshape(EXPERTS, n, -1, a.shape[1])
        return [
            lax.dynamic_slice_in_dim(split, (own + d) % n, 1, axis=1).reshape(-1, a.shape[1])
            for d in range(n)
        ]

    out_part = dot(context, grad_attention, 0, 0, bf16)
    blocks_o = row_blocks(out_part, columns, my_column)
    got = after(grad_attention, down_total, *blocks_o)
    grad_attention, down_total, blocks_o = got[0], got[1], got[2:]
    down_grad = side_sum(down_total)
    came_o = [column_shift(block, d) for d, block in enumerate(blocks_o) if d]
    grad_context = dot(grad_attention, w_o, 1, 1, bf16)
    grad_qkv = attention_backward(
        perm, block, q, k, v, log_total, grad_context, cos, sin
    )
    qkv_part = dot(normed_mixed, grad_qkv, 0, 0, bf16)
    qkv_sum = lax.psum_scatter(qkv_part, "fsdp", scatter_dimension=0, tiled=True)

    got = after(qkv_part, grad_qkv, hidden_t, grad_gate, grad_up, *away_first)
    grad_qkv, hidden_t, gate_t, up_t, *away_first = got[1:]
    gate_part = dot(gate_t, all_slots, 0, 0, bf16)
    gate_part, hidden_t, *came_o = after(gate_part, hidden_t, *came_o)
    blocks_o = row_blocks(add_parts(blocks_o[0], came_o), pair, my_side)
    hidden_t, *blocks_o = after(hidden_t, *blocks_o)
    came_o = pair_swap(blocks_o[1])
    outs_first = add_parts(out_rows_of(0, 0, hidden_t), away_first)
    away_second = [out_rows_of(1, j, hidden_t) for j in range(1, columns)]
    gate_total = core_sum(gate_part)
    outs_first, gate_total, up_t, *away_second = after(outs_first, gate_total, up_t, *away_second)
    away_second = columns_home(away_second)
    outs_first = swap_experts(outs_first)
    gate_own, gate_came = side_swap_sum(gate_total)

    up_part = dot(up_t, all_slots, 0, 0, bf16)
    got = after(up_part, hidden_t, grad_qkv, outs_first, came_o, gate_came, *away_second)
    up_part, hidden_t, grad_qkv, outs_first, came_o, gate_came, *away_second = got
    out_grad = expert_sum(add_parts(blocks_o[0], [came_o]))
    outs_second = add_parts(out_rows_of(1, 0, hidden_t), away_second)
    up_total = core_sum(up_part)
    outs_second, up_total, grad_qkv, out_grad = after(outs_second, up_total, grad_qkv, out_grad)
    outs_second = swap_experts(outs_second)
    up_own, up_came = side_swap_sum(up_total)

    def back_rows(s, out):
        return dot(grad_qkv[s * rows : (s + 1) * rows], full_qkv, 1, 1, out)

    back_away = [back_rows(s, bf16) for s in range(1, ctx_count)]
    grad_normed = back_rows(0, f32)
    for s in range(1, ctx_count):
        grad_normed = grad_normed + core_shift(back_away[s - 1], -s).astype(f32)
    _, unit_one, inverse_one = normalize_parts(inputs, norm1_gain)
    grad_norm_one, norm1_part = norm_backward(grad_normed, unit_one, inverse_one, norm1_gain)
    tokens_grad = (grad_hidden_in + grad_norm_one).astype(bf16)
    tokens_grad, norm1_part, outs_second, qkv_sum = after(
        tokens_grad, norm1_part, outs_second, qkv_sum
    )
    gate_grad = gate_own.astype(f32) + gate_came.astype(f32)

    gains = jnp.stack([norm1_part, norm2_part]).reshape(2, ctx_count, fsdp_count, per)
    gains = lax.all_to_all(gains.transpose(2, 1, 0, 3), "fsdp", 0, 0, tiled=True)
    gains = jnp.sum(gains, axis=0)

    def gains_of(c):
        return lax.dynamic_index_in_dim(gains, c % ctx_count, 0, keepdims=False)

    gains_own = gains_of(core)
    for s in range(1, ctx_count):
        gains_own = gains_own + core_shift(gains_of(core + s), s)
    gains_own, up_own, up_came = after(gains_own, up_own, up_came)
    up_grad = up_own.astype(f32) + up_came.astype(f32)
    sums = qkv_sum.reshape(ctx_count, per, heads, 3, HD).astype(f32)
    sums = sums.transpose(3, 0, 1, 2, 4).reshape(3, ctx_count, per, width)

    def core_piece(c):
        return lax.dynamic_index_in_dim(sums, c % ctx_count, 1, keepdims=False)

    if ctx_count == 2:
        own_part, other = core_piece(core), core_shift(core_piece(core + 1), 1)
        qkv_own = jnp.concatenate(
            [jnp.where(core == 0, own_part, other), jnp.where(core == 0, other, own_part)], axis=2
        )
    else:
        qkv_own = lax.all_to_all(sums.astype(bf16), "ctx", 1, 1).astype(f32)
        qkv_own = qkv_own.transpose(0, 2, 1, 3).reshape(3, per, D)
    query_grad, key_grad, value_grad = qkv_own[0], qkv_own[1], qkv_own[2]

    slot_out = jnp.concatenate([outs_first, outs_second], axis=0).reshape(halves * half, D)
    mixed = hidden_in
    for i in range(TOPK):
        mixed = mixed + dot(select[i], slot_out, 1, 0) * gates[:, i : i + 1]

    return (
        mixed.astype(bf16)[None],
        tokens_grad[None],
        gains_own[0],
        query_grad,
        key_grad,
        value_grad,
        out_grad,
        gains_own[1],
        gate_grad,
        up_grad,
        down_grad,
    )


def solution(mesh):
    in_specs = (
        P("fsdp", "ctx", None),
        P("fsdp", "ctx", None),
        P("fsdp", "ctx", None),
        P("fsdp", None),
        P(),
        P("fsdp", None),
        P("fsdp", None),
        P("fsdp", None),
        P("fsdp", None),
        P(),
        P("fsdp", None),
        P("fsdp", None),
        P("fsdp", None),
        P("fsdp", "ctx", None),
    )
    out_specs = (
        P("fsdp", "ctx", None),
        P("fsdp", "ctx", None),
        P(("ctx", "fsdp")),
        P(("ctx", "fsdp"), None),
        P(("ctx", "fsdp"), None),
        P(("ctx", "fsdp"), None),
        P(("ctx", "fsdp"), None),
        P(("ctx", "fsdp")),
        P("fsdp", "ctx"),
        P("fsdp", "ctx"),
        P("fsdp", "ctx"),
    )
    return jax.shard_map(shards, mesh=mesh, in_specs=in_specs, out_specs=out_specs, check_vma=False)
```

```python
import functools
import math

import jax
import jax.numpy as jnp
from jax import lax
from jax.experimental import pallas as pl
from jax.experimental.layout import Layout, with_layout_constraint
from jax.experimental.pallas import tpu as pltpu
from jax.sharding import PartitionSpec as P

D = 2048
HEADS = 16
HD = 128
EXPERTS = 4
TOPK = 2
PROMPT = 512
CONT = 256
TILE = 256

norm_eps = 1e-05
scale = 1.0 / math.sqrt(HD)
bf16 = jnp.bfloat16
f32 = jnp.float32


def dot(a, b, ca, cb, out=f32):
    r = lax.dot_general(a, b, (((ca,), (cb,)), ((), ())), preferred_element_type=f32)
    return r.astype(out)


def tile_keys(t):
    prompt_tiles = PROMPT // TILE
    if t < prompt_tiles:
        return list(range(t + 1))
    per = CONT // TILE
    first = prompt_tiles + ((t - prompt_tiles) // per) * per
    return list(range(prompt_tiles)) + list(range(first, t + 1))


def load_tile(ref, perm, t, block, cols):
    per = TILE // block
    parts = [
        ref[pl.ds(pl.multiple_of(perm[t * per + i] * block, block), block), cols]
        for i in range(per)
    ]
    return parts[0] if per == 1 else jnp.concatenate(parts, axis=0)


def store_tile(ref, perm, t, block, cols, value):
    per = TILE // block
    for i in range(per):
        ref[pl.ds(pl.multiple_of(perm[t * per + i] * block, block), block), cols] = value[
            i * block : (i + 1) * block
        ]


def spread_keys(ref, tiles):
    runs, start = [], tiles[0]
    for a, b in zip(tiles, tiles[1:] + [None]):
        if b != a + 1:
            runs.append((start, a + 1))
            start = b
    parts = [ref[lo * TILE : hi * TILE, :] for lo, hi in runs]
    return parts[0] if len(parts) == 1 else jnp.concatenate(parts, axis=0)


def causal_fill(scores, value):
    width = scores.shape[1] - TILE
    row = lax.broadcasted_iota(jnp.int32, (TILE, TILE), 0)
    col = lax.broadcasted_iota(jnp.int32, (TILE, TILE), 1)
    last = jnp.where(col <= row, scores[:, width:], value)
    return last if width == 0 else jnp.concatenate([scores[:, :width], last], axis=1)


def forward_kernel(
    block, perm, pre_q, pre_k, pre_v, cos_ref, sin_ref, ctx_ref, q_ref, k_ref, v_ref, log_ref
):
    tiles = pre_q.shape[0] // TILE
    for t in range(tiles):
        rows = slice(t * TILE, (t + 1) * TILE)
        cos, sin = cos_ref[rows, :], sin_ref[rows, :]
        q = load_tile(pre_q, perm, t, block, slice(None))
        q_ref[rows, :] = (q * cos + pltpu.roll(q, HD // 2, 1) * sin).astype(bf16)
        k = load_tile(pre_k, perm, t, block, slice(None))
        k_ref[rows, :] = (k * cos + pltpu.roll(k, HD // 2, 1) * sin).astype(bf16)
        v_ref[rows, :] = load_tile(pre_v, perm, t, block, slice(None)).astype(bf16)
    for t in range(tiles):
        rows = slice(t * TILE, (t + 1) * TILE)
        seen = tile_keys(t)
        keys, values = spread_keys(k_ref, seen), spread_keys(v_ref, seen)
        scores = dot(q_ref[rows, :], keys, 1, 1) * scale
        scores = causal_fill(scores, -1e30)
        top = jnp.max(scores, axis=1, keepdims=True)
        expo = jnp.exp(scores - top)
        total = jnp.sum(expo, axis=1, keepdims=True)
        probs = (expo * (1.0 / total)).astype(bf16)
        context = dot(probs, values, 1, 0).astype(bf16)
        store_tile(ctx_ref, perm, t, block, slice(None), context)
        log_ref[rows, :] = jnp.broadcast_to(top + jnp.log(total), (TILE, HD))


def backward_kernel(
    block,
    perm,
    q_ref,
    k_ref,
    v_ref,
    log_ref,
    do_ref,
    cos_ref,
    sin_ref,
    out_ref,
    dk_ref,
    dv_ref,
):
    tiles = q_ref.shape[0] // TILE
    dk_ref[...] = jnp.zeros_like(dk_ref)
    dv_ref[...] = jnp.zeros_like(dv_ref)
    for t in range(tiles):
        rows = slice(t * TILE, (t + 1) * TILE)
        seen = tile_keys(t)
        keys, values = spread_keys(k_ref, seen), spread_keys(v_ref, seen)
        query = q_ref[rows, :]
        grad = load_tile(do_ref, perm, t, block, slice(None))
        scores = dot(query, keys, 1, 1) * scale
        soft = causal_fill(jnp.exp(scores - log_ref[rows, 0:1]), 0.0)
        grad_prob = dot(grad, values, 1, 1)
        delta = jnp.sum(grad_prob * soft, axis=1, keepdims=True)
        grad_scores = (soft * (grad_prob - delta)).astype(bf16)
        values_back = dot(soft.astype(bf16), grad, 0, 0)
        keys_back = dot(grad_scores, query, 0, 0)
        for i, s in enumerate(seen):
            part, own = slice(i * TILE, (i + 1) * TILE), slice(s * TILE, (s + 1) * TILE)
            dv_ref[own, :] += values_back[part]
            dk_ref[own, :] += keys_back[part]
        back = dot(grad_scores, keys, 1, 0) * scale
        cos, sin = cos_ref[rows, :], sin_ref[rows, :]
        back = back * cos - pltpu.roll(back, HD // 2, 1) * sin
        store_tile(out_ref, perm, t, block, slice(0, HD), back.astype(bf16))
    for t in range(tiles):
        rows = slice(t * TILE, (t + 1) * TILE)
        cos, sin = cos_ref[rows, :], sin_ref[rows, :]
        back = dk_ref[rows, :] * scale
        back = back * cos - pltpu.roll(back, HD // 2, 1) * sin
        store_tile(out_ref, perm, t, block, slice(HD, 2 * HD), back.astype(bf16))
        store_tile(out_ref, perm, t, block, slice(2 * HD, 3 * HD), dv_ref[rows, :].astype(bf16))


def attention_forward(perm, block, pre, cos, sin):
    rows, heads = pre.shape[0], pre.shape[1] // (3 * HD)
    per_head = pl.BlockSpec((rows, HD), lambda h, p: (0, h))
    table = pl.BlockSpec((rows, HD), lambda h, p: (0, 0))
    head_array = jax.ShapeDtypeStruct((rows, heads * HD), bf16)
    return pl.pallas_call(
        functools.partial(forward_kernel, block),
        grid_spec=pltpu.PrefetchScalarGridSpec(
            num_scalar_prefetch=1,
            grid=(heads,),
            in_specs=[
                pl.BlockSpec((rows, HD), lambda h, p: (0, 3 * h)),
                pl.BlockSpec((rows, HD), lambda h, p: (0, 3 * h + 1)),
                pl.BlockSpec((rows, HD), lambda h, p: (0, 3 * h + 2)),
                table,
                table,
            ],
            out_specs=[per_head] * 5,
        ),
        out_shape=[head_array] * 4 + [jax.ShapeDtypeStruct((rows, heads * HD), f32)],
        name="attention_forward",
    )(perm, pre, pre, pre, cos, sin)


def attention_backward(perm, block, q, k, v, log_total, grad, cos, sin):
    rows, heads = q.shape[0], q.shape[1] // HD
    per_head = pl.BlockSpec((rows, HD), lambda h, p: (0, h))
    table = pl.BlockSpec((rows, HD), lambda h, p: (0, 0))
    return pl.pallas_call(
        functools.partial(backward_kernel, block),
        grid_spec=pltpu.PrefetchScalarGridSpec(
            num_scalar_prefetch=1,
            grid=(heads,),
            in_specs=[per_head] * 5 + [table, table],
            out_specs=pl.BlockSpec((rows, 3 * HD), lambda h, p: (0, h)),
            scratch_shapes=[pltpu.VMEM((rows, HD), f32), pltpu.VMEM((rows, HD), f32)],
        ),
        out_shape=jax.ShapeDtypeStruct((rows, 3 * heads * HD), bf16),
        name="attention_backward",
    )(perm, q, k, v, log_total, grad, cos, sin)


def expert_kernel(kept, x_ref, g_ref, wg_ref, wu_ref, wd_ref, *refs):
    hidden_ref, gate_ref, up_ref, back_ref, total_ref = refs[kept:]
    count = x_ref.shape[0] // 2

    @pl.when(pl.program_id(0) == 0)
    def _():
        total_ref[...] = jnp.zeros_like(total_ref)

    both = jnp.concatenate([wg_ref[...], wu_ref[...]], axis=0)
    for p in range(2):
        rows = slice(p * count, (p + 1) * count)
        gate = dot(x_ref[rows, :], wg_ref[...], 1, 1)
        up = dot(x_ref[rows, :], wu_ref[...], 1, 1)
        grad = dot(g_ref[rows, :], wd_ref[...], 1, 1)
        sigmoid = jax.nn.sigmoid(gate)
        silu = gate * sigmoid
        hidden_ref[rows, :] = (silu * up).astype(bf16)
        grad_gate = (grad * up * sigmoid * (1.0 + gate * (1.0 - sigmoid))).astype(bf16)
        grad_up = (grad * silu).astype(bf16)
        gate_ref[rows, :] = grad_gate
        up_ref[rows, :] = grad_up
        total_ref[rows, :] += dot(jnp.concatenate([grad_gate, grad_up], axis=1), both, 1, 0)

    @pl.when(pl.program_id(0) == pl.num_programs(0) - 1)
    def _():
        back_ref[...] = total_ref[...].astype(bf16)


def expert_hidden(part, parts, slots, grads, weights, kept):
    rows, units = slots.shape[0], weights[0].shape[0]
    tile = 256 if units % 256 == 0 else 128
    whole = pl.BlockSpec((rows, D), lambda i: (0, 0))
    weight = pl.BlockSpec((tile, D), lambda i: (i, 0))
    result = pl.BlockSpec((rows, tile), lambda i: (part, i))
    return pl.pallas_call(
        functools.partial(expert_kernel, len(kept)),
        grid=(units // tile,),
        in_specs=[whole] * 2 + [weight] * 3 + [pl.BlockSpec(memory_space=pl.ANY)] * len(kept),
        out_specs=[result] * 3 + [whole],
        out_shape=[jax.ShapeDtypeStruct((parts * rows, units), bf16)] * 3
        + [jax.ShapeDtypeStruct((rows, D), bf16)],
        scratch_shapes=[pltpu.VMEM((rows, D), f32)],
        input_output_aliases={5 + i: i for i in range(len(kept))},
        name="expert_hidden",
    )(slots, grads, *weights, *kept)


def rows_kernel(count, *refs):
    total = dot(refs[0][...], refs[count][...], 1, 0)
    for i in range(1, count):
        total = total + dot(refs[i][...], refs[count + i][...], 1, 0)
    refs[-1][...] = total.astype(bf16)


def expert_rows(part, rows, left, right):
    units, tile = right[0].shape[0], 256
    return pl.pallas_call(
        functools.partial(rows_kernel, len(left)),
        grid=(D // tile,),
        in_specs=[pl.BlockSpec((rows, units), lambda n: (part, 0))] * len(left)
        + [pl.BlockSpec((units, tile), lambda n: (0, n))] * len(right),
        out_specs=pl.BlockSpec((rows, tile), lambda n: (0, n)),
        out_shape=jax.ShapeDtypeStruct((rows, D), bf16),
        name="expert_rows",
    )(*left, *right)


def join_kernel(own_blocks, part_blocks, where, own_ref, *refs):
    parts, out_ref = refs[:-1], refs[-1]
    i = pl.program_id(0)
    inside = i - where[0] * own_blocks

    @pl.when((inside >= 0) & (inside < own_blocks))
    def _():
        out_ref[...] = own_ref[...]

    for s, part in enumerate(parts):
        place = i - where[1 + s]

        @pl.when((place >= 0) & (place < part_blocks))
        def _(part=part):
            out_ref[...] = part[...]


def join_weights(side, starts, own, parts):
    size, count = own.shape[0], parts[0].shape[0]
    tile = count // 2 if count % 32 == 0 else count
    own_blocks, part_blocks = size // tile, count // tile
    where = jnp.stack([side] + [start * part_blocks for start in starts]).astype(jnp.int32)

    def part_spec(s):
        return pl.BlockSpec(
            (tile, D), lambda i, w: (jnp.clip(i - w[1 + s], 0, part_blocks - 1), 0)
        )

    return pl.pallas_call(
        functools.partial(join_kernel, own_blocks, part_blocks),
        grid_spec=pltpu.PrefetchScalarGridSpec(
            num_scalar_prefetch=1,
            grid=(2 * own_blocks,),
            in_specs=[
                pl.BlockSpec(
                    (tile, D),
                    lambda i, w: (jnp.clip(i - w[0] * own_blocks, 0, own_blocks - 1), 0),
                )
            ]
            + [part_spec(s) for s in range(len(parts))],
            out_specs=pl.BlockSpec((tile, D), lambda i, w: (i, 0)),
        ),
        out_shape=jax.ShapeDtypeStruct((2 * size, D), own.dtype),
        name="join_weights",
    )(where, own, *parts)


def rope_tables(group_len):
    index = jnp.arange(group_len, dtype=jnp.int32)
    position = jnp.where(index < PROMPT, index, PROMPT + (index - PROMPT) % CONT).astype(f32)
    half = HD // 2
    frequency = jnp.exp(-math.log(10000.0) * jnp.arange(half, dtype=f32) / half)
    angles = position[:, None] * frequency[None, :]
    cosine, sine = jnp.cos(angles), jnp.sin(angles)
    return (
        jnp.concatenate([cosine, cosine], axis=1),
        jnp.concatenate([-sine, sine], axis=1),
    )


def after(*arrays):
    return lax.optimization_barrier(arrays)


def normalize_parts(values, gain):
    inverse = lax.rsqrt(jnp.mean(values * values, axis=-1, keepdims=True) + norm_eps)
    unit_rows = values * inverse
    return (unit_rows * gain, unit_rows, inverse)


def norm_backward(grad_outer, unit_rows, inverse, gain):
    grad_unit = grad_outer * gain
    grad_inner = inverse * (
        grad_unit - unit_rows * jnp.mean(grad_unit * unit_rows, axis=-1, keepdims=True)
    )
    return (grad_inner, jnp.sum(grad_outer * unit_rows, axis=0))


def shards(
    tokens,
    route_ids,
    gate_values,
    deal,
    norm1_gain,
    w_query,
    w_key,
    w_value,
    w_out,
    norm2_gain,
    w_gate,
    w_up,
    w_down,
    cotangent,
):
    rows = tokens.shape[1]
    ctx_count = lax.axis_size("ctx")
    fsdp_count = lax.axis_size("fsdp")
    group_len = rows * ctx_count
    capacity = 5 * rows * TOPK // (4 * EXPERTS)
    repeats = fsdp_count // EXPERTS
    pair = 2
    columns = repeats // pair
    core = lax.axis_index("ctx")
    expert = lax.axis_index("fsdp") // repeats
    width = D // ctx_count
    heads = HEADS // ctx_count

    def core_shift(a, s):
        return lax.ppermute(a, "ctx", [(i, (i + s) % ctx_count) for i in range(ctx_count)])

    def fsdp_shift(a, move):
        return lax.ppermute(a, "fsdp", [(i, move(i)) for i in range(fsdp_count)])

    def expert_shift(a, k):
        return fsdp_shift(a, lambda i: (i + k * repeats) % fsdp_count)

    def column_shift(a, j):
        def move(i):
            e, r = divmod(i, repeats)
            t, w = divmod(r, pair)
            return e * repeats + ((t + j) % columns) * pair + w

        return fsdp_shift(a, move)

    def pair_swap(a):
        return fsdp_shift(a, lambda i: i ^ 1)

    def core_gather(a):
        return jnp.concatenate([a] + [core_shift(a, s) for s in range(1, ctx_count)], axis=0)

    block_count = deal.shape[1]
    block = group_len // block_count
    local_blocks = block_count // ctx_count
    dealt = jnp.argsort(deal[0]).astype(jnp.int32)
    perm = ((core - dealt // local_blocks) % ctx_count) * local_blocks + dealt % local_blocks
    cos, sin = rope_tables(group_len)

    def own_columns(w):
        return lax.dynamic_slice_in_dim(w, core * width, width, axis=1)

    by_head = [own_columns(w).reshape(-1, heads, HD) for w in (w_query, w_key, w_value)]
    packed = jnp.concatenate(
        [jnp.stack(by_head, axis=2).reshape(-1, 3 * width), own_columns(w_out)], axis=1
    )
    packed = with_layout_constraint(packed, Layout(major_to_minor=(0, 1)))
    gathered = lax.all_gather(packed, "fsdp", axis=0, tiled=True)
    gathered = with_layout_constraint(gathered, Layout(major_to_minor=(0, 1)))

    halves = 2
    part_slots = capacity // halves
    half = EXPERTS * part_slots
    ids = route_ids[0]
    flat = ids.reshape(-1)
    onehot = (flat[:, None] == jnp.arange(EXPERTS, dtype=jnp.int32)[None, :]).astype(jnp.int32)
    earlier = jnp.cumsum(onehot, axis=0) - onehot
    slot = jnp.sum(earlier * onehot, axis=1)
    place = (slot // part_slots) * half + flat * part_slots + slot % part_slots
    place = jnp.where(slot < capacity, place, -1).reshape(rows, TOPK)
    targets = jnp.arange(halves * half, dtype=jnp.int32)
    select = [(place[:, k : k + 1] == targets[None, :]).astype(bf16) for k in range(TOPK)]
    spread = [(targets[:, None] == place[None, :, k]).astype(bf16) for k in range(TOPK)]
    gates = gate_values[0]

    dy = cotangent[0].astype(f32)
    grad_pairs = jnp.concatenate([(dy * gates[:, k : k + 1]).astype(bf16) for k in range(TOPK)])
    spread_both = jnp.concatenate(spread, axis=1)
    grad_blocks = [
        dot(spread_both[h * half : (h + 1) * half], grad_pairs, 1, 0, bf16) for h in range(halves)
    ]

    inputs = tokens[0].astype(f32)
    normed_f, _, _ = normalize_parts(inputs, norm1_gain)
    normed = core_gather(normed_f.astype(bf16))

    per = D // (ctx_count * fsdp_count)
    mine = lax.axis_index("fsdp")
    my_column, my_side = (mine % repeats) // pair, mine % pair

    index = jnp.arange(D, dtype=jnp.int32)
    source = (index // per % ctx_count) * (D // ctx_count)
    source = source + index // (per * ctx_count) * per + index % per
    shuffle = (index[:, None] == source[None, :]).astype(bf16)
    normed_mixed = dot(normed, shuffle, 1, 0, bf16)

    def weight_part(w):
        count = w.shape[0] // ctx_count
        return lax.dynamic_slice_in_dim(w, core * count, count, axis=0)

    weight_parts = [weight_part(w) for w in (w_gate, w_up, w_down)]
    gathered, normed_mixed, *tied = after(gathered, normed_mixed, *grad_blocks, *weight_parts)
    grad_blocks, weight_parts = tied[:halves], tied[halves:]
    out_columns = gathered[:, 3 * width :]
    full_qkv = gathered[:, : 3 * width]

    lines = [[r + e * repeats for e in range(EXPERTS)] for r in range(repeats)]

    def swap_experts(a, width=D):
        blocks = a.reshape(EXPERTS, -1, width)
        return lax.all_to_all(blocks, "fsdp", 0, 0, axis_index_groups=lines, tiled=True)

    def to_columns(a):
        return [a] + [column_shift(a, j) for j in range(1, columns)]

    grads_first = swap_experts(grad_blocks[0]).reshape(half, D)

    sides = [[i, i ^ 1] for i in range(0, fsdp_count, 2)]
    sides = [sorted(group) for group in sides]
    swapped = [
        lax.all_gather(part, "fsdp", axis=0, tiled=True, axis_index_groups=sides)
        for part in weight_parts
    ]

    starts = [(1 - my_side) * ctx_count + (core - s) % ctx_count for s in range(ctx_count)]

    def pair_weights(own, both):
        count = both.shape[0] // pair
        part = lax.dynamic_slice_in_dim(both, (1 - my_side) * count, count, axis=0)
        return join_weights(
            my_side, starts, own, [part] + [core_shift(part, s) for s in range(1, ctx_count)]
        )

    pre = dot(normed, full_qkv, 1, 0)
    context, q, k, v, log_total = attention_forward(perm, block, pre, cos, sin)

    def out_rows(c):
        return lax.dynamic_slice_in_dim(out_columns, (c % ctx_count) * width, width, axis=0)

    if ctx_count == 2:
        own_part, other = out_rows(core), core_shift(out_rows(core + 1), 1)
        w_o = jnp.concatenate(
            [jnp.where(core == 0, own_part, other), jnp.where(core == 0, other, own_part)], axis=1
        )
    else:
        w_o = lax.all_to_all(out_columns.reshape(ctx_count, width, width), "ctx", 0, 0)
        w_o = w_o.transpose(1, 0, 2).reshape(width, D)
    away = [dot(context[s * rows : (s + 1) * rows], w_o, 1, 0, bf16) for s in range(1, ctx_count)]
    attention = dot(context[:rows], w_o, 1, 0)
    for s in range(1, ctx_count):
        attention = attention + core_shift(away[s - 1], -s).astype(f32)
    hidden_in = inputs + attention
    normed_two_f, unit_two, inverse_two = normalize_parts(hidden_in, norm2_gain)
    normed_two = normed_two_f.astype(bf16)

    spread_any = spread[0] + spread[1]
    slot_blocks = [
        dot(spread_any[h * half : (h + 1) * half], normed_two, 1, 0, bf16) for h in range(halves)
    ]
    grads_first, waiting, _ = after(grads_first, grad_blocks[1], away[0])
    grads_second = swap_experts(waiting).reshape(half, D)
    grad_parts = to_columns(grads_first)
    got = after(grads_second, *slot_blocks, *swapped[:2], *grad_parts[1:])
    grads_second, slots_a, slots_b, *swapped_two = got[:5]
    grad_parts[1:] = got[5:]
    grad_parts += to_columns(grads_second)
    first = swap_experts(slots_a).reshape(half, D)
    wg, wu = (pair_weights(*w) for w in zip((w_gate, w_up), swapped_two))
    got = after(first, slots_b, swapped[2], wg, wu, *grad_parts[columns + 1 :])
    first, slots_b, swapped_down, wg, wu = got[:5]
    grad_parts[columns + 1 :] = got[5:]
    second = swap_experts(slots_b).reshape(half, D)
    wd = pair_weights(w_down, swapped_down)
    weights = (wg, wu, wd)
    parts = halves * columns

    def hidden_part(index, slots, state):
        *state, back = expert_hidden(index, parts, slots, grad_parts[index], weights, state)
        return state, back

    def columns_home(pieces):
        return [column_shift(part, -(j + 1)) for j, part in enumerate(pieces)]

    def add_parts(own, returned):
        total = own.astype(f32)
        for part in returned:
            total = total + part.astype(f32)
        return total.astype(bf16)

    slot_parts = to_columns(first)
    back, came = {}, [None] * halves
    state, back[0] = hidden_part(0, slot_parts[0], ())
    second, *got = after(second, *state, *slot_parts[1:])
    state, slot_parts[1:] = got[:3], got[3:]
    slot_parts += to_columns(second)
    for h in range(halves):
        for j in range(1, columns):
            index = h * columns + j
            state, back[index] = hidden_part(index, slot_parts[index], state)
            back[index], *state = after(back[index], *state)
        if h == 0:
            got = after(*state, *slot_parts[columns + 1 :])
            state, slot_parts[columns + 1 :] = got[:3], got[3:]
        came[h] = columns_home([back[h * columns + j] for j in range(1, columns)])
    home_first, *got = after(back[0], *state, *came[0])
    state = got[:3]
    home_first = add_parts(home_first, got[3:])
    home_first, *state = after(home_first, *state)
    home_first = swap_experts(home_first)
    state, back[columns] = hidden_part(columns, slot_parts[columns], state)
    back[columns], home_first, *state = after(back[columns], home_first, *state)
    hidden, grad_gate, grad_up = state
    all_slots = jnp.concatenate(slot_parts, axis=0)
    all_grads = jnp.concatenate(grad_parts, axis=0)

    def core_sum(part):
        total = lax.dynamic_slice_in_dim(part, core * width, width, axis=1).astype(f32)
        for s in range(1, ctx_count):
            start = ((core + s) % ctx_count) * width
            total = total + core_shift(
                lax.dynamic_slice_in_dim(part, start, width, axis=1), s
            ).astype(f32)
        return total.astype(bf16)

    def side_sum(total):
        return lax.psum_scatter(
            total, "fsdp", scatter_dimension=0, tiled=True, axis_index_groups=sides
        ).astype(f32)

    def out_rows_of(h, j, left):
        return expert_rows(h * columns + j, half, (left,), (wd,))

    home_second, hidden_t, *got = after(back[columns], hidden, *came[1])
    home_second = add_parts(home_second, got)
    home_second, hidden_t = after(home_second, hidden_t)
    home_second = swap_experts(home_second)
    down_part = dot(hidden_t, all_grads, 0, 0, bf16)
    down_part, hidden_t = after(down_part, hidden_t)
    away_first = [out_rows_of(0, j, hidden_t) for j in range(1, columns)]
    home_second, hidden_t, *away_first = after(home_second, hidden_t, *away_first)
    away_first = columns_home(away_first)
    down_total = core_sum(down_part)

    def side_swap_sum(total):
        def side_rows(i):
            size = total.shape[0] // pair
            return lax.dynamic_slice_in_dim(total, (i % pair) * size, size, axis=0)

        return side_rows(my_side), pair_swap(side_rows(my_side + 1))

    grad_slot_in = jnp.concatenate([home_first, home_second], axis=0).reshape(halves * half, D)

    grad_normed_two = dot(select[0] + select[1], grad_slot_in, 1, 0)
    grad_norm_two, norm2_part = norm_backward(grad_normed_two, unit_two, inverse_two, norm2_gain)
    grad_hidden_in = dy + grad_norm_two
    grad_attention = core_gather(grad_hidden_in.astype(bf16))
    def reduce_blocks(blocks, shift):
        total = blocks[0].astype(f32)
        for d in range(1, len(blocks)):
            total = total + shift(blocks[d].astype(bf16), d).astype(f32)
        return total.astype(bf16)

    def cut(a, n):
        size = a.shape[0] // n
        return [a[i * size : (i + 1) * size] for i in range(n)]

    def expert_sum(total):
        blocks = swap_experts(total, total.shape[1])
        return jnp.sum(blocks.reshape(EXPERTS, -1, total.shape[1]).astype(f32), axis=0)

    def row_blocks(a, n, own):
        split = a.reshape(EXPERTS, n, -1, a.shape[1])
        return [
            lax.dynamic_slice_in_dim(split, (own + d) % n, 1, axis=1).reshape(-1, a.shape[1])
            for d in range(n)
        ]

    out_part = dot(context, grad_attention, 0, 0, bf16)
    blocks_o = row_blocks(out_part, columns, my_column)
    got = after(grad_attention, down_total, *blocks_o)
    grad_attention, down_total, blocks_o = got[0], got[1], got[2:]
    down_grad = side_sum(down_total)
    came_o = [column_shift(block, d) for d, block in enumerate(blocks_o) if d]
    grad_context = dot(grad_attention, w_o, 1, 1, bf16)
    grad_qkv = attention_backward(
        perm, block, q, k, v, log_total, grad_context, cos, sin
    )
    qkv_part = dot(normed_mixed, grad_qkv, 0, 0, bf16)
    qkv_sum = lax.psum_scatter(qkv_part, "fsdp", scatter_dimension=0, tiled=True)

    got = after(qkv_part, grad_qkv, hidden_t, grad_gate, grad_up, *away_first)
    grad_qkv, hidden_t, gate_t, up_t, *away_first = got[1:]
    gate_part = dot(gate_t, all_slots, 0, 0, bf16)
    gate_part, hidden_t, *came_o = after(gate_part, hidden_t, *came_o)
    blocks_o = row_blocks(add_parts(blocks_o[0], came_o), pair, my_side)
    hidden_t, *blocks_o = after(hidden_t, *blocks_o)
    came_o = pair_swap(blocks_o[1])
    outs_first = add_parts(out_rows_of(0, 0, hidden_t), away_first)
    away_second = [out_rows_of(1, j, hidden_t) for j in range(1, columns)]
    gate_total = core_sum(gate_part)
    outs_first, gate_total, up_t, *away_second = after(outs_first, gate_total, up_t, *away_second)
    away_second = columns_home(away_second)
    outs_first = swap_experts(outs_first)
    gate_own, gate_came = side_swap_sum(gate_total)

    up_part = dot(up_t, all_slots, 0, 0, bf16)
    got = after(up_part, hidden_t, grad_qkv, outs_first, came_o, gate_came, *away_second)
    up_part, hidden_t, grad_qkv, outs_first, came_o, gate_came, *away_second = got
    out_grad = expert_sum(add_parts(blocks_o[0], [came_o]))
    outs_second = add_parts(out_rows_of(1, 0, hidden_t), away_second)
    outs_second, up_part, grad_qkv, out_grad = after(outs_second, up_part, grad_qkv, out_grad)
    outs_second = swap_experts(outs_second)
    up_own, up_came = side_swap_sum(core_sum(up_part))

    def back_rows(s, out):
        return dot(grad_qkv[s * rows : (s + 1) * rows], full_qkv, 1, 1, out)

    back_away = [back_rows(s, bf16) for s in range(1, ctx_count)]
    grad_normed = back_rows(0, f32)
    for s in range(1, ctx_count):
        grad_normed = grad_normed + core_shift(back_away[s - 1], -s).astype(f32)
    _, unit_one, inverse_one = normalize_parts(inputs, norm1_gain)
    grad_norm_one, norm1_part = norm_backward(grad_normed, unit_one, inverse_one, norm1_gain)
    tokens_grad = (grad_hidden_in + grad_norm_one).astype(bf16)
    tokens_grad, norm1_part, outs_second, qkv_sum = after(
        tokens_grad, norm1_part, outs_second, qkv_sum
    )
    gate_grad = gate_own.astype(f32) + gate_came.astype(f32)

    gains = jnp.stack([norm1_part, norm2_part]).reshape(2, ctx_count, fsdp_count, per)
    gains = lax.all_to_all(gains.transpose(2, 1, 0, 3), "fsdp", 0, 0, tiled=True)
    gains = jnp.sum(gains, axis=0)

    def gains_of(c):
        return lax.dynamic_index_in_dim(gains, c % ctx_count, 0, keepdims=False)

    gains_own = gains_of(core)
    for s in range(1, ctx_count):
        gains_own = gains_own + core_shift(gains_of(core + s), s)
    gains_own, up_own, up_came = after(gains_own, up_own, up_came)
    up_grad = up_own.astype(f32) + up_came.astype(f32)
    sums = qkv_sum.reshape(ctx_count, per, heads, 3, HD).astype(f32)
    sums = sums.transpose(3, 0, 1, 2, 4).reshape(3, ctx_count, per, width)

    def core_piece(c):
        return lax.dynamic_index_in_dim(sums, c % ctx_count, 1, keepdims=False)

    if ctx_count == 2:
        own_part, other = core_piece(core), core_shift(core_piece(core + 1), 1)
        qkv_own = jnp.concatenate(
            [jnp.where(core == 0, own_part, other), jnp.where(core == 0, other, own_part)], axis=2
        )
    else:
        qkv_own = lax.all_to_all(sums.astype(bf16), "ctx", 1, 1).astype(f32)
        qkv_own = qkv_own.transpose(0, 2, 1, 3).reshape(3, per, D)
    query_grad, key_grad, value_grad = qkv_own[0], qkv_own[1], qkv_own[2]

    slot_out = jnp.concatenate([outs_first, outs_second], axis=0).reshape(halves * half, D)
    mixed = hidden_in
    for i in range(TOPK):
        mixed = mixed + dot(select[i], slot_out, 1, 0) * gates[:, i : i + 1]

    return (
        mixed.astype(bf16)[None],
        tokens_grad[None],
        gains_own[0],
        query_grad,
        key_grad,
        value_grad,
        out_grad,
        gains_own[1],
        gate_grad,
        up_grad,
        down_grad,
    )


def solution(mesh):
    in_specs = (
        P("fsdp", "ctx", None),
        P("fsdp", "ctx", None),
        P("fsdp", "ctx", None),
        P("fsdp", None),
        P(),
        P("fsdp", None),
        P("fsdp", None),
        P("fsdp", None),
        P("fsdp", None),
        P(),
        P("fsdp", None),
        P("fsdp", None),
        P("fsdp", None),
        P("fsdp", "ctx", None),
    )
    out_specs = (
        P("fsdp", "ctx", None),
        P("fsdp", "ctx", None),
        P(("ctx", "fsdp")),
        P(("ctx", "fsdp"), None),
        P(("ctx", "fsdp"), None),
        P(("ctx", "fsdp"), None),
        P(("ctx", "fsdp"), None),
        P(("ctx", "fsdp")),
        P("fsdp", "ctx"),
        P("fsdp", "ctx"),
        P("fsdp", "ctx"),
    )
    return jax.shard_map(shards, mesh=mesh, in_specs=in_specs, out_specs=out_specs, check_vma=False)
```

```python
import functools
import math

import jax
import jax.numpy as jnp
from jax import lax
from jax.experimental import pallas as pl
from jax.experimental.layout import Layout, with_layout_constraint
from jax.experimental.pallas import tpu as pltpu
from jax.sharding import PartitionSpec as P

D = 2048
HEADS = 16
HD = 128
EXPERTS = 4
TOPK = 2
PROMPT = 512
CONT = 256
TILE = 256

norm_eps = 1e-05
scale = 1.0 / math.sqrt(HD)
bf16 = jnp.bfloat16
f32 = jnp.float32


def dot(a, b, ca, cb, out=f32):
    r = lax.dot_general(a, b, (((ca,), (cb,)), ((), ())), preferred_element_type=f32)
    return r.astype(out)


def tile_keys(t):
    prompt_tiles = PROMPT // TILE
    if t < prompt_tiles:
        return list(range(t + 1))
    per = CONT // TILE
    first = prompt_tiles + ((t - prompt_tiles) // per) * per
    return list(range(prompt_tiles)) + list(range(first, t + 1))


def load_tile(ref, perm, t, block, cols):
    per = TILE // block
    parts = [
        ref[pl.ds(pl.multiple_of(perm[t * per + i] * block, block), block), cols]
        for i in range(per)
    ]
    return parts[0] if per == 1 else jnp.concatenate(parts, axis=0)


def store_tile(ref, perm, t, block, cols, value):
    per = TILE // block
    for i in range(per):
        ref[pl.ds(pl.multiple_of(perm[t * per + i] * block, block), block), cols] = value[
            i * block : (i + 1) * block
        ]


def spread_keys(ref, tiles):
    runs, start = [], tiles[0]
    for a, b in zip(tiles, tiles[1:] + [None]):
        if b != a + 1:
            runs.append((start, a + 1))
            start = b
    parts = [ref[lo * TILE : hi * TILE, :] for lo, hi in runs]
    return parts[0] if len(parts) == 1 else jnp.concatenate(parts, axis=0)


def causal_fill(scores, value):
    width = scores.shape[1] - TILE
    row = lax.broadcasted_iota(jnp.int32, (TILE, TILE), 0)
    col = lax.broadcasted_iota(jnp.int32, (TILE, TILE), 1)
    last = jnp.where(col <= row, scores[:, width:], value)
    return last if width == 0 else jnp.concatenate([scores[:, :width], last], axis=1)


def forward_kernel(
    block, perm, pre_q, pre_k, pre_v, cos_ref, sin_ref, ctx_ref, q_ref, k_ref, v_ref, log_ref
):
    tiles = pre_q.shape[0] // TILE
    for t in range(tiles):
        rows = slice(t * TILE, (t + 1) * TILE)
        cos, sin = cos_ref[rows, :], sin_ref[rows, :]
        q = load_tile(pre_q, perm, t, block, slice(None))
        q_ref[rows, :] = (q * cos + pltpu.roll(q, HD // 2, 1) * sin).astype(bf16)
        k = load_tile(pre_k, perm, t, block, slice(None))
        k_ref[rows, :] = (k * cos + pltpu.roll(k, HD // 2, 1) * sin).astype(bf16)
        v_ref[rows, :] = load_tile(pre_v, perm, t, block, slice(None)).astype(bf16)
    for t in range(tiles):
        rows = slice(t * TILE, (t + 1) * TILE)
        seen = tile_keys(t)
        keys, values = spread_keys(k_ref, seen), spread_keys(v_ref, seen)
        scores = dot(q_ref[rows, :], keys, 1, 1) * scale
        scores = causal_fill(scores, -1e30)
        top = jnp.max(scores, axis=1, keepdims=True)
        expo = jnp.exp(scores - top)
        total = jnp.sum(expo, axis=1, keepdims=True)
        probs = (expo * (1.0 / total)).astype(bf16)
        context = dot(probs, values, 1, 0).astype(bf16)
        store_tile(ctx_ref, perm, t, block, slice(None), context)
        log_ref[rows, :] = jnp.broadcast_to(top + jnp.log(total), (TILE, HD))


def backward_kernel(
    block,
    perm,
    q_ref,
    k_ref,
    v_ref,
    log_ref,
    do_ref,
    cos_ref,
    sin_ref,
    out_ref,
    dk_ref,
    dv_ref,
):
    tiles = q_ref.shape[0] // TILE
    dk_ref[...] = jnp.zeros_like(dk_ref)
    dv_ref[...] = jnp.zeros_like(dv_ref)
    for t in range(tiles):
        rows = slice(t * TILE, (t + 1) * TILE)
        seen = tile_keys(t)
        keys, values = spread_keys(k_ref, seen), spread_keys(v_ref, seen)
        query = q_ref[rows, :]
        grad = load_tile(do_ref, perm, t, block, slice(None))
        scores = dot(query, keys, 1, 1) * scale
        soft = causal_fill(jnp.exp(scores - log_ref[rows, 0:1]), 0.0)
        grad_prob = dot(grad, values, 1, 1)
        delta = jnp.sum(grad_prob * soft, axis=1, keepdims=True)
        grad_scores = (soft * (grad_prob - delta)).astype(bf16)
        values_back = dot(soft.astype(bf16), grad, 0, 0)
        keys_back = dot(grad_scores, query, 0, 0)
        for i, s in enumerate(seen):
            part, own = slice(i * TILE, (i + 1) * TILE), slice(s * TILE, (s + 1) * TILE)
            dv_ref[own, :] += values_back[part]
            dk_ref[own, :] += keys_back[part]
        back = dot(grad_scores, keys, 1, 0) * scale
        cos, sin = cos_ref[rows, :], sin_ref[rows, :]
        back = back * cos - pltpu.roll(back, HD // 2, 1) * sin
        store_tile(out_ref, perm, t, block, slice(0, HD), back.astype(bf16))
    for t in range(tiles):
        rows = slice(t * TILE, (t + 1) * TILE)
        cos, sin = cos_ref[rows, :], sin_ref[rows, :]
        back = dk_ref[rows, :] * scale
        back = back * cos - pltpu.roll(back, HD // 2, 1) * sin
        store_tile(out_ref, perm, t, block, slice(HD, 2 * HD), back.astype(bf16))
        store_tile(out_ref, perm, t, block, slice(2 * HD, 3 * HD), dv_ref[rows, :].astype(bf16))


def attention_forward(perm, block, pre, cos, sin):
    rows, heads = pre.shape[0], pre.shape[1] // (3 * HD)
    per_head = pl.BlockSpec((rows, HD), lambda h, p: (0, h))
    table = pl.BlockSpec((rows, HD), lambda h, p: (0, 0))
    head_array = jax.ShapeDtypeStruct((rows, heads * HD), bf16)
    return pl.pallas_call(
        functools.partial(forward_kernel, block),
        grid_spec=pltpu.PrefetchScalarGridSpec(
            num_scalar_prefetch=1,
            grid=(heads,),
            in_specs=[
                pl.BlockSpec((rows, HD), lambda h, p: (0, 3 * h)),
                pl.BlockSpec((rows, HD), lambda h, p: (0, 3 * h + 1)),
                pl.BlockSpec((rows, HD), lambda h, p: (0, 3 * h + 2)),
                table,
                table,
            ],
            out_specs=[per_head] * 5,
        ),
        out_shape=[head_array] * 4 + [jax.ShapeDtypeStruct((rows, heads * HD), f32)],
        name="attention_forward",
    )(perm, pre, pre, pre, cos, sin)


def attention_backward(perm, block, q, k, v, log_total, grad, cos, sin):
    rows, heads = q.shape[0], q.shape[1] // HD
    per_head = pl.BlockSpec((rows, HD), lambda h, p: (0, h))
    table = pl.BlockSpec((rows, HD), lambda h, p: (0, 0))
    return pl.pallas_call(
        functools.partial(backward_kernel, block),
        grid_spec=pltpu.PrefetchScalarGridSpec(
            num_scalar_prefetch=1,
            grid=(heads,),
            in_specs=[per_head] * 5 + [table, table],
            out_specs=pl.BlockSpec((rows, 3 * HD), lambda h, p: (0, h)),
            scratch_shapes=[pltpu.VMEM((rows, HD), f32), pltpu.VMEM((rows, HD), f32)],
        ),
        out_shape=jax.ShapeDtypeStruct((rows, 3 * heads * HD), bf16),
        name="attention_backward",
    )(perm, q, k, v, log_total, grad, cos, sin)


def expert_kernel(kept, x_ref, g_ref, wg_ref, wu_ref, wd_ref, *refs):
    hidden_ref, gate_ref, up_ref = refs[kept:]
    count = x_ref.shape[0] // 2
    for p in range(2):
        rows = slice(p * count, (p + 1) * count)
        gate = dot(x_ref[rows, :], wg_ref[...], 1, 1)
        up = dot(x_ref[rows, :], wu_ref[...], 1, 1)
        grad = dot(g_ref[rows, :], wd_ref[...], 1, 1)
        sigmoid = jax.nn.sigmoid(gate)
        silu = gate * sigmoid
        hidden_ref[rows, :] = (silu * up).astype(bf16)
        gate_ref[rows, :] = (grad * up * sigmoid * (1.0 + gate * (1.0 - sigmoid))).astype(bf16)
        up_ref[rows, :] = (grad * silu).astype(bf16)


def expert_hidden(part, parts, slots, grads, weights, kept):
    rows, units = slots.shape[0], weights[0].shape[0]
    tile = 256 if units % 256 == 0 else 128
    whole = pl.BlockSpec((rows, D), lambda i: (0, 0))
    weight = pl.BlockSpec((tile, D), lambda i: (i, 0))
    result = pl.BlockSpec((rows, tile), lambda i: (part, i))
    return pl.pallas_call(
        functools.partial(expert_kernel, len(kept)),
        grid=(units // tile,),
        in_specs=[whole] * 2 + [weight] * 3 + [pl.BlockSpec(memory_space=pl.ANY)] * len(kept),
        out_specs=[result] * 3,
        out_shape=[jax.ShapeDtypeStruct((parts * rows, units), bf16)] * 3,
        input_output_aliases={5 + i: i for i in range(len(kept))},
        name="expert_hidden",
    )(slots, grads, *weights, *kept)


def rows_kernel(count, *refs):
    total = dot(refs[0][...], refs[count][...], 1, 0)
    for i in range(1, count):
        total = total + dot(refs[i][...], refs[count + i][...], 1, 0)
    refs[-1][...] = total.astype(bf16)


def expert_rows(part, rows, left, right):
    units, tile = right[0].shape[0], 256
    return pl.pallas_call(
        functools.partial(rows_kernel, len(left)),
        grid=(D // tile,),
        in_specs=[pl.BlockSpec((rows, units), lambda n: (part, 0))] * len(left)
        + [pl.BlockSpec((units, tile), lambda n: (0, n))] * len(right),
        out_specs=pl.BlockSpec((rows, tile), lambda n: (0, n)),
        out_shape=jax.ShapeDtypeStruct((rows, D), bf16),
        name="expert_rows",
    )(*left, *right)


def join_kernel(own_blocks, part_blocks, where, own_ref, *refs):
    parts, out_ref = refs[:-1], refs[-1]
    i = pl.program_id(0)
    inside = i - where[0] * own_blocks

    @pl.when((inside >= 0) & (inside < own_blocks))
    def _():
        out_ref[...] = own_ref[...]

    for s, part in enumerate(parts):
        place = i - where[1 + s]

        @pl.when((place >= 0) & (place < part_blocks))
        def _(part=part):
            out_ref[...] = part[...]


def join_weights(side, starts, own, parts):
    size, count = own.shape[0], parts[0].shape[0]
    tile = count // 2 if count % 32 == 0 else count
    own_blocks, part_blocks = size // tile, count // tile
    where = jnp.stack([side] + [start * part_blocks for start in starts]).astype(jnp.int32)

    def part_spec(s):
        return pl.BlockSpec(
            (tile, D), lambda i, w: (jnp.clip(i - w[1 + s], 0, part_blocks - 1), 0)
        )

    return pl.pallas_call(
        functools.partial(join_kernel, own_blocks, part_blocks),
        grid_spec=pltpu.PrefetchScalarGridSpec(
            num_scalar_prefetch=1,
            grid=(2 * own_blocks,),
            in_specs=[
                pl.BlockSpec(
                    (tile, D),
                    lambda i, w: (jnp.clip(i - w[0] * own_blocks, 0, own_blocks - 1), 0),
                )
            ]
            + [part_spec(s) for s in range(len(parts))],
            out_specs=pl.BlockSpec((tile, D), lambda i, w: (i, 0)),
        ),
        out_shape=jax.ShapeDtypeStruct((2 * size, D), own.dtype),
        name="join_weights",
    )(where, own, *parts)


def rope_tables(group_len):
    index = jnp.arange(group_len, dtype=jnp.int32)
    position = jnp.where(index < PROMPT, index, PROMPT + (index - PROMPT) % CONT).astype(f32)
    half = HD // 2
    frequency = jnp.exp(-math.log(10000.0) * jnp.arange(half, dtype=f32) / half)
    angles = position[:, None] * frequency[None, :]
    cosine, sine = jnp.cos(angles), jnp.sin(angles)
    return (
        jnp.concatenate([cosine, cosine], axis=1),
        jnp.concatenate([-sine, sine], axis=1),
    )


def after(*arrays):
    return lax.optimization_barrier(arrays)


def normalize_parts(values, gain):
    inverse = lax.rsqrt(jnp.mean(values * values, axis=-1, keepdims=True) + norm_eps)
    unit_rows = values * inverse
    return (unit_rows * gain, unit_rows, inverse)


def norm_backward(grad_outer, unit_rows, inverse, gain):
    grad_unit = grad_outer * gain
    grad_inner = inverse * (
        grad_unit - unit_rows * jnp.mean(grad_unit * unit_rows, axis=-1, keepdims=True)
    )
    return (grad_inner, jnp.sum(grad_outer * unit_rows, axis=0))


def shards(
    tokens,
    route_ids,
    gate_values,
    deal,
    norm1_gain,
    w_query,
    w_key,
    w_value,
    w_out,
    norm2_gain,
    w_gate,
    w_up,
    w_down,
    cotangent,
):
    rows = tokens.shape[1]
    ctx_count = lax.axis_size("ctx")
    fsdp_count = lax.axis_size("fsdp")
    group_len = rows * ctx_count
    capacity = 5 * rows * TOPK // (4 * EXPERTS)
    repeats = fsdp_count // EXPERTS
    pair = 2
    columns = repeats // pair
    core = lax.axis_index("ctx")
    expert = lax.axis_index("fsdp") // repeats
    width = D // ctx_count
    heads = HEADS // ctx_count

    def core_shift(a, s):
        return lax.ppermute(a, "ctx", [(i, (i + s) % ctx_count) for i in range(ctx_count)])

    def fsdp_shift(a, move):
        return lax.ppermute(a, "fsdp", [(i, move(i)) for i in range(fsdp_count)])

    def expert_shift(a, k):
        return fsdp_shift(a, lambda i: (i + k * repeats) % fsdp_count)

    def column_shift(a, j):
        def move(i):
            e, r = divmod(i, repeats)
            t, w = divmod(r, pair)
            return e * repeats + ((t + j) % columns) * pair + w

        return fsdp_shift(a, move)

    def pair_swap(a):
        return fsdp_shift(a, lambda i: i ^ 1)

    def core_gather(a):
        return jnp.concatenate([a] + [core_shift(a, s) for s in range(1, ctx_count)], axis=0)

    block_count = deal.shape[1]
    block = group_len // block_count
    local_blocks = block_count // ctx_count
    dealt = jnp.argsort(deal[0]).astype(jnp.int32)
    perm = ((core - dealt // local_blocks) % ctx_count) * local_blocks + dealt % local_blocks
    cos, sin = rope_tables(group_len)

    def own_columns(w):
        return lax.dynamic_slice_in_dim(w, core * width, width, axis=1)

    by_head = [own_columns(w).reshape(-1, heads, HD) for w in (w_query, w_key, w_value)]
    packed = jnp.concatenate(
        [jnp.stack(by_head, axis=2).reshape(-1, 3 * width), own_columns(w_out)], axis=1
    )
    packed = with_layout_constraint(packed, Layout(major_to_minor=(0, 1)))
    gathered = lax.all_gather(packed, "fsdp", axis=0, tiled=True)
    gathered = with_layout_constraint(gathered, Layout(major_to_minor=(0, 1)))

    halves = 2
    part_slots = capacity // halves
    half = EXPERTS * part_slots
    ids = route_ids[0]
    flat = ids.reshape(-1)
    onehot = (flat[:, None] == jnp.arange(EXPERTS, dtype=jnp.int32)[None, :]).astype(jnp.int32)
    earlier = jnp.cumsum(onehot, axis=0) - onehot
    slot = jnp.sum(earlier * onehot, axis=1)
    place = (slot // part_slots) * half + flat * part_slots + slot % part_slots
    place = jnp.where(slot < capacity, place, -1).reshape(rows, TOPK)
    targets = jnp.arange(halves * half, dtype=jnp.int32)
    select = [(place[:, k : k + 1] == targets[None, :]).astype(bf16) for k in range(TOPK)]
    spread = [(targets[:, None] == place[None, :, k]).astype(bf16) for k in range(TOPK)]
    gates = gate_values[0]

    dy = cotangent[0].astype(f32)
    grad_pairs = jnp.concatenate([(dy * gates[:, k : k + 1]).astype(bf16) for k in range(TOPK)])
    spread_both = jnp.concatenate(spread, axis=1)
    grad_blocks = [
        dot(spread_both[h * half : (h + 1) * half], grad_pairs, 1, 0, bf16) for h in range(halves)
    ]

    inputs = tokens[0].astype(f32)
    normed_f, _, _ = normalize_parts(inputs, norm1_gain)
    normed = core_gather(normed_f.astype(bf16))

    per = D // (ctx_count * fsdp_count)
    mine = lax.axis_index("fsdp")
    my_column, my_side = (mine % repeats) // pair, mine % pair

    index = jnp.arange(D, dtype=jnp.int32)
    source = (index // per % ctx_count) * (D // ctx_count)
    source = source + index // (per * ctx_count) * per + index % per
    shuffle = (index[:, None] == source[None, :]).astype(bf16)
    normed_mixed = dot(normed, shuffle, 1, 0, bf16)

    def weight_part(w):
        count = w.shape[0] // ctx_count
        return lax.dynamic_slice_in_dim(w, core * count, count, axis=0)

    weight_parts = [weight_part(w) for w in (w_gate, w_up, w_down)]
    gathered, normed_mixed, *tied = after(gathered, normed_mixed, *grad_blocks, *weight_parts)
    grad_blocks, weight_parts = tied[:halves], tied[halves:]
    out_columns = gathered[:, 3 * width :]
    full_qkv = gathered[:, : 3 * width]

    lines = [[r + e * repeats for e in range(EXPERTS)] for r in range(repeats)]

    def swap_experts(a, width=D):
        blocks = a.reshape(EXPERTS, -1, width)
        return lax.all_to_all(blocks, "fsdp", 0, 0, axis_index_groups=lines, tiled=True)

    def to_columns(a):
        return [a] + [column_shift(a, j) for j in range(1, columns)]

    grads_first = swap_experts(grad_blocks[0]).reshape(half, D)

    sides = [[i, i ^ 1] for i in range(0, fsdp_count, 2)]
    sides = [sorted(group) for group in sides]
    swapped = [
        lax.all_gather(part, "fsdp", axis=0, tiled=True, axis_index_groups=sides)
        for part in weight_parts
    ]

    starts = [(1 - my_side) * ctx_count + (core - s) % ctx_count for s in range(ctx_count)]

    def pair_weights(own, both):
        count = both.shape[0] // pair
        part = lax.dynamic_slice_in_dim(both, (1 - my_side) * count, count, axis=0)
        return join_weights(
            my_side, starts, own, [part] + [core_shift(part, s) for s in range(1, ctx_count)]
        )

    pre = dot(normed, full_qkv, 1, 0)
    context, q, k, v, log_total = attention_forward(perm, block, pre, cos, sin)

    def out_rows(c):
        return lax.dynamic_slice_in_dim(out_columns, (c % ctx_count) * width, width, axis=0)

    if ctx_count == 2:
        own_part, other = out_rows(core), core_shift(out_rows(core + 1), 1)
        w_o = jnp.concatenate(
            [jnp.where(core == 0, own_part, other), jnp.where(core == 0, other, own_part)], axis=1
        )
    else:
        w_o = lax.all_to_all(out_columns.reshape(ctx_count, width, width), "ctx", 0, 0)
        w_o = w_o.transpose(1, 0, 2).reshape(width, D)
    away = [dot(context[s * rows : (s + 1) * rows], w_o, 1, 0, bf16) for s in range(1, ctx_count)]
    attention = dot(context[:rows], w_o, 1, 0)
    for s in range(1, ctx_count):
        attention = attention + core_shift(away[s - 1], -s).astype(f32)
    hidden_in = inputs + attention
    normed_two_f, unit_two, inverse_two = normalize_parts(hidden_in, norm2_gain)
    normed_two = normed_two_f.astype(bf16)

    spread_any = spread[0] + spread[1]
    slot_blocks = [
        dot(spread_any[h * half : (h + 1) * half], normed_two, 1, 0, bf16) for h in range(halves)
    ]
    grads_first, waiting, _ = after(grads_first, grad_blocks[1], away[0])
    grads_second = swap_experts(waiting).reshape(half, D)
    grad_parts = to_columns(grads_first)
    got = after(grads_second, *slot_blocks, *swapped[:2], *grad_parts[1:])
    grads_second, slots_a, slots_b, *swapped_two = got[:5]
    grad_parts[1:] = got[5:]
    grad_parts += to_columns(grads_second)
    first = swap_experts(slots_a).reshape(half, D)
    wg, wu = (pair_weights(*w) for w in zip((w_gate, w_up), swapped_two))
    got = after(first, slots_b, swapped[2], wg, wu, *grad_parts[columns + 1 :])
    first, slots_b, swapped_down, wg, wu = got[:5]
    grad_parts[columns + 1 :] = got[5:]
    second = swap_experts(slots_b).reshape(half, D)
    wd = pair_weights(w_down, swapped_down)
    weights = (wg, wu, wd)
    parts = halves * columns

    def hidden_part(index, slots, state):
        return expert_hidden(index, parts, slots, grad_parts[index], weights, state)

    def grad_rows(index, state):
        return expert_rows(index, half, state[1:], weights[:2])

    def columns_home(pieces):
        return [column_shift(part, -(j + 1)) for j, part in enumerate(pieces)]

    def add_parts(own, returned):
        total = own.astype(f32)
        for part in returned:
            total = total + part.astype(f32)
        return total.astype(bf16)

    slot_parts = to_columns(first)
    back, came = {}, [None] * halves
    state = hidden_part(0, slot_parts[0], ())
    second, *state = after(second, *state)
    slot_parts += to_columns(second)
    back[0] = grad_rows(0, state)
    back[0], *got = after(back[0], *state, *slot_parts[1:columns])
    state, slot_parts[1:columns] = got[:3], got[3:]
    for h in range(halves):
        for j in range(1, columns):
            index = h * columns + j
            state = hidden_part(index, slot_parts[index], state)
            back[index] = grad_rows(index, state)
            back[index], *state = after(back[index], *state)
        if h == 0:
            got = after(*state, *slot_parts[columns + 1 :])
            state, slot_parts[columns + 1 :] = got[:3], got[3:]
        came[h] = columns_home([back[h * columns + j] for j in range(1, columns)])
    home_first, *got = after(back[0], *state, *came[0])
    state = got[:3]
    home_first = add_parts(home_first, got[3:])
    home_first, *state = after(home_first, *state)
    home_first = swap_experts(home_first)
    state = hidden_part(columns, slot_parts[columns], state)
    back[columns] = grad_rows(columns, state)
    back[columns], home_first, *state = after(back[columns], home_first, *state)
    hidden, grad_gate, grad_up = state
    all_slots = jnp.concatenate(slot_parts, axis=0)
    all_grads = jnp.concatenate(grad_parts, axis=0)

    def core_sum(part):
        total = lax.dynamic_slice_in_dim(part, core * width, width, axis=1).astype(f32)
        for s in range(1, ctx_count):
            start = ((core + s) % ctx_count) * width
            total = total + core_shift(
                lax.dynamic_slice_in_dim(part, start, width, axis=1), s
            ).astype(f32)
        return total.astype(bf16)

    def side_sum(total):
        return lax.psum_scatter(
            total, "fsdp", scatter_dimension=0, tiled=True, axis_index_groups=sides
        ).astype(f32)

    def out_rows_of(h, j, left):
        return expert_rows(h * columns + j, half, (left,), (wd,))

    home_second, hidden_t, *got = after(back[columns], hidden, *came[1])
    home_second = add_parts(home_second, got)
    home_second, hidden_t = after(home_second, hidden_t)
    home_second = swap_experts(home_second)
    down_part = dot(hidden_t, all_grads, 0, 0, bf16)
    down_part, hidden_t = after(down_part, hidden_t)
    away_first = [out_rows_of(0, j, hidden_t) for j in range(1, columns)]
    home_second, hidden_t, *away_first = after(home_second, hidden_t, *away_first)
    away_first = columns_home(away_first)
    down_total = core_sum(down_part)

    def side_swap_sum(total):
        def side_rows(i):
            size = total.shape[0] // pair
            return lax.dynamic_slice_in_dim(total, (i % pair) * size, size, axis=0)

        return side_rows(my_side), pair_swap(side_rows(my_side + 1))

    grad_slot_in = jnp.concatenate([home_first, home_second], axis=0).reshape(halves * half, D)

    grad_normed_two = dot(select[0] + select[1], grad_slot_in, 1, 0)
    grad_norm_two, norm2_part = norm_backward(grad_normed_two, unit_two, inverse_two, norm2_gain)
    grad_hidden_in = dy + grad_norm_two
    grad_attention = core_gather(grad_hidden_in.astype(bf16))
    def reduce_blocks(blocks, shift):
        total = blocks[0].astype(f32)
        for d in range(1, len(blocks)):
            total = total + shift(blocks[d].astype(bf16), d).astype(f32)
        return total.astype(bf16)

    def cut(a, n):
        size = a.shape[0] // n
        return [a[i * size : (i + 1) * size] for i in range(n)]

    def expert_sum(total):
        blocks = swap_experts(total, total.shape[1])
        return jnp.sum(blocks.reshape(EXPERTS, -1, total.shape[1]).astype(f32), axis=0)

    def row_blocks(a, n, own):
        split = a.reshape(EXPERTS, n, -1, a.shape[1])
        return [
            lax.dynamic_slice_in_dim(split, (own + d) % n, 1, axis=1).reshape(-1, a.shape[1])
            for d in range(n)
        ]

    out_part = dot(context, grad_attention, 0, 0, bf16)
    blocks_o = row_blocks(out_part, columns, my_column)
    got = after(grad_attention, down_total, *blocks_o)
    grad_attention, down_total, blocks_o = got[0], got[1], got[2:]
    down_grad = side_sum(down_total)
    came_o = [column_shift(block, d) for d, block in enumerate(blocks_o) if d]
    grad_context = dot(grad_attention, w_o, 1, 1, bf16)
    grad_qkv = attention_backward(
        perm, block, q, k, v, log_total, grad_context, cos, sin
    )
    qkv_part = dot(normed_mixed, grad_qkv, 0, 0, bf16)
    qkv_sum = lax.psum_scatter(qkv_part, "fsdp", scatter_dimension=0, tiled=True)

    got = after(qkv_part, grad_qkv, hidden_t, grad_gate, grad_up, *away_first)
    grad_qkv, hidden_t, gate_t, up_t, *away_first = got[1:]
    gate_part = dot(gate_t, all_slots, 0, 0, bf16)
    gate_part, hidden_t, *came_o = after(gate_part, hidden_t, *came_o)
    blocks_o = row_blocks(add_parts(blocks_o[0], came_o), pair, my_side)
    hidden_t, *blocks_o = after(hidden_t, *blocks_o)
    came_o = pair_swap(blocks_o[1])
    outs_first = add_parts(out_rows_of(0, 0, hidden_t), away_first)
    away_second = [out_rows_of(1, j, hidden_t) for j in range(1, columns)]
    gate_total = core_sum(gate_part)
    outs_first, gate_total, up_t, *away_second = after(outs_first, gate_total, up_t, *away_second)
    away_second = columns_home(away_second)
    outs_first = swap_experts(outs_first)
    gate_own, gate_came = side_swap_sum(gate_total)

    up_part = dot(up_t, all_slots, 0, 0, bf16)
    got = after(up_part, hidden_t, grad_qkv, outs_first, came_o, gate_came, *away_second)
    up_part, hidden_t, grad_qkv, outs_first, came_o, gate_came, *away_second = got
    out_grad = expert_sum(add_parts(blocks_o[0], [came_o]))
    outs_second = add_parts(out_rows_of(1, 0, hidden_t), away_second)
    up_total = core_sum(up_part)
    outs_second, up_total, grad_qkv, out_grad = after(outs_second, up_total, grad_qkv, out_grad)
    outs_second = swap_experts(outs_second)
    up_own, up_came = side_swap_sum(up_total)

    def back_rows(s, out):
        return dot(grad_qkv[s * rows : (s + 1) * rows], full_qkv, 1, 1, out)

    back_away = [back_rows(s, bf16) for s in range(1, ctx_count)]
    grad_normed = back_rows(0, f32)
    for s in range(1, ctx_count):
        grad_normed = grad_normed + core_shift(back_away[s - 1], -s).astype(f32)
    _, unit_one, inverse_one = normalize_parts(inputs, norm1_gain)
    grad_norm_one, norm1_part = norm_backward(grad_normed, unit_one, inverse_one, norm1_gain)
    tokens_grad = (grad_hidden_in + grad_norm_one).astype(bf16)
    tokens_grad, norm1_part, outs_second, qkv_sum = after(
        tokens_grad, norm1_part, outs_second, qkv_sum
    )
    gate_grad = gate_own.astype(f32) + gate_came.astype(f32)

    gains = jnp.stack([norm1_part, norm2_part]).reshape(2, ctx_count, fsdp_count, per)
    gains = lax.all_to_all(gains.transpose(2, 1, 0, 3), "fsdp", 0, 0, tiled=True)
    gains = jnp.sum(gains, axis=0)

    def gains_of(c):
        return lax.dynamic_index_in_dim(gains, c % ctx_count, 0, keepdims=False)

    gains_own = gains_of(core)
    for s in range(1, ctx_count):
        gains_own = gains_own + core_shift(gains_of(core + s), s)
    gains_own, up_own, up_came = after(gains_own, up_own, up_came)
    up_grad = up_own.astype(f32) + up_came.astype(f32)
    sums = qkv_sum.reshape(ctx_count, per, heads, 3, HD).astype(f32)
    sums = sums.transpose(3, 0, 1, 2, 4).reshape(3, ctx_count, per, width)

    def core_piece(c):
        return lax.dynamic_index_in_dim(sums, c % ctx_count, 1, keepdims=False)

    if ctx_count == 2:
        own_part, other = core_piece(core), core_shift(core_piece(core + 1), 1)
        qkv_own = jnp.concatenate(
            [jnp.where(core == 0, own_part, other), jnp.where(core == 0, other, own_part)], axis=2
        )
    else:
        qkv_own = lax.all_to_all(sums.astype(bf16), "ctx", 1, 1).astype(f32)
        qkv_own = qkv_own.transpose(0, 2, 1, 3).reshape(3, per, D)
    query_grad, key_grad, value_grad = qkv_own[0], qkv_own[1], qkv_own[2]

    slot_out = jnp.concatenate([outs_first, outs_second], axis=0).reshape(halves * half, D)
    mixed = hidden_in
    for i in range(TOPK):
        mixed = mixed + dot(select[i], slot_out, 1, 0) * gates[:, i : i + 1]

    return (
        mixed.astype(bf16)[None],
        tokens_grad[None],
        gains_own[0],
        query_grad,
        key_grad,
        value_grad,
        out_grad,
        gains_own[1],
        gate_grad,
        up_grad,
        down_grad,
    )


def solution(mesh):
    in_specs = (
        P("fsdp", "ctx", None),
        P("fsdp", "ctx", None),
        P("fsdp", "ctx", None),
        P("fsdp", None),
        P(),
        P("fsdp", None),
        P("fsdp", None),
        P("fsdp", None),
        P("fsdp", None),
        P(),
        P("fsdp", None),
        P("fsdp", None),
        P("fsdp", None),
        P("fsdp", "ctx", None),
    )
    out_specs = (
        P("fsdp", "ctx", None),
        P("fsdp", "ctx", None),
        P(("ctx", "fsdp")),
        P(("ctx", "fsdp"), None),
        P(("ctx", "fsdp"), None),
        P(("ctx", "fsdp"), None),
        P(("ctx", "fsdp"), None),
        P(("ctx", "fsdp")),
        P("fsdp", "ctx"),
        P("fsdp", "ctx"),
        P("fsdp", "ctx"),
    )
    return jax.shard_map(shards, mesh=mesh, in_specs=in_specs, out_specs=out_specs, check_vma=False)
```

```python
import functools
import math

import jax
import jax.numpy as jnp
from jax import lax
from jax.experimental import pallas as pl
from jax.experimental.layout import Layout, with_layout_constraint
from jax.experimental.pallas import tpu as pltpu
from jax.sharding import PartitionSpec as P

D = 2048
HEADS = 16
HD = 128
EXPERTS = 4
TOPK = 2
PROMPT = 512
CONT = 256
TILE = 256

norm_eps = 1e-05
scale = 1.0 / math.sqrt(HD)
bf16 = jnp.bfloat16
f32 = jnp.float32


def dot(a, b, ca, cb, out=f32):
    r = lax.dot_general(a, b, (((ca,), (cb,)), ((), ())), preferred_element_type=f32)
    return r.astype(out)


def tile_keys(t):
    prompt_tiles = PROMPT // TILE
    if t < prompt_tiles:
        return list(range(t + 1))
    per = CONT // TILE
    first = prompt_tiles + ((t - prompt_tiles) // per) * per
    return list(range(prompt_tiles)) + list(range(first, t + 1))


def load_tile(ref, perm, t, block, cols):
    per = TILE // block
    parts = [
        ref[pl.ds(pl.multiple_of(perm[t * per + i] * block, block), block), cols]
        for i in range(per)
    ]
    return parts[0] if per == 1 else jnp.concatenate(parts, axis=0)


def store_tile(ref, perm, t, block, cols, value):
    per = TILE // block
    for i in range(per):
        ref[pl.ds(pl.multiple_of(perm[t * per + i] * block, block), block), cols] = value[
            i * block : (i + 1) * block
        ]


def spread_keys(ref, tiles):
    runs, start = [], tiles[0]
    for a, b in zip(tiles, tiles[1:] + [None]):
        if b != a + 1:
            runs.append((start, a + 1))
            start = b
    parts = [ref[lo * TILE : hi * TILE, :] for lo, hi in runs]
    return parts[0] if len(parts) == 1 else jnp.concatenate(parts, axis=0)


def causal_fill(scores, value):
    width = scores.shape[1] - TILE
    row = lax.broadcasted_iota(jnp.int32, (TILE, TILE), 0)
    col = lax.broadcasted_iota(jnp.int32, (TILE, TILE), 1)
    last = jnp.where(col <= row, scores[:, width:], value)
    return last if width == 0 else jnp.concatenate([scores[:, :width], last], axis=1)


def forward_kernel(
    block, perm, pre_q, pre_k, pre_v, cos_ref, sin_ref, ctx_ref, q_ref, k_ref, v_ref, log_ref
):
    tiles = pre_q.shape[0] // TILE
    for t in range(tiles):
        rows = slice(t * TILE, (t + 1) * TILE)
        cos, sin = cos_ref[rows, :], sin_ref[rows, :]
        q = load_tile(pre_q, perm, t, block, slice(None))
        q_ref[rows, :] = (q * cos + pltpu.roll(q, HD // 2, 1) * sin).astype(bf16)
        k = load_tile(pre_k, perm, t, block, slice(None))
        k_ref[rows, :] = (k * cos + pltpu.roll(k, HD // 2, 1) * sin).astype(bf16)
        v_ref[rows, :] = load_tile(pre_v, perm, t, block, slice(None)).astype(bf16)
    for t in range(tiles):
        rows = slice(t * TILE, (t + 1) * TILE)
        seen = tile_keys(t)
        keys, values = spread_keys(k_ref, seen), spread_keys(v_ref, seen)
        scores = dot(q_ref[rows, :], keys, 1, 1) * scale
        scores = causal_fill(scores, -1e30)
        top = jnp.max(scores, axis=1, keepdims=True)
        expo = jnp.exp(scores - top)
        total = jnp.sum(expo, axis=1, keepdims=True)
        probs = (expo * (1.0 / total)).astype(bf16)
        context = dot(probs, values, 1, 0).astype(bf16)
        store_tile(ctx_ref, perm, t, block, slice(None), context)
        log_ref[rows, :] = jnp.broadcast_to(top + jnp.log(total), (TILE, HD))


def backward_kernel(
    block,
    perm,
    q_ref,
    k_ref,
    v_ref,
    log_ref,
    do_ref,
    cos_ref,
    sin_ref,
    out_ref,
    dk_ref,
    dv_ref,
):
    tiles = q_ref.shape[0] // TILE
    dk_ref[...] = jnp.zeros_like(dk_ref)
    dv_ref[...] = jnp.zeros_like(dv_ref)
    for t in range(tiles):
        rows = slice(t * TILE, (t + 1) * TILE)
        seen = tile_keys(t)
        keys, values = spread_keys(k_ref, seen), spread_keys(v_ref, seen)
        query = q_ref[rows, :]
        grad = load_tile(do_ref, perm, t, block, slice(None))
        scores = dot(query, keys, 1, 1) * scale
        soft = causal_fill(jnp.exp(scores - log_ref[rows, 0:1]), 0.0)
        grad_prob = dot(grad, values, 1, 1)
        delta = jnp.sum(grad_prob * soft, axis=1, keepdims=True)
        grad_scores = (soft * (grad_prob - delta)).astype(bf16)
        values_back = dot(soft.astype(bf16), grad, 0, 0)
        keys_back = dot(grad_scores, query, 0, 0)
        for i, s in enumerate(seen):
            part, own = slice(i * TILE, (i + 1) * TILE), slice(s * TILE, (s + 1) * TILE)
            dv_ref[own, :] += values_back[part]
            dk_ref[own, :] += keys_back[part]
        back = dot(grad_scores, keys, 1, 0) * scale
        cos, sin = cos_ref[rows, :], sin_ref[rows, :]
        back = back * cos - pltpu.roll(back, HD // 2, 1) * sin
        store_tile(out_ref, perm, t, block, slice(0, HD), back.astype(bf16))
    for t in range(tiles):
        rows = slice(t * TILE, (t + 1) * TILE)
        cos, sin = cos_ref[rows, :], sin_ref[rows, :]
        back = dk_ref[rows, :] * scale
        back = back * cos - pltpu.roll(back, HD // 2, 1) * sin
        store_tile(out_ref, perm, t, block, slice(HD, 2 * HD), back.astype(bf16))
        store_tile(out_ref, perm, t, block, slice(2 * HD, 3 * HD), dv_ref[rows, :].astype(bf16))


def attention_forward(perm, block, pre, cos, sin):
    rows, heads = pre.shape[0], pre.shape[1] // (3 * HD)
    per_head = pl.BlockSpec((rows, HD), lambda h, p: (0, h))
    table = pl.BlockSpec((rows, HD), lambda h, p: (0, 0))
    head_array = jax.ShapeDtypeStruct((rows, heads * HD), bf16)
    return pl.pallas_call(
        functools.partial(forward_kernel, block),
        grid_spec=pltpu.PrefetchScalarGridSpec(
            num_scalar_prefetch=1,
            grid=(heads,),
            in_specs=[
                pl.BlockSpec((rows, HD), lambda h, p: (0, 3 * h)),
                pl.BlockSpec((rows, HD), lambda h, p: (0, 3 * h + 1)),
                pl.BlockSpec((rows, HD), lambda h, p: (0, 3 * h + 2)),
                table,
                table,
            ],
            out_specs=[per_head] * 5,
        ),
        out_shape=[head_array] * 4 + [jax.ShapeDtypeStruct((rows, heads * HD), f32)],
        name="attention_forward",
    )(perm, pre, pre, pre, cos, sin)


def attention_backward(perm, block, q, k, v, log_total, grad, cos, sin):
    rows, heads = q.shape[0], q.shape[1] // HD
    per_head = pl.BlockSpec((rows, HD), lambda h, p: (0, h))
    table = pl.BlockSpec((rows, HD), lambda h, p: (0, 0))
    return pl.pallas_call(
        functools.partial(backward_kernel, block),
        grid_spec=pltpu.PrefetchScalarGridSpec(
            num_scalar_prefetch=1,
            grid=(heads,),
            in_specs=[per_head] * 5 + [table, table],
            out_specs=pl.BlockSpec((rows, 3 * HD), lambda h, p: (0, h)),
            scratch_shapes=[pltpu.VMEM((rows, HD), f32), pltpu.VMEM((rows, HD), f32)],
        ),
        out_shape=jax.ShapeDtypeStruct((rows, 3 * heads * HD), bf16),
        name="attention_backward",
    )(perm, q, k, v, log_total, grad, cos, sin)


def expert_kernel(kept, x_ref, g_ref, wg_ref, wu_ref, wd_ref, *refs):
    hidden_ref, gate_ref, up_ref = refs[kept:]
    count = x_ref.shape[0] // 2
    for p in range(2):
        rows = slice(p * count, (p + 1) * count)
        gate = dot(x_ref[rows, :], wg_ref[...], 1, 1)
        up = dot(x_ref[rows, :], wu_ref[...], 1, 1)
        grad = dot(g_ref[rows, :], wd_ref[...], 1, 1)
        sigmoid = jax.nn.sigmoid(gate)
        silu = gate * sigmoid
        hidden_ref[rows, :] = (silu * up).astype(bf16)
        gate_ref[rows, :] = (grad * up * sigmoid * (1.0 + gate * (1.0 - sigmoid))).astype(bf16)
        up_ref[rows, :] = (grad * silu).astype(bf16)


def expert_hidden(part, parts, slots, grads, weights, kept):
    rows, units = slots.shape[0], weights[0].shape[0]
    tile = 256 if units % 256 == 0 else 128
    whole = pl.BlockSpec((rows, D), lambda i: (0, 0))
    weight = pl.BlockSpec((tile, D), lambda i: (i, 0))
    result = pl.BlockSpec((rows, tile), lambda i: (part, i))
    return pl.pallas_call(
        functools.partial(expert_kernel, len(kept)),
        grid=(units // tile,),
        in_specs=[whole] * 2 + [weight] * 3 + [pl.BlockSpec(memory_space=pl.ANY)] * len(kept),
        out_specs=[result] * 3,
        out_shape=[jax.ShapeDtypeStruct((parts * rows, units), bf16)] * 3,
        input_output_aliases={5 + i: i for i in range(len(kept))},
        name="expert_hidden",
    )(slots, grads, *weights, *kept)


def rows_kernel(count, *refs):
    total = dot(refs[0][...], refs[count][...], 1, 0)
    for i in range(1, count):
        total = total + dot(refs[i][...], refs[count + i][...], 1, 0)
    refs[-1][...] = total.astype(bf16)


def expert_rows(part, rows, left, right):
    units, tile = right[0].shape[0], 256
    return pl.pallas_call(
        functools.partial(rows_kernel, len(left)),
        grid=(D // tile,),
        in_specs=[pl.BlockSpec((rows, units), lambda n: (part, 0))] * len(left)
        + [pl.BlockSpec((units, tile), lambda n: (0, n))] * len(right),
        out_specs=pl.BlockSpec((rows, tile), lambda n: (0, n)),
        out_shape=jax.ShapeDtypeStruct((rows, D), bf16),
        name="expert_rows",
    )(*left, *right)


def join_kernel(own_blocks, part_blocks, where, own_ref, *refs):
    parts, out_ref = refs[:-1], refs[-1]
    i = pl.program_id(0)
    inside = i - where[0] * own_blocks

    @pl.when((inside >= 0) & (inside < own_blocks))
    def _():
        out_ref[...] = own_ref[...]

    for s, part in enumerate(parts):
        place = i - where[1 + s]

        @pl.when((place >= 0) & (place < part_blocks))
        def _(part=part):
            out_ref[...] = part[...]


def join_weights(side, starts, own, parts):
    size, count = own.shape[0], parts[0].shape[0]
    tile = count // 2 if count % 32 == 0 else count
    own_blocks, part_blocks = size // tile, count // tile
    where = jnp.stack([side] + [start * part_blocks for start in starts]).astype(jnp.int32)

    def part_spec(s):
        return pl.BlockSpec(
            (tile, D), lambda i, w: (jnp.clip(i - w[1 + s], 0, part_blocks - 1), 0)
        )

    return pl.pallas_call(
        functools.partial(join_kernel, own_blocks, part_blocks),
        grid_spec=pltpu.PrefetchScalarGridSpec(
            num_scalar_prefetch=1,
            grid=(2 * own_blocks,),
            in_specs=[
                pl.BlockSpec(
                    (tile, D),
                    lambda i, w: (jnp.clip(i - w[0] * own_blocks, 0, own_blocks - 1), 0),
                )
            ]
            + [part_spec(s) for s in range(len(parts))],
            out_specs=pl.BlockSpec((tile, D), lambda i, w: (i, 0)),
        ),
        out_shape=jax.ShapeDtypeStruct((2 * size, D), own.dtype),
        name="join_weights",
    )(where, own, *parts)


def rope_tables(group_len):
    index = jnp.arange(group_len, dtype=jnp.int32)
    position = jnp.where(index < PROMPT, index, PROMPT + (index - PROMPT) % CONT).astype(f32)
    half = HD // 2
    frequency = jnp.exp(-math.log(10000.0) * jnp.arange(half, dtype=f32) / half)
    angles = position[:, None] * frequency[None, :]
    cosine, sine = jnp.cos(angles), jnp.sin(angles)
    return (
        jnp.concatenate([cosine, cosine], axis=1),
        jnp.concatenate([-sine, sine], axis=1),
    )


def after(*arrays):
    return lax.optimization_barrier(arrays)


def normalize_parts(values, gain):
    inverse = lax.rsqrt(jnp.mean(values * values, axis=-1, keepdims=True) + norm_eps)
    unit_rows = values * inverse
    return (unit_rows * gain, unit_rows, inverse)


def norm_backward(grad_outer, unit_rows, inverse, gain):
    grad_unit = grad_outer * gain
    grad_inner = inverse * (
        grad_unit - unit_rows * jnp.mean(grad_unit * unit_rows, axis=-1, keepdims=True)
    )
    return (grad_inner, jnp.sum(grad_outer * unit_rows, axis=0))


def shards(
    tokens,
    route_ids,
    gate_values,
    deal,
    norm1_gain,
    w_query,
    w_key,
    w_value,
    w_out,
    norm2_gain,
    w_gate,
    w_up,
    w_down,
    cotangent,
):
    rows = tokens.shape[1]
    ctx_count = lax.axis_size("ctx")
    fsdp_count = lax.axis_size("fsdp")
    group_len = rows * ctx_count
    capacity = 5 * rows * TOPK // (4 * EXPERTS)
    repeats = fsdp_count // EXPERTS
    pair = 2
    columns = repeats // pair
    core = lax.axis_index("ctx")
    expert = lax.axis_index("fsdp") // repeats
    width = D // ctx_count
    heads = HEADS // ctx_count

    def core_shift(a, s):
        return lax.ppermute(a, "ctx", [(i, (i + s) % ctx_count) for i in range(ctx_count)])

    def fsdp_shift(a, move):
        return lax.ppermute(a, "fsdp", [(i, move(i)) for i in range(fsdp_count)])

    def expert_shift(a, k):
        return fsdp_shift(a, lambda i: (i + k * repeats) % fsdp_count)

    def column_shift(a, j):
        def move(i):
            e, r = divmod(i, repeats)
            t, w = divmod(r, pair)
            return e * repeats + ((t + j) % columns) * pair + w

        return fsdp_shift(a, move)

    def pair_swap(a):
        return fsdp_shift(a, lambda i: i ^ 1)

    def core_gather(a):
        return jnp.concatenate([a] + [core_shift(a, s) for s in range(1, ctx_count)], axis=0)

    block_count = deal.shape[1]
    block = group_len // block_count
    local_blocks = block_count // ctx_count
    dealt = jnp.argsort(deal[0]).astype(jnp.int32)
    perm = ((core - dealt // local_blocks) % ctx_count) * local_blocks + dealt % local_blocks
    cos, sin = rope_tables(group_len)

    def own_columns(w):
        return lax.dynamic_slice_in_dim(w, core * width, width, axis=1)

    by_head = [own_columns(w).reshape(-1, heads, HD) for w in (w_query, w_key, w_value)]
    packed = jnp.concatenate(
        [jnp.stack(by_head, axis=2).reshape(-1, 3 * width), own_columns(w_out)], axis=1
    )
    packed = with_layout_constraint(packed, Layout(major_to_minor=(0, 1)))
    gathered = lax.all_gather(packed, "fsdp", axis=0, tiled=True)
    gathered = with_layout_constraint(gathered, Layout(major_to_minor=(0, 1)))

    halves = 2
    part_slots = capacity // halves
    half = EXPERTS * part_slots
    ids = route_ids[0]
    flat = ids.reshape(-1)
    onehot = (flat[:, None] == jnp.arange(EXPERTS, dtype=jnp.int32)[None, :]).astype(jnp.int32)
    earlier = jnp.cumsum(onehot, axis=0) - onehot
    slot = jnp.sum(earlier * onehot, axis=1)
    place = (slot // part_slots) * half + flat * part_slots + slot % part_slots
    place = jnp.where(slot < capacity, place, -1).reshape(rows, TOPK)
    targets = jnp.arange(halves * half, dtype=jnp.int32)
    select = [(place[:, k : k + 1] == targets[None, :]).astype(bf16) for k in range(TOPK)]
    spread = [(targets[:, None] == place[None, :, k]).astype(bf16) for k in range(TOPK)]
    gates = gate_values[0]

    dy = cotangent[0].astype(f32)
    grad_pairs = jnp.concatenate([(dy * gates[:, k : k + 1]).astype(bf16) for k in range(TOPK)])
    spread_both = jnp.concatenate(spread, axis=1)
    grad_blocks = [
        dot(spread_both[h * half : (h + 1) * half], grad_pairs, 1, 0, bf16) for h in range(halves)
    ]

    inputs = tokens[0].astype(f32)
    normed_f, _, _ = normalize_parts(inputs, norm1_gain)
    normed = core_gather(normed_f.astype(bf16))

    per = D // (ctx_count * fsdp_count)
    mine = lax.axis_index("fsdp")
    my_column, my_side = (mine % repeats) // pair, mine % pair

    index = jnp.arange(D, dtype=jnp.int32)
    source = (index // per % ctx_count) * (D // ctx_count)
    source = source + index // (per * ctx_count) * per + index % per
    shuffle = (index[:, None] == source[None, :]).astype(bf16)
    normed_mixed = dot(normed, shuffle, 1, 0, bf16)

    def weight_part(w):
        count = w.shape[0] // ctx_count
        return lax.dynamic_slice_in_dim(w, core * count, count, axis=0)

    weight_parts = [weight_part(w) for w in (w_gate, w_up, w_down)]
    gathered, normed_mixed, *tied = after(gathered, normed_mixed, *grad_blocks, *weight_parts)
    grad_blocks, weight_parts = tied[:halves], tied[halves:]
    out_columns = gathered[:, 3 * width :]
    full_qkv = gathered[:, : 3 * width]

    lines = [[r + e * repeats for e in range(EXPERTS)] for r in range(repeats)]

    def swap_experts(a, width=D):
        blocks = a.reshape(EXPERTS, -1, width)
        return lax.all_to_all(blocks, "fsdp", 0, 0, axis_index_groups=lines, tiled=True)

    def to_columns(a):
        return [a] + [column_shift(a, j) for j in range(1, columns)]

    grads_first = swap_experts(grad_blocks[0]).reshape(half, D)

    sides = [[i, i ^ 1] for i in range(0, fsdp_count, 2)]
    sides = [sorted(group) for group in sides]
    swapped = [
        lax.all_gather(part, "fsdp", axis=0, tiled=True, axis_index_groups=sides)
        for part in weight_parts
    ]

    starts = [(1 - my_side) * ctx_count + (core - s) % ctx_count for s in range(ctx_count)]

    def pair_weights(own, both):
        count = both.shape[0] // pair
        part = lax.dynamic_slice_in_dim(both, (1 - my_side) * count, count, axis=0)
        return join_weights(
            my_side, starts, own, [part] + [core_shift(part, s) for s in range(1, ctx_count)]
        )

    pre = dot(normed, full_qkv, 1, 0)
    context, q, k, v, log_total = attention_forward(perm, block, pre, cos, sin)

    def out_rows(c):
        return lax.dynamic_slice_in_dim(out_columns, (c % ctx_count) * width, width, axis=0)

    if ctx_count == 2:
        own_part, other = out_rows(core), core_shift(out_rows(core + 1), 1)
        w_o = jnp.concatenate(
            [jnp.where(core == 0, own_part, other), jnp.where(core == 0, other, own_part)], axis=1
        )
    else:
        w_o = lax.all_to_all(out_columns.reshape(ctx_count, width, width), "ctx", 0, 0)
        w_o = w_o.transpose(1, 0, 2).reshape(width, D)
    away = [dot(context[s * rows : (s + 1) * rows], w_o, 1, 0, bf16) for s in range(1, ctx_count)]
    attention = dot(context[:rows], w_o, 1, 0)
    for s in range(1, ctx_count):
        attention = attention + core_shift(away[s - 1], -s).astype(f32)
    hidden_in = inputs + attention
    normed_two_f, unit_two, inverse_two = normalize_parts(hidden_in, norm2_gain)
    normed_two = normed_two_f.astype(bf16)

    spread_any = spread[0] + spread[1]
    slot_blocks = [
        dot(spread_any[h * half : (h + 1) * half], normed_two, 1, 0, bf16) for h in range(halves)
    ]
    grads_first, waiting, _ = after(grads_first, grad_blocks[1], away[0])
    grads_second = swap_experts(waiting).reshape(half, D)
    grad_parts = to_columns(grads_first)
    got = after(grads_second, *slot_blocks, *swapped[:2], *grad_parts[1:])
    grads_second, slots_a, slots_b, *swapped_two = got[:5]
    grad_parts[1:] = got[5:]
    grad_parts += to_columns(grads_second)
    first = swap_experts(slots_a).reshape(half, D)
    wg, wu = (pair_weights(*w) for w in zip((w_gate, w_up), swapped_two))
    got = after(first, slots_b, swapped[2], wg, wu, *grad_parts[columns + 1 :])
    first, slots_b, swapped_down, wg, wu = got[:5]
    grad_parts[columns + 1 :] = got[5:]
    second = swap_experts(slots_b).reshape(half, D)
    wd = pair_weights(w_down, swapped_down)
    weights = (wg, wu, wd)
    parts = halves * columns

    def hidden_part(index, slots, state):
        return expert_hidden(index, parts, slots, grad_parts[index], weights, state)

    def grad_rows(index, state):
        return expert_rows(index, half, state[1:], weights[:2])

    def columns_home(pieces):
        return [column_shift(part, -(j + 1)) for j, part in enumerate(pieces)]

    def add_parts(own, returned):
        total = own.astype(f32)
        for part in returned:
            total = total + part.astype(f32)
        return total.astype(bf16)

    slot_parts = to_columns(first)
    back, came = {}, [None] * halves
    state = hidden_part(0, slot_parts[0], ())
    second, *state = after(second, *state)
    slot_parts += to_columns(second)
    back[0] = grad_rows(0, state)
    back[0], *got = after(back[0], *state, *slot_parts[1:columns])
    state, slot_parts[1:columns] = got[:3], got[3:]
    for h in range(halves):
        for j in range(1, columns):
            index = h * columns + j
            state = hidden_part(index, slot_parts[index], state)
            back[index] = grad_rows(index, state)
            back[index], *state = after(back[index], *state)
        if h == 0:
            got = after(*state, *slot_parts[columns + 1 :])
            state, slot_parts[columns + 1 :] = got[:3], got[3:]
        came[h] = columns_home([back[h * columns + j] for j in range(1, columns)])
    home_first, *got = after(back[0], *state, *came[0])
    state = got[:3]
    home_first = add_parts(home_first, got[3:])
    home_first, *state = after(home_first, *state)
    home_first = swap_experts(home_first)
    state = hidden_part(columns, slot_parts[columns], state)
    back[columns] = grad_rows(columns, state)
    back[columns], home_first, *state = after(back[columns], home_first, *state)
    hidden, grad_gate, grad_up = state
    all_slots = jnp.concatenate(slot_parts, axis=0)
    all_grads = jnp.concatenate(grad_parts, axis=0)

    def core_sum(part):
        total = lax.dynamic_slice_in_dim(part, core * width, width, axis=1).astype(f32)
        for s in range(1, ctx_count):
            start = ((core + s) % ctx_count) * width
            total = total + core_shift(
                lax.dynamic_slice_in_dim(part, start, width, axis=1), s
            ).astype(f32)
        return total.astype(bf16)

    def side_sum(total):
        return lax.psum_scatter(
            total, "fsdp", scatter_dimension=0, tiled=True, axis_index_groups=sides
        ).astype(f32)

    def out_rows_of(h, j, left):
        return expert_rows(h * columns + j, half, (left,), (wd,))

    home_second, hidden_t, *got = after(back[columns], hidden, *came[1])
    home_second = add_parts(home_second, got)
    home_second, hidden_t = after(home_second, hidden_t)
    home_second = swap_experts(home_second)
    down_part = dot(hidden_t, all_grads, 0, 0, bf16)
    down_part, hidden_t = after(down_part, hidden_t)
    away_first = [out_rows_of(0, j, hidden_t) for j in range(1, columns)]
    home_second, hidden_t, *away_first = after(home_second, hidden_t, *away_first)
    away_first = columns_home(away_first)
    down_total = core_sum(down_part)

    def side_swap_sum(total):
        def side_rows(i):
            size = total.shape[0] // pair
            return lax.dynamic_slice_in_dim(total, (i % pair) * size, size, axis=0)

        return side_rows(my_side), pair_swap(side_rows(my_side + 1))

    grad_slot_in = jnp.concatenate([home_first, home_second], axis=0).reshape(halves * half, D)

    grad_normed_two = dot(select[0] + select[1], grad_slot_in, 1, 0)
    grad_norm_two, norm2_part = norm_backward(grad_normed_two, unit_two, inverse_two, norm2_gain)
    grad_hidden_in = dy + grad_norm_two
    grad_attention = core_gather(grad_hidden_in.astype(bf16))
    def reduce_blocks(blocks, shift):
        total = blocks[0].astype(f32)
        for d in range(1, len(blocks)):
            total = total + shift(blocks[d].astype(bf16), d).astype(f32)
        return total.astype(bf16)

    def cut(a, n):
        size = a.shape[0] // n
        return [a[i * size : (i + 1) * size] for i in range(n)]

    def expert_sum(total):
        blocks = swap_experts(total, total.shape[1])
        return jnp.sum(blocks.reshape(EXPERTS, -1, total.shape[1]).astype(f32), axis=0)

    def row_blocks(a, n, own):
        split = a.reshape(EXPERTS, n, -1, a.shape[1])
        return [
            lax.dynamic_slice_in_dim(split, (own + d) % n, 1, axis=1).reshape(-1, a.shape[1])
            for d in range(n)
        ]

    out_part = dot(context, grad_attention, 0, 0, bf16)
    blocks_o = row_blocks(out_part, columns, my_column)
    got = after(grad_attention, down_total, *blocks_o)
    grad_attention, down_total, blocks_o = got[0], got[1], got[2:]
    down_grad = side_sum(down_total)
    came_o = [column_shift(block, d) for d, block in enumerate(blocks_o) if d]
    grad_context = dot(grad_attention, w_o, 1, 1, bf16)
    grad_qkv = attention_backward(
        perm, block, q, k, v, log_total, grad_context, cos, sin
    )
    qkv_part = dot(normed_mixed, grad_qkv, 0, 0, bf16)
    qkv_sum = lax.psum_scatter(qkv_part, "fsdp", scatter_dimension=0, tiled=True)

    got = after(qkv_part, grad_qkv, hidden_t, grad_gate, grad_up, *away_first)
    grad_qkv, hidden_t, gate_t, up_t, *away_first = got[1:]
    gate_part = dot(gate_t, all_slots, 0, 0, bf16)
    gate_part, hidden_t, *came_o = after(gate_part, hidden_t, *came_o)
    blocks_o = row_blocks(add_parts(blocks_o[0], came_o), pair, my_side)
    hidden_t, *blocks_o = after(hidden_t, *blocks_o)
    came_o = pair_swap(blocks_o[1])
    outs_first = add_parts(out_rows_of(0, 0, hidden_t), away_first)
    away_second = [out_rows_of(1, j, hidden_t) for j in range(1, columns)]
    gate_total = core_sum(gate_part)
    outs_first, gate_total, up_t, *away_second = after(outs_first, gate_total, up_t, *away_second)
    away_second = columns_home(away_second)
    outs_first = swap_experts(outs_first)
    gate_own, gate_came = side_swap_sum(gate_total)

    up_part = dot(up_t, all_slots, 0, 0, bf16)
    got = after(up_part, hidden_t, grad_qkv, outs_first, came_o, gate_came, *away_second)
    up_part, hidden_t, grad_qkv, outs_first, came_o, gate_came, *away_second = got
    out_grad = expert_sum(add_parts(blocks_o[0], [came_o]))
    outs_second = add_parts(out_rows_of(1, 0, hidden_t), away_second)
    up_total = core_sum(up_part)
    gate_grad = gate_own.astype(f32) + gate_came.astype(f32)
    got = after(outs_second, up_total, grad_qkv, out_grad, gate_grad, down_grad)
    outs_second, up_total, grad_qkv, out_grad, gate_grad, down_grad = got
    outs_second = swap_experts(outs_second)
    up_own, up_came = side_swap_sum(up_total)

    def back_rows(s, out):
        return dot(grad_qkv[s * rows : (s + 1) * rows], full_qkv, 1, 1, out)

    back_away = [back_rows(s, bf16) for s in range(1, ctx_count)]
    grad_normed = back_rows(0, f32)
    for s in range(1, ctx_count):
        grad_normed = grad_normed + core_shift(back_away[s - 1], -s).astype(f32)
    _, unit_one, inverse_one = normalize_parts(inputs, norm1_gain)
    grad_norm_one, norm1_part = norm_backward(grad_normed, unit_one, inverse_one, norm1_gain)
    tokens_grad = (grad_hidden_in + grad_norm_one).astype(bf16)
    tokens_grad, norm1_part, outs_second, qkv_sum = after(
        tokens_grad, norm1_part, outs_second, qkv_sum
    )

    gains = jnp.stack([norm1_part, norm2_part]).reshape(2, ctx_count, fsdp_count, per)
    gains = lax.all_to_all(gains.transpose(2, 1, 0, 3), "fsdp", 0, 0, tiled=True)
    gains = jnp.sum(gains, axis=0)

    def gains_of(c):
        return lax.dynamic_index_in_dim(gains, c % ctx_count, 0, keepdims=False)

    gains_own = gains_of(core)
    for s in range(1, ctx_count):
        gains_own = gains_own + core_shift(gains_of(core + s), s)
    gains_own, up_own, up_came = after(gains_own, up_own, up_came)
    up_grad = up_own.astype(f32) + up_came.astype(f32)
    sums = qkv_sum.reshape(ctx_count, per, heads, 3, HD).astype(f32)
    sums = sums.transpose(3, 0, 1, 2, 4).reshape(3, ctx_count, per, width)

    def core_piece(c):
        return lax.dynamic_index_in_dim(sums, c % ctx_count, 1, keepdims=False)

    if ctx_count == 2:
        own_part, other = core_piece(core), core_shift(core_piece(core + 1), 1)
        qkv_own = jnp.concatenate(
            [jnp.where(core == 0, own_part, other), jnp.where(core == 0, other, own_part)], axis=2
        )
    else:
        qkv_own = lax.all_to_all(sums.astype(bf16), "ctx", 1, 1).astype(f32)
        qkv_own = qkv_own.transpose(0, 2, 1, 3).reshape(3, per, D)
    query_grad, key_grad, value_grad = qkv_own[0], qkv_own[1], qkv_own[2]

    slot_out = jnp.concatenate([outs_first, outs_second], axis=0).reshape(halves * half, D)
    mixed = hidden_in
    for i in range(TOPK):
        mixed = mixed + dot(select[i], slot_out, 1, 0) * gates[:, i : i + 1]

    return (
        mixed.astype(bf16)[None],
        tokens_grad[None],
        gains_own[0],
        query_grad,
        key_grad,
        value_grad,
        out_grad,
        gains_own[1],
        gate_grad,
        up_grad,
        down_grad,
    )


def solution(mesh):
    in_specs = (
        P("fsdp", "ctx", None),
        P("fsdp", "ctx", None),
        P("fsdp", "ctx", None),
        P("fsdp", None),
        P(),
        P("fsdp", None),
        P("fsdp", None),
        P("fsdp", None),
        P("fsdp", None),
        P(),
        P("fsdp", None),
        P("fsdp", None),
        P("fsdp", None),
        P("fsdp", "ctx", None),
    )
    out_specs = (
        P("fsdp", "ctx", None),
        P("fsdp", "ctx", None),
        P(("ctx", "fsdp")),
        P(("ctx", "fsdp"), None),
        P(("ctx", "fsdp"), None),
        P(("ctx", "fsdp"), None),
        P(("ctx", "fsdp"), None),
        P(("ctx", "fsdp")),
        P("fsdp", "ctx"),
        P("fsdp", "ctx"),
        P("fsdp", "ctx"),
    )
    return jax.shard_map(shards, mesh=mesh, in_specs=in_specs, out_specs=out_specs, check_vma=False)
```
